32 devices in a mesh: dp: 8 (over z, y), tensor: 4 (over x, core).
Axes of the slice: x: 2, y: 2, z: 4, core: 2. Of those that a mesh axis runs over, the one named last changes fastest.
Arguments:
- tokens: bfloat16 [4, 2048, 2048], P(None, ('dp', 'tensor')), may hold values from -6 to 6
- cotangent: bfloat16 [4, 2048, 2048], P(None, ('dp', 'tensor')), may hold values from -6 to 6
- query_weight: bfloat16 [2048, 2048], P('dp', 'tensor'), may hold values from -0.125 to 0.125
- key_weight: bfloat16 [2048, 2048], P('dp', 'tensor'), may hold values from -0.125 to 0.125
- value_weight: bfloat16 [2048, 2048], P('dp', 'tensor'), may hold values from -0.125 to 0.125
- beta_weight: bfloat16 [2048, 16], P('dp', 'tensor'), may hold values from -0.125 to 0.125
- conv_filter: bfloat16 [12, 16, 128], P(None, 'tensor', 'dp'), may hold values from -3 to 3
- norm_gain: bfloat16 [2, 2048], P(None, 'dp'), may hold values from 0.25 to 1.75
- head_gain: bfloat16 [128], P('dp'), may hold values from 0.25 to 1.75
- out_weight: bfloat16 [2048, 2048], P('tensor', 'dp'), may hold values from -0.125 to 0.125
- gate_weight: bfloat16 [2048, 5632], P('dp', 'tensor'), may hold values from -0.125 to 0.125
- up_weight: bfloat16 [2048, 5632], P('dp', 'tensor'), may hold values from -0.125 to 0.125
- down_weight: bfloat16 [5632, 2048], P('tensor', 'dp'), may hold values from -0.078125 to 0.078125
Outputs:
- layer_out: bfloat16 [4, 2048, 2048], P(None, ('dp', 'tensor'))
- d_tokens: bfloat16 [4, 2048, 2048], P(None, ('dp', 'tensor'))
- grad_query_weight: float32 [2048, 2048], P('dp', 'tensor')
- grad_key_weight: float32 [2048, 2048], P('dp', 'tensor')
- grad_value_weight: float32 [2048, 2048], P('dp', 'tensor')
- grad_beta_weight: float32 [2048, 16], P('dp', 'tensor')
- grad_conv_filter: float32 [12, 16, 128], P(None, 'tensor', 'dp')
- grad_norm_gain: float32 [2, 2048], P(None, 'dp')
- grad_head_gain: float32 [128], P('dp')
- grad_out_weight: float32 [2048, 2048], P('tensor', 'dp')
- grad_gate_weight: float32 [2048, 5632], P('dp', 'tensor')
- grad_up_weight: float32 [2048, 5632], P('dp', 'tensor')
- grad_down_weight: float32 [5632, 2048], P('tensor', 'dp')
The draws below stay inside these ranges and needn't reach their ends.
All inputs are finite; a program needn't handle non-finite values.
Results may differ from the reference program's by a relative error of at most 0.018.
Values may be sent and summed in bfloat16 or wider, within the bound.
A program may use at most 384 MiB of HBM per device.

```python
import jax
import jax.numpy as jnp
from jax import lax

D = 2048
H = 16
HD = 128
FF = 5632
KCONV = 4
GROUP = 64
SEQS = 4
LEN = 2048


def spiked(values, own_key, source, target, blocks, factor):
    def block_of(axis_at):
        return (jnp.arange(values.shape[axis_at]) // (values.shape[axis_at] // blocks)).reshape((-1,) + (1,) * (values.ndim - 1 - axis_at))

    near = jax.random.permutation(own_key, blocks)[block_of(target)]
    second = (block_of(target) + blocks // 2) % blocks
    return jnp.where((block_of(source) == near) | (block_of(source) == second), factor * values, values)


def level_of(own_key, shape, shards, least, high):
    def one(position, blocks):
        heights = jax.random.uniform(jax.random.fold_in(jax.random.fold_in(own_key, 6), position), (blocks,), jnp.float32, least / len(shards), high / len(shards))
        return jnp.repeat(jnp.exp(heights), shape[position] // blocks).reshape((-1,) + (1,) * (len(shape) - position - 1))

    loudness = one(*shards[0])
    for cut in shards[1:]:
        loudness = loudness * one(*cut)
    return loudness


def scatter_about(key, dims, width, limit, pieces=(), kind=jnp.bfloat16):
    gain = level_of(key, dims, pieces, -0.22, 0.18) if pieces else 1.0
    array = jax.random.normal(key, dims, jnp.float32) * width * gain
    return jnp.minimum(jnp.maximum(array, -limit), limit).astype(kind)


def heavy_noise(key, shape, width, reach, pieces, heavy, kind=jnp.bfloat16):
    array = width * jax.random.normal(key, shape, jnp.float32)
    if pieces:
        array = array * level_of(key, shape, pieces, -0.22, 0.18)
    return jnp.clip(spiked(array, jax.random.fold_in(key, 3), *heavy), -reach, reach).astype(kind)


def setup_inputs(seed: int = 0) -> dict:
    seeds = jax.random.split(jax.random.key(seed), 14)
    return {
        "tokens": scatter_about(seeds[0], (SEQS, LEN, D), 1.0, 6.0, ((1, 32),)),
        "cotangent": heavy_noise(seeds[1], (SEQS, LEN, D), 1.0, 6.0, ((1, 32),), (1, 2, 32, 2.75)),
        "query_weight": scatter_about(seeds[2], (D, D), D ** -0.5, 0.125, ((0, 8), (1, 4))),
        "key_weight": scatter_about(seeds[3], (D, D), D ** -0.5, 0.125, ((0, 8), (1, 4))),
        "value_weight": scatter_about(seeds[4], (D, D), D ** -0.5, 0.125, ((0, 8), (1, 4))),
        "beta_weight": scatter_about(seeds[5], (D, H), D ** -0.5, 0.125, ((0, 8), (1, 4))),
        "conv_filter": scatter_about(seeds[6], (3 * KCONV, H, HD), KCONV ** -0.5, 3.0, ((1, 4), (2, 8))),
        "norm_gain": jnp.clip(1.0 + 0.15 * jax.random.normal(seeds[7], (2, D), jnp.float32), 0.25, 1.75).astype(jnp.bfloat16),
        "head_gain": jnp.clip(1.0 + 0.15 * jax.random.normal(seeds[8], (HD,), jnp.float32), 0.25, 1.75).astype(jnp.bfloat16),
        "out_weight": scatter_about(seeds[9], (D, D), D ** -0.5, 0.125, ((0, 4), (1, 8))),
        "gate_weight": scatter_about(seeds[10], (D, FF), D ** -0.5, 0.125, ((0, 8), (1, 4))),
        "up_weight": scatter_about(seeds[11], (D, FF), D ** -0.5, 0.125, ((0, 8), (1, 4))),
        "down_weight": scatter_about(seeds[12], (FF, D), FF ** -0.5, 0.078125, ((0, 4), (1, 8))),
    }


highest_precision = lax.Precision.HIGHEST
epsilon = 1e-06

@jax.custom_vjp
def low(v):
    return lax.optimization_barrier(v.astype(jnp.bfloat16)).astype(jnp.float32)

@jax.custom_vjp
def low_back(v):
    return v

def low_keep(v):
    return (low(v), None)

def low_pass(kept, grad):
    return (grad,)

def back_keep(v):
    return (v, None)

def back_low(kept, grad):
    return (low(grad),)
low.defvjp(low_keep, low_pass)
low_back.defvjp(back_keep, back_low)

def matmul_high(left, right):
    return jnp.matmul(left, right, precision=highest_precision)

def rms_scale(values, gain_row):
    return values * lax.rsqrt(lax.optimization_barrier(jnp.mean(values * values, axis=-1, keepdims=True)) + epsilon) * gain_row

def unit_rows(values):
    return values * lax.rsqrt(lax.optimization_barrier(jnp.sum(values * values, axis=-1, keepdims=True)) + epsilon)

def causal_conv(signal, filter_taps):
    padded = jnp.concatenate([jnp.zeros((KCONV - 1, signal.shape[1]), signal.dtype), signal], 0)
    running = jnp.zeros_like(signal)
    for tap_index in range(KCONV):
        running = running + filter_taps[tap_index] * padded[tap_index:tap_index + signal.shape[0]]
    return running

def delta_block(carried_state, inputs):
    query_rows, input_keys, values_in, strength = inputs
    block_len = input_keys.shape[1]
    gram_matrix = jnp.einsum('hck,hdk->hcd', input_keys, input_keys, precision=highest_precision)
    strict = jnp.tril(jnp.ones((block_len, block_len), gram_matrix.dtype), -1)
    inclusive = jnp.tril(jnp.ones((block_len, block_len), gram_matrix.dtype))
    system = jnp.eye(block_len, dtype=gram_matrix.dtype) + strength[:, :, None] * gram_matrix * strict
    key_mixture = jax.scipy.linalg.solve_triangular(system, strength[:, :, None] * input_keys, lower=True, unit_diagonal=True)
    value_mixture = jax.scipy.linalg.solve_triangular(system, strength[:, :, None] * values_in, lower=True, unit_diagonal=True)
    state_update = value_mixture - jnp.einsum('qgw,qwj->qgj', key_mixture, carried_state, precision=highest_precision)
    scores = jnp.einsum('hck,hdk->hcd', query_rows, input_keys, precision=highest_precision) * inclusive
    block_output = jnp.einsum('qgw,qwj->qgj', query_rows, carried_state, precision=highest_precision)
    block_output = block_output + jnp.einsum('hcd,hdv->hcv', scores, state_update, precision=highest_precision)
    updated_state = carried_state + jnp.einsum('zto,zty->zoy', input_keys, state_update, precision=highest_precision)
    return (updated_state, block_output)

def delta_rule(query_rows, input_keys, values_in, strength):
    blocks = query_rows.shape[0] // GROUP

    def to_blocks(array_in):
        return jnp.moveaxis(array_in.reshape((blocks, GROUP) + array_in.shape[1:]), 2, 1)
    initial = jnp.zeros((H, HD, HD), query_rows.dtype)
    _, outputs = lax.scan(jax.checkpoint(delta_block), initial, (to_blocks(query_rows), to_blocks(input_keys), to_blocks(values_in), to_blocks(strength)))
    return jnp.moveaxis(outputs, 1, 2).reshape(query_rows.shape)

def layer(tokens_row, query_weight, key_weight, value_weight, beta_weight, conv_filter, norm_gain, head_gain, out_weight, gate_weight, up_weight, down_weight):
    length = tokens_row.shape[0]
    normed_first = low(rms_scale(tokens_row, norm_gain[0]))
    filters = conv_filter.reshape(3, KCONV, D)
    activated = []
    for column, weight in enumerate((query_weight, key_weight, value_weight)):
        projected = low_back(low(matmul_high(normed_first, weight)))
        activated.append(jax.nn.silu(causal_conv(projected, filters[column])))
    query_rows = low(unit_rows(activated[0].reshape(length, H, HD)))
    input_keys = low(unit_rows(activated[1].reshape(length, H, HD)))
    values_in = low(activated[2].reshape(length, H, HD))
    strength = jax.nn.sigmoid(low_back(matmul_high(normed_first, beta_weight)))
    mix_out = delta_rule(query_rows, input_keys, values_in, strength)
    normed_mix = low(rms_scale(mix_out, head_gain)).reshape(length, D)
    hidden_state = tokens_row + low_back(matmul_high(normed_mix, out_weight))
    normed_second = low(rms_scale(hidden_state, norm_gain[1]))
    gate_pre = low_back(matmul_high(normed_second, gate_weight))
    up_pre = low_back(matmul_high(normed_second, up_weight))
    ffn_hidden = low(jax.nn.silu(gate_pre) * up_pre)
    return hidden_state + low_back(matmul_high(ffn_hidden, down_weight))

def reference(tokens, cotangent, query_weight, key_weight, value_weight, beta_weight, conv_filter, norm_gain, head_gain, out_weight, gate_weight, up_weight, down_weight):
    params = tuple((param_in.astype(jnp.float32) for param_in in (query_weight, key_weight, value_weight, beta_weight, conv_filter, norm_gain, head_gain, out_weight, gate_weight, up_weight, down_weight)))

    def one_sequence(totals, pair_in):
        sequence_in, grad_in = pair_in
        result, pullback = jax.vjp(layer, sequence_in.astype(jnp.float32), *params)
        all_grads = pullback(grad_in.astype(jnp.float32))
        summed = tuple((total_grad + new_grad for total_grad, new_grad in zip(totals, all_grads[1:])))
        return (summed, (result.astype(jnp.bfloat16), all_grads[0].astype(jnp.bfloat16)))
    zero_grads = tuple((jnp.zeros_like(param_in) for param_in in params))
    grad_sums, (layer_out, d_tokens) = lax.scan(one_sequence, zero_grads, (tokens, cotangent))
    return (layer_out, d_tokens, grad_sums[0], grad_sums[1], grad_sums[2], grad_sums[3], grad_sums[4], grad_sums[5], grad_sums[6], grad_sums[7], grad_sums[8], grad_sums[9], grad_sums[10])
```

```python
import functools

import jax
import jax.numpy as jnp
from jax import lax
from jax.experimental import pallas as pl
from jax.experimental.pallas import tpu as pltpu
from jax.sharding import PartitionSpec as P

HD = 128
KCONV = 4
RIM = 8
PAIR = 2

epsilon = 1e-06
f32 = jnp.float32
bf16 = jnp.bfloat16
MESH = pl.DeviceIdType.MESH
VMEM_LIMIT = 60 * 1024 * 1024


def halves(value):
    high = value.astype(bf16)
    return (high, (value - high.astype(f32)).astype(bf16))


def product(left, right, left_dim=1, right_dim=0):
    left = left if isinstance(left, tuple) else (left,)
    right = right if isinstance(right, tuple) else (right,)
    total = None
    for i, a in enumerate(left):
        for j, b in enumerate(right):
            if i + j < 2:
                term = lax.dot_general(
                    a, b, (((left_dim,), (right_dim,)), ((), ())), preferred_element_type=f32
                )
                total = term if total is None else total + term
    return total


def conv_act(x_ref, x_in, filt_ref, column, rows):
    x_ref[...] = x_in.astype(f32)
    running = None
    for tap in range(KCONV):
        term = filt_ref[pl.ds(column * KCONV + tap, 1), :] * x_ref[pl.ds(RIM - KCONV + 1 + tap, rows), :]
        running = term if running is None else running + term
    gate = jax.nn.sigmoid(running)
    return running, gate


def unit_scale(act):
    return lax.rsqrt(jnp.sum(act * act, axis=-1, keepdims=True) + epsilon)


def masks(rows):
    at_row = lax.broadcasted_iota(jnp.int32, (rows, rows), 0)
    at_col = lax.broadcasted_iota(jnp.int32, (rows, rows), 1)
    return at_row, at_col


def mixer_kernel(
    n, rows,
    pq_ref, pk_ref, pv_ref, strength_ref, filt_ref, gain_ref,
    normed_ref, mix_ref, carry_ref, inv_ref, kw_ref, state_ref,
    x_ref, low_ref, sol_ref, recv_ref, send_ref, send_sem, recv_sem,
):
    me = lax.axis_index("dp")
    seq, pair = pl.program_id(0), pl.program_id(1)
    step = seq * pl.num_programs(1) + pair
    steps = pl.num_programs(0) * pl.num_programs(1)

    def hop(at):
        return pltpu.make_async_remote_copy(
            src_ref=send_ref.at[at],
            dst_ref=recv_ref.at[at],
            send_sem=send_sem.at[at],
            recv_sem=recv_sem.at[at],
            device_id={"dp": lax.rem(me + 1, n)},
            device_id_type=MESH,
        )

    @pl.when(step == 0)
    def _():
        barrier = pltpu.get_barrier_semaphore()

        @pl.when(me > 0)
        def _():
            pl.semaphore_signal(barrier, inc=1, device_id={"dp": lax.rem(me + n - 1, n)}, device_id_type=MESH)

        @pl.when(me == 0)
        def _():
            recv_ref[...] = jnp.zeros_like(recv_ref)

        @pl.when(me < n - 1)
        def _():
            pl.semaphore_wait(barrier, 1)

    at_row, at_col = masks(rows)
    acts = []
    for column, ref in enumerate((pq_ref, pk_ref, pv_ref)):
        running, gate = conv_act(x_ref, ref[0], filt_ref, column, rows)
        acts.append(running * gate)
    strengths = strength_ref[0]
    lane = lax.broadcasted_iota(jnp.int32, strengths.shape, 1)
    heads = []
    for h in range(PAIR):
        cut = slice(h * HD, (h + 1) * HD)
        act_q, act_k = acts[0][:, cut], acts[1][:, cut]
        q = (act_q * unit_scale(act_q)).astype(bf16)
        k = (act_k * unit_scale(act_k)).astype(bf16)
        v = acts[2][:, cut].astype(bf16)
        beta = jnp.sum(jnp.where(lane == pair * PAIR + h, strengths, 0.0), axis=-1, keepdims=True)
        gram = product(k, k, 1, 1)
        low = jnp.where(at_row > at_col, beta * gram, 0.0)
        low_ref[h] = low
        first = (at_row & 1 == 1) & (at_row - 1 == at_col)
        sol_ref[h] = jnp.where(at_row == at_col, 1.0, 0.0) - jnp.where(first, low, 0.0)
        heads.append((q, k, v, beta))

    levels = (rows - 1).bit_length()

    def refine(level, carry):
        band_row, band_col = at_row >> level, at_col >> level
        band = (band_row & 1 == 1) & (band_row - 1 == band_col)
        sols = [halves(sol_ref[h]) for h in range(PAIR)]
        mids = [halves(product(halves(jnp.where(band, low_ref[h], 0.0)), sols[h])) for h in range(PAIR)]
        for h in range(PAIR):
            sol_ref[h] = sol_ref[h] - product(sols[h], mids[h])
        return carry

    lax.fori_loop(1, levels, refine, 0)

    wides = []
    for h in range(PAIR):
        q, k, v, beta = heads[h]
        inv = halves(sol_ref[h])
        inv_ref[h] = sol_ref[h]
        right = jnp.concatenate([beta * k.astype(f32), beta * v.astype(f32)], axis=1)
        wides.append(halves(product(inv, halves(right))))
    carries, bases, kws, ends = [], [], [], []
    for h in range(PAIR):
        q, k, v, beta = heads[h]
        scores = halves(jnp.where(at_row >= at_col, product(q, k, 1, 1), 0.0))
        seen = product(scores, wides[h])
        carry = q.astype(f32) - seen[:, :HD]
        carry_ref[0, :, h * HD : (h + 1) * HD] = carry
        carries.append(halves(carry))
        bases.append(seen[:, HD:])
        kwu = product(k, wides[h], 0, 0)
        kw_ref[h] = kwu[:, :HD]
        kws.append(halves(kwu[:, :HD]))
        ends.append(kwu[:, HD:])

    @pl.when(me > 0)
    def _():
        hop(step).wait_recv()

    states = [recv_ref[step, h] for h in range(PAIR)]
    for h in range(PAIR):
        out_state = ends[h] + states[h].astype(f32) - product(kws[h], states[h])
        send_ref[step, h] = out_state.astype(bf16)

    @pl.when(me < n - 1)
    def _():
        hop(step).start()

    for h in range(PAIR):
        cut = slice(h * HD, (h + 1) * HD)
        state_ref[h] = states[h]
        mix = bases[h] + product(carries[h], states[h])
        mix_ref[0, :, cut] = mix
        scale = lax.rsqrt(jnp.mean(mix * mix, axis=-1, keepdims=True) + epsilon)
        normed_ref[0, :, cut] = (mix * scale * gain_ref[...]).astype(bf16)

    @pl.when(step == steps - 1)
    def _():
        @pl.when(me < n - 1)
        def _():
            def done(at, carry):
                hop(at).wait_send()
                return carry

            lax.fori_loop(0, steps, done, 0)


def mixer(projected, strength, filters, gain):
    n = lax.axis_size("dp")
    seqs, extended, width = projected.shape
    rows = extended - RIM
    local = width // 3
    pairs = local // (PAIR * HD)
    wide = PAIR * HD

    def part(column):
        return pl.BlockSpec((1, extended, wide), lambda s, p: (s, 0, column * pairs + p))

    def flat():
        return pl.BlockSpec((1, rows, wide), lambda s, p: (s, 0, p))

    def square(size):
        return pl.BlockSpec((PAIR, size, size), lambda s, p: (s * pairs + p, 0, 0))

    total = seqs * pairs * PAIR
    return pl.pallas_call(
        functools.partial(mixer_kernel, n, rows),
        grid=(seqs, pairs),
        in_specs=[
            part(0), part(1), part(2),
            pl.BlockSpec((1, rows, strength.shape[2]), lambda s, p: (s, 0, 0)),
            pl.BlockSpec((3 * KCONV, wide), lambda s, p: (0, p)),
            pl.BlockSpec((1, HD), lambda s, p: (0, 0)),
        ],
        out_specs=[flat(), flat(), flat(), square(rows), square(HD), square(HD)],
        out_shape=[
            jax.ShapeDtypeStruct((seqs, rows, local), bf16),
            jax.ShapeDtypeStruct((seqs, rows, local), f32),
            jax.ShapeDtypeStruct((seqs, rows, local), f32),
            jax.ShapeDtypeStruct((total, rows, rows), f32),
            jax.ShapeDtypeStruct((total, HD, HD), f32),
            jax.ShapeDtypeStruct((total, HD, HD), bf16),
        ],
        scratch_shapes=[
            pltpu.VMEM((extended, wide), f32),
            pltpu.VMEM((PAIR, rows, rows), f32),
            pltpu.VMEM((PAIR, rows, rows), f32),
            pltpu.VMEM((seqs * pairs, PAIR, HD, HD), bf16),
            pltpu.VMEM((seqs * pairs, PAIR, HD, HD), bf16),
            pltpu.SemaphoreType.DMA((seqs * pairs,)),
            pltpu.SemaphoreType.DMA((seqs * pairs,)),
        ],
        compiler_params=pltpu.CompilerParams(
            collective_id=0, has_side_effects=True, vmem_limit_bytes=VMEM_LIMIT,
            dimension_semantics=("arbitrary", "arbitrary"),
        ),
        name="mixer",
    )(projected, projected, projected, strength, filters, gain)


def mixer_back_kernel(
    n, rows,
    pq_ref, pk_ref, pv_ref, strength_ref, filt_ref, gain_ref,
    back_ref, mix_ref, carry_ref, inv_ref, kw_ref, state_ref,
    proj_ref, last_ref, rim_ref, logit_ref, conv_ref, head_ref,
    xq_ref, xk_ref, xv_ref, bc_ref, recv_ref, send_ref, send_sem, recv_sem,
):
    me = lax.axis_index("dp")
    seq, pair = pl.program_id(0), pl.program_id(1)
    pairs = pl.num_programs(1)
    step = seq * pairs + pair
    steps = pl.num_programs(0) * pairs
    wide = PAIR * HD
    local = proj_ref.shape[2] // 3

    def hop(at):
        return pltpu.make_async_remote_copy(
            src_ref=send_ref.at[at],
            dst_ref=recv_ref.at[at],
            send_sem=send_sem.at[at],
            recv_sem=recv_sem.at[at],
            device_id={"dp": lax.rem(me + n - 1, n)},
            device_id_type=MESH,
        )

    @pl.when(step == 0)
    def _():
        barrier = pltpu.get_barrier_semaphore()

        @pl.when(me < n - 1)
        def _():
            pl.semaphore_signal(barrier, inc=1, device_id={"dp": lax.rem(me + 1, n)}, device_id_type=MESH)

        @pl.when(me == n - 1)
        def _():
            recv_ref[...] = jnp.zeros_like(recv_ref)

        @pl.when(me > 0)
        def _():
            pl.semaphore_wait(barrier, 1)

        head_ref[...] = jnp.zeros_like(head_ref)
        bc_ref[...] = jnp.zeros_like(bc_ref)
        conv_ref[...] = jnp.zeros_like(conv_ref)

    @pl.when(pair == 0)
    def _():
        logit_ref[...] = jnp.zeros_like(logit_ref)

    outs, kws, adds = [], [], []
    head_sum = jnp.zeros((1, HD), f32)
    for h in range(PAIR):
        cut = slice(h * HD, (h + 1) * HD)
        mix, back = mix_ref[0, :, cut], back_ref[0, :, cut]
        scale = lax.rsqrt(jnp.mean(mix * mix, axis=-1, keepdims=True) + epsilon)
        unit = mix * scale
        head_sum = head_sum + jnp.sum(back * unit, axis=0, keepdims=True)
        scaled = back * gain_ref[...]
        out = scale * (scaled - unit * jnp.mean(scaled * unit, axis=-1, keepdims=True))
        outs.append(halves(out))
        adds.append(product(halves(carry_ref[0, :, cut]), outs[h], 0, 0))
        kws.append(halves(kw_ref[h]))
    head_ref[...] += jnp.broadcast_to(head_sum, head_ref.shape) * jnp.where(
        lax.broadcasted_iota(jnp.int32, head_ref.shape, 0) == 0, 1.0, 0.0
    )

    @pl.when(me < n - 1)
    def _():
        hop(step).wait_recv()

    ends = [recv_ref[step, h] for h in range(PAIR)]
    for h in range(PAIR):
        before = adds[h] + ends[h].astype(f32) - product(kws[h], ends[h], 0, 0)
        send_ref[step, h] = before.astype(bf16)

    @pl.when(me > 0)
    def _():
        hop(step).start()

    at_row, at_col = masks(rows)
    strengths = strength_ref[0]
    lane = lax.broadcasted_iota(jnp.int32, strengths.shape, 1)
    run_q, gate_q = conv_act(xq_ref, pq_ref[0], filt_ref, 0, rows)
    run_k, gate_k = conv_act(xk_ref, pk_ref[0], filt_ref, 1, rows)
    run_v, gate_v = conv_act(xv_ref, pv_ref[0], filt_ref, 2, rows)
    act_q, act_k, act_v = run_q * gate_q, run_k * gate_k, run_v * gate_v
    back_acts = ([], [], [])
    for h in range(PAIR):
        cut = slice(h * HD, (h + 1) * HD)
        scale_q, scale_k = unit_scale(act_q[:, cut]), unit_scale(act_k[:, cut])
        unit_q, unit_k = act_q[:, cut] * scale_q, act_k[:, cut] * scale_k
        q, k, v = unit_q.astype(bf16), unit_k.astype(bf16), act_v[:, cut].astype(bf16)
        chosen = lane == pair * PAIR + h
        beta = jnp.sum(jnp.where(chosen, strengths, 0.0), axis=-1, keepdims=True)
        gram = product(k, k, 1, 1)
        scores = halves(jnp.where(at_row >= at_col, product(q, k, 1, 1), 0.0))
        state, end, out = state_ref[h], ends[h], outs[h]
        inv = halves(inv_ref[h])
        rest = v.astype(f32) - product(k, state)
        update = halves(product(inv, halves(beta * rest)))
        back_update = product(scores, out, 0, 0) + product(k, end)
        back_scores = halves(jnp.where(at_row >= at_col, product(out, update, 1, 1), 0.0))
        solved = product(inv, halves(back_update), 0, 0)
        solved_terms = halves(solved)
        back_low = jnp.where(at_row > at_col, -product(solved_terms, update, 1, 1), 0.0)
        back_beta = jnp.sum(back_low * gram, axis=-1, keepdims=True) + jnp.sum(
            solved * rest, axis=-1, keepdims=True
        )
        back_gram = beta * back_low
        back_gram = halves(back_gram + back_gram.T)
        back_value = beta * solved
        back_q = product(out, state, 1, 1) + product(back_scores, k)
        back_k = (
            product(back_scores, q, 0, 0)
            + product(update, end, 1, 1)
            + product(back_gram, k)
            - product(halves(back_value), state, 1, 1)
        )
        logit_ref[0] += jnp.where(chosen, back_beta * beta * (1.0 - beta), 0.0)
        back_acts[0].append(
            (back_q - unit_q * jnp.sum(unit_q * back_q, axis=-1, keepdims=True)) * scale_q
        )
        back_acts[1].append(
            (back_k - unit_k * jnp.sum(unit_k * back_k, axis=-1, keepdims=True)) * scale_k
        )
        back_acts[2].append(back_value)

    for column, (running, gate, x_ref) in enumerate(
        ((run_q, gate_q, xq_ref), (run_k, gate_k, xk_ref), (run_v, gate_v, xv_ref))
    ):
        back_conv = jnp.concatenate(back_acts[column], axis=1) * gate * (1.0 + running * (1.0 - gate))
        bc_ref[pl.ds(RIM, rows), :] = back_conv
        back_x, back_rim = None, None
        for tap in range(KCONV):
            weight = filt_ref[pl.ds(column * KCONV + tap, 1), :]
            term = weight * bc_ref[pl.ds(RIM + KCONV - 1 - tap, rows), :]
            edge = weight * bc_ref[pl.ds(KCONV - 1 - tap, RIM), :]
            back_x = term if back_x is None else back_x + term
            back_rim = edge if back_rim is None else back_rim + edge
            grad = jnp.sum(
                back_conv * x_ref[pl.ds(RIM - KCONV + 1 + tap, rows), :], axis=0, keepdims=True
            )
            conv_ref[pair, pl.ds(column * KCONV + tap, 1), :] += grad
        lanes = pl.ds(pl.multiple_of(column * local + pair * wide, wide), wide)
        proj_ref[0, :, lanes] = back_x.astype(bf16)
        last_ref[0, :, lanes] = back_x[rows - RIM :, :]
        rim_ref[0, :, lanes] = back_rim.astype(bf16)

    @pl.when(step == steps - 1)
    def _():
        @pl.when(me > 0)
        def _():
            def done(at, carry):
                hop(at).wait_send()
                return carry

            lax.fori_loop(0, steps, done, 0)


def mixer_back(projected, strength, filters, gain, back_normed, mix, carry, inverse, kw, state):
    n = lax.axis_size("dp")
    seqs, extended, width = projected.shape
    rows = extended - RIM
    local = width // 3
    pairs = local // (PAIR * HD)
    wide = PAIR * HD

    def part(column):
        return pl.BlockSpec((1, extended, wide), lambda s, p: (s, 0, column * pairs + p))

    def flat():
        return pl.BlockSpec((1, rows, wide), lambda s, p: (s, 0, p))

    def square(size):
        return pl.BlockSpec((PAIR, size, size), lambda s, p: (s * pairs + p, 0, 0))

    def whole(size, span):
        return pl.BlockSpec((1, size, span), lambda s, p: (s, 0, 0))

    heads = strength.shape[2]
    return pl.pallas_call(
        functools.partial(mixer_back_kernel, n, rows),
        grid=(seqs, pairs),
        in_specs=[
            part(0), part(1), part(2),
            whole(rows, heads),
            pl.BlockSpec((3 * KCONV, wide), lambda s, p: (0, p)),
            pl.BlockSpec((1, HD), lambda s, p: (0, 0)),
            flat(), flat(), flat(), square(rows), square(HD), square(HD),
        ],
        out_specs=[
            whole(rows, width), whole(RIM, width), whole(RIM, width), whole(rows, heads),
            pl.BlockSpec((pairs, 3 * KCONV, wide), lambda s, p: (0, 0, 0)),
            pl.BlockSpec((8, HD), lambda s, p: (0, 0)),
        ],
        out_shape=[
            jax.ShapeDtypeStruct((seqs, rows, width), bf16),
            jax.ShapeDtypeStruct((seqs, RIM, width), f32),
            jax.ShapeDtypeStruct((seqs, RIM, width), bf16),
            jax.ShapeDtypeStruct((seqs, rows, heads), f32),
            jax.ShapeDtypeStruct((pairs, 3 * KCONV, wide), f32),
            jax.ShapeDtypeStruct((8, HD), f32),
        ],
        scratch_shapes=[
            pltpu.VMEM((extended, wide), f32),
            pltpu.VMEM((extended, wide), f32),
            pltpu.VMEM((extended, wide), f32),
            pltpu.VMEM((rows + 2 * RIM, wide), f32),
            pltpu.VMEM((seqs * pairs, PAIR, HD, HD), bf16),
            pltpu.VMEM((seqs * pairs, PAIR, HD, HD), bf16),
            pltpu.SemaphoreType.DMA((seqs * pairs,)),
            pltpu.SemaphoreType.DMA((seqs * pairs,)),
        ],
        compiler_params=pltpu.CompilerParams(
            collective_id=1, has_side_effects=True, vmem_limit_bytes=VMEM_LIMIT,
            dimension_semantics=("arbitrary", "arbitrary"),
        ),
        name="mixer_back",
    )(
        projected, projected, projected, strength, filters, gain,
        back_normed, mix, carry, inverse, kw, state,
    )


def from_behind(block, axis, distance):
    devices = range(lax.axis_size(axis))
    route = [(i - distance, i) for i in devices if i - distance in devices]
    return lax.ppermute(block, axis, route)


def rms_unit(values):
    scale = lax.rsqrt(jnp.mean(values * values, axis=-1, keepdims=True) + epsilon)
    return values * scale, scale


def rms_back(back, unit, scale, gain):
    scaled = back * gain
    return scale * (scaled - unit * jnp.mean(scaled * unit, axis=-1, keepdims=True))


def matmul(spec, left, right):
    return jnp.einsum(spec, left, right, preferred_element_type=f32)


def shards(
    tokens,
    cotangent,
    query_weight,
    key_weight,
    value_weight,
    beta_weight,
    conv_filter,
    norm_gain,
    head_gain,
    out_weight,
    gate_weight,
    up_weight,
    down_weight,
):
    n = lax.axis_size("dp")
    tensor = lax.axis_size("tensor")
    seqs, own_len, width = tokens.shape
    local = query_weight.shape[1]
    heads = local // HD
    hidden = gate_weight.shape[1]

    full_small = lax.all_gather(
        jnp.concatenate(
            [conv_filter.reshape(-1), norm_gain.reshape(-1), head_gain, beta_weight.reshape(-1)]
        ),
        "dp",
    )
    full_qkv = lax.all_gather(
        jnp.concatenate([query_weight, key_weight, value_weight], axis=1), "dp", axis=0, tiled=True
    )
    full_out = lax.all_gather(out_weight.T, "dp", axis=0, tiled=True)
    full_gate_up = lax.all_gather(
        jnp.concatenate([gate_weight, up_weight], axis=1), "dp", axis=0, tiled=True
    )
    full_down = lax.all_gather(down_weight.T, "dp", axis=0, tiled=True)
    sizes = [conv_filter.size, norm_gain.size, head_gain.size, beta_weight.size]
    ends = [sum(sizes[: i + 1]) for i in range(4)]
    filters = (
        full_small[:, : ends[0]]
        .reshape(n, 3 * KCONV, heads, HD // n)
        .transpose(1, 2, 0, 3)
        .reshape(3 * KCONV, local)
        .astype(f32)
    )
    gains = (
        full_small[:, ends[0] : ends[1]].reshape(n, 2, width // n).transpose(1, 0, 2).reshape(2, width)
    ).astype(f32)
    head_row = full_small[:, ends[1] : ends[2]].reshape(1, HD).astype(f32)
    full_beta = full_small[:, ends[2] :].reshape(width, heads)

    rows_tokens = lax.all_gather(tokens, "tensor", axis=1, tiled=True)
    rows_cotangent = lax.all_gather(cotangent, "tensor", axis=1, tiled=True)
    rim_tokens = from_behind(rows_tokens[:, -RIM:], "dp", 1)
    extended = jnp.concatenate([rim_tokens, rows_tokens], axis=1).astype(f32)
    unit_ext, _ = rms_unit(extended)
    normed_ext = (unit_ext * gains[0]).astype(bf16)
    normed_first = normed_ext[:, RIM:]
    projected = matmul("std,dm->stm", normed_ext, full_qkv).astype(bf16)
    strength = jax.nn.sigmoid(matmul("std,dh->sth", normed_first, full_beta))
    normed_mix, mix, carry, inverse, kw, state = mixer(projected, strength, filters, head_row)

    branch_part = matmul("stk,dk->std", normed_mix, full_out)
    branch = lax.psum_scatter(branch_part.astype(bf16), "tensor", scatter_dimension=1, tiled=True)
    own_tokens = tokens.astype(f32)
    hidden_state = own_tokens + branch.astype(f32)
    unit_second, scale_second = rms_unit(hidden_state)
    normed_second = lax.all_gather(
        (unit_second * gains[1]).astype(bf16), "tensor", axis=1, tiled=True
    )
    gate_up = matmul("std,df->stf", normed_second, full_gate_up)
    gate_pre, up_pre = gate_up[..., :hidden], gate_up[..., hidden:]
    gate_sigmoid = jax.nn.sigmoid(gate_pre)
    ffn_hidden = (gate_pre * gate_sigmoid * up_pre).astype(bf16)
    ffn_part = matmul("stf,df->std", ffn_hidden, full_down)
    ffn_branch = lax.psum_scatter(
        ffn_part.astype(bf16), "tensor", scatter_dimension=1, tiled=True
    ).astype(f32)
    layer_out = (hidden_state + ffn_branch).astype(bf16)

    back_hidden = matmul("std,df->stf", rows_cotangent, full_down)
    back_gate = (
        back_hidden * up_pre * gate_sigmoid * (1.0 + gate_pre * (1.0 - gate_sigmoid))
    ).astype(bf16)
    back_up = (back_hidden * gate_pre * gate_sigmoid).astype(bf16)
    back_gate_up = jnp.concatenate([back_gate, back_up], axis=2)
    back_second = matmul("stf,df->std", back_gate_up, full_gate_up)
    back_second_rows = lax.psum_scatter(
        back_second.astype(bf16), "tensor", scatter_dimension=1, tiled=True
    ).astype(f32)
    grad_down = matmul("std,stf->df", rows_cotangent, ffn_hidden)
    grad_gate_up = matmul("std,stf->df", normed_second, back_gate_up)
    gain_second = jnp.sum(back_second_rows * unit_second, axis=(0, 1))
    back_state = cotangent.astype(f32) + rms_back(back_second_rows, unit_second, scale_second, gains[1])
    rows_back = lax.all_gather(back_state.astype(bf16), "tensor", axis=1, tiled=True)
    grad_out = matmul("std,stk->dk", rows_back, normed_mix)
    back_normed = matmul("std,dk->stk", rows_back, full_out)
    back_proj, last, rim, back_logit, conv_part, head_part = mixer_back(
        projected, strength, filters, head_row, back_normed, mix, carry, inverse, kw, state
    )
    rim = from_behind(rim, "dp", -1).astype(f32)
    back_proj = lax.dynamic_update_slice_in_dim(
        back_proj, (last + rim).astype(bf16), back_proj.shape[1] - RIM, 1
    )
    back_logit = back_logit.astype(bf16)
    grad_qkv = matmul("std,stm->dm", normed_first, back_proj)
    grad_beta = matmul("std,sth->dh", normed_first, back_logit)
    back_first = matmul("stm,dm->std", back_proj, full_qkv) + matmul(
        "sth,dh->std", back_logit, full_beta
    )
    back_first_rows = lax.psum_scatter(
        back_first.astype(bf16), "tensor", scatter_dimension=1, tiled=True
    ).astype(f32)
    unit_first, scale_first = rms_unit(own_tokens)
    gain_first = jnp.sum(back_first_rows * unit_first, axis=(0, 1))
    d_tokens = (back_state + rms_back(back_first_rows, unit_first, scale_first, gains[0])).astype(bf16)

    grad_conv = conv_part.transpose(1, 0, 2).reshape(3 * KCONV, local)
    shared = lax.psum(jnp.concatenate([gain_first, gain_second, head_part[0]]), "tensor")

    def scatter(grad):
        return lax.psum_scatter(grad.astype(bf16), "dp", scatter_dimension=0, tiled=True).astype(f32)

    small = jnp.concatenate(
        [
            grad_conv.reshape(3 * KCONV, heads, n, HD // n).transpose(2, 0, 1, 3).reshape(n, -1),
            shared[: 2 * width].reshape(2, n, width // n).transpose(1, 0, 2).reshape(n, -1),
            shared[2 * width :].reshape(n, HD // n),
            grad_beta.reshape(n, -1),
        ],
        axis=1,
    )
    small = scatter(small)[0]
    grad_down = scatter(grad_down).T
    grad_gate_up = scatter(grad_gate_up)
    grad_out = scatter(grad_out).T
    grad_qkv = scatter(grad_qkv)
    return (
        layer_out,
        d_tokens,
        grad_qkv[:, :local],
        grad_qkv[:, local : 2 * local],
        grad_qkv[:, 2 * local :],
        small[ends[2] :].reshape(beta_weight.shape),
        small[: ends[0]].reshape(conv_filter.shape),
        small[ends[0] : ends[1]].reshape(norm_gain.shape),
        small[ends[1] : ends[2]],
        grad_out,
        grad_gate_up[:, :hidden],
        grad_gate_up[:, hidden:],
        grad_down,
    )


def solution(mesh):
    both = P(None, ("dp", "tensor"), None)
    rows, cols = P("dp", "tensor"), P("tensor", "dp")
    conv, gain, head = P(None, "tensor", "dp"), P(None, "dp"), P("dp")
    return jax.shard_map(
        shards,
        mesh=mesh,
        in_specs=(both, both, rows, rows, rows, rows, conv, gain, head, cols, rows, rows, cols),
        out_specs=(both, both, rows, rows, rows, rows, conv, gain, head, cols, rows, rows, cols),
        check_vma=False,
    )
```

```python
import functools

import jax
import jax.numpy as jnp
from jax import lax
from jax.experimental import pallas as pl
from jax.experimental.pallas import tpu as pltpu
from jax.sharding import PartitionSpec as P

HD = 128
KCONV = 4
RIM = 8
PAIR = 2

epsilon = 1e-06
f32 = jnp.float32
bf16 = jnp.bfloat16
MESH = pl.DeviceIdType.MESH
VMEM_LIMIT = 60 * 1024 * 1024


def halves(value):
    high = value.astype(bf16)
    return (high, (value - high.astype(f32)).astype(bf16))


def product(left, right, left_dim=1, right_dim=0):
    left = left if isinstance(left, tuple) else (left,)
    right = right if isinstance(right, tuple) else (right,)
    total = None
    for i, a in enumerate(left):
        for j, b in enumerate(right):
            if i + j < 2:
                term = lax.dot_general(
                    a, b, (((left_dim,), (right_dim,)), ((), ())), preferred_element_type=f32
                )
                total = term if total is None else total + term
    return total


def conv_act(x_ref, x_in, filt_ref, column, rows):
    x_ref[...] = x_in.astype(f32)
    running = None
    for tap in range(KCONV):
        term = filt_ref[pl.ds(column * KCONV + tap, 1), :] * x_ref[pl.ds(RIM - KCONV + 1 + tap, rows), :]
        running = term if running is None else running + term
    gate = jax.nn.sigmoid(running)
    return running, gate


def unit_scale(act):
    return lax.rsqrt(jnp.sum(act * act, axis=-1, keepdims=True) + epsilon)


def masks(rows):
    at_row = lax.broadcasted_iota(jnp.int32, (rows, rows), 0)
    at_col = lax.broadcasted_iota(jnp.int32, (rows, rows), 1)
    return at_row, at_col


def mixer_kernel(
    n, rows,
    pq_ref, pk_ref, pv_ref, strength_ref, filt_ref, gain_ref,
    normed_ref, mix_ref, carry_ref, inv_ref, kw_ref, state_ref,
    x_ref, low_ref, sol_ref, recv_ref, send_ref, send_sem, recv_sem,
):
    me = lax.axis_index("dp")
    seq, pair = pl.program_id(0), pl.program_id(1)
    step = seq * pl.num_programs(1) + pair
    steps = pl.num_programs(0) * pl.num_programs(1)

    def hop(at):
        return pltpu.make_async_remote_copy(
            src_ref=send_ref.at[at],
            dst_ref=recv_ref.at[at],
            send_sem=send_sem.at[at],
            recv_sem=recv_sem.at[at],
            device_id={"dp": lax.rem(me + 1, n)},
            device_id_type=MESH,
        )

    @pl.when(step == 0)
    def _():
        barrier = pltpu.get_barrier_semaphore()

        @pl.when(me > 0)
        def _():
            pl.semaphore_signal(barrier, inc=1, device_id={"dp": lax.rem(me + n - 1, n)}, device_id_type=MESH)

        @pl.when(me == 0)
        def _():
            recv_ref[...] = jnp.zeros_like(recv_ref)

        @pl.when(me < n - 1)
        def _():
            pl.semaphore_wait(barrier, 1)

    at_row, at_col = masks(rows)
    acts = []
    for column, ref in enumerate((pq_ref, pk_ref, pv_ref)):
        running, gate = conv_act(x_ref, ref[0], filt_ref, column, rows)
        acts.append(running * gate)
    strengths = strength_ref[0]
    lane = lax.broadcasted_iota(jnp.int32, strengths.shape, 1)
    heads = []
    for h in range(PAIR):
        cut = slice(h * HD, (h + 1) * HD)
        act_q, act_k = acts[0][:, cut], acts[1][:, cut]
        q = (act_q * unit_scale(act_q)).astype(bf16)
        k = (act_k * unit_scale(act_k)).astype(bf16)
        v = acts[2][:, cut].astype(bf16)
        beta = jnp.sum(jnp.where(lane == pair * PAIR + h, strengths, 0.0), axis=-1, keepdims=True)
        gram = product(k, k, 1, 1)
        low = jnp.where(at_row > at_col, beta * gram, 0.0)
        low_ref[h] = low
        first = (at_row & 1 == 1) & (at_row - 1 == at_col)
        sol_ref[h] = jnp.where(at_row == at_col, 1.0, 0.0) - jnp.where(first, low, 0.0)
        heads.append((q, k, v, beta))

    levels = (rows - 1).bit_length()

    def refine(level, carry):
        band_row, band_col = at_row >> level, at_col >> level
        band = (band_row & 1 == 1) & (band_row - 1 == band_col)
        sols = [halves(sol_ref[h]) for h in range(PAIR)]
        mids = [halves(product(halves(jnp.where(band, low_ref[h], 0.0)), sols[h])) for h in range(PAIR)]
        for h in range(PAIR):
            sol_ref[h] = sol_ref[h] - product(sols[h], mids[h])
        return carry

    lax.fori_loop(1, levels, refine, 0)

    wides = []
    for h in range(PAIR):
        q, k, v, beta = heads[h]
        inv = halves(sol_ref[h])
        inv_ref[h] = sol_ref[h]
        right = jnp.concatenate([beta * k.astype(f32), beta * v.astype(f32)], axis=1)
        wides.append(halves(product(inv, halves(right))))
    carries, bases, kws, ends = [], [], [], []
    for h in range(PAIR):
        q, k, v, beta = heads[h]
        scores = halves(jnp.where(at_row >= at_col, product(q, k, 1, 1), 0.0))
        seen = product(scores, wides[h])
        carry = q.astype(f32) - seen[:, :HD]
        carry_ref[0, :, h * HD : (h + 1) * HD] = carry
        carries.append(halves(carry))
        bases.append(seen[:, HD:])
        kwu = product(k, wides[h], 0, 0)
        kw_ref[h] = kwu[:, :HD]
        kws.append(halves(kwu[:, :HD]))
        ends.append(kwu[:, HD:])

    @pl.when(me > 0)
    def _():
        hop(step).wait_recv()

    states = [recv_ref[step, h] for h in range(PAIR)]
    for h in range(PAIR):
        out_state = ends[h] + states[h].astype(f32) - product(kws[h], states[h])
        send_ref[step, h] = out_state.astype(bf16)

    @pl.when(me < n - 1)
    def _():
        hop(step).start()

    for h in range(PAIR):
        cut = slice(h * HD, (h + 1) * HD)
        state_ref[h] = states[h]
        mix = bases[h] + product(carries[h], states[h])
        mix_ref[0, :, cut] = mix
        scale = lax.rsqrt(jnp.mean(mix * mix, axis=-1, keepdims=True) + epsilon)
        normed_ref[0, :, cut] = (mix * scale * gain_ref[...]).astype(bf16)

    @pl.when(step == steps - 1)
    def _():
        @pl.when(me < n - 1)
        def _():
            def done(at, carry):
                hop(at).wait_send()
                return carry

            lax.fori_loop(0, steps, done, 0)


def mixer(projected, strength, filters, gain):
    n = lax.axis_size("dp")
    seqs, extended, width = projected.shape
    rows = extended - RIM
    local = width // 3
    pairs = local // (PAIR * HD)
    wide = PAIR * HD

    def part(column):
        return pl.BlockSpec((1, extended, wide), lambda s, p: (s, 0, column * pairs + p))

    def flat():
        return pl.BlockSpec((1, rows, wide), lambda s, p: (s, 0, p))

    def square(size):
        return pl.BlockSpec((PAIR, size, size), lambda s, p: (s * pairs + p, 0, 0))

    total = seqs * pairs * PAIR
    return pl.pallas_call(
        functools.partial(mixer_kernel, n, rows),
        grid=(seqs, pairs),
        in_specs=[
            part(0), part(1), part(2),
            pl.BlockSpec((1, rows, strength.shape[2]), lambda s, p: (s, 0, 0)),
            pl.BlockSpec((3 * KCONV, wide), lambda s, p: (0, p)),
            pl.BlockSpec((1, HD), lambda s, p: (0, 0)),
        ],
        out_specs=[flat(), flat(), flat(), square(rows), square(HD), square(HD)],
        out_shape=[
            jax.ShapeDtypeStruct((seqs, rows, local), bf16),
            jax.ShapeDtypeStruct((seqs, rows, local), f32),
            jax.ShapeDtypeStruct((seqs, rows, local), f32),
            jax.ShapeDtypeStruct((total, rows, rows), f32),
            jax.ShapeDtypeStruct((total, HD, HD), f32),
            jax.ShapeDtypeStruct((total, HD, HD), bf16),
        ],
        scratch_shapes=[
            pltpu.VMEM((extended, wide), f32),
            pltpu.VMEM((PAIR, rows, rows), f32),
            pltpu.VMEM((PAIR, rows, rows), f32),
            pltpu.VMEM((seqs * pairs, PAIR, HD, HD), bf16),
            pltpu.VMEM((seqs * pairs, PAIR, HD, HD), bf16),
            pltpu.SemaphoreType.DMA((seqs * pairs,)),
            pltpu.SemaphoreType.DMA((seqs * pairs,)),
        ],
        compiler_params=pltpu.CompilerParams(
            collective_id=0, has_side_effects=True, vmem_limit_bytes=VMEM_LIMIT,
            dimension_semantics=("arbitrary", "arbitrary"),
        ),
        name="mixer",
    )(projected, projected, projected, strength, filters, gain)


def mixer_back_kernel(
    n, rows,
    pq_ref, pk_ref, pv_ref, strength_ref, filt_ref, gain_ref,
    back_ref, mix_ref, carry_ref, inv_ref, kw_ref, state_ref,
    proj_ref, last_ref, rim_ref, logit_ref, conv_ref, head_ref,
    xq_ref, xk_ref, xv_ref, bc_ref, recv_ref, send_ref, send_sem, recv_sem,
):
    me = lax.axis_index("dp")
    seq, pair = pl.program_id(0), pl.program_id(1)
    pairs = pl.num_programs(1)
    step = seq * pairs + pair
    steps = pl.num_programs(0) * pairs
    wide = PAIR * HD
    local = proj_ref.shape[2] // 3

    def hop(at):
        return pltpu.make_async_remote_copy(
            src_ref=send_ref.at[at],
            dst_ref=recv_ref.at[at],
            send_sem=send_sem.at[at],
            recv_sem=recv_sem.at[at],
            device_id={"dp": lax.rem(me + n - 1, n)},
            device_id_type=MESH,
        )

    @pl.when(step == 0)
    def _():
        barrier = pltpu.get_barrier_semaphore()

        @pl.when(me < n - 1)
        def _():
            pl.semaphore_signal(barrier, inc=1, device_id={"dp": lax.rem(me + 1, n)}, device_id_type=MESH)

        @pl.when(me == n - 1)
        def _():
            recv_ref[...] = jnp.zeros_like(recv_ref)

        @pl.when(me > 0)
        def _():
            pl.semaphore_wait(barrier, 1)

        head_ref[...] = jnp.zeros_like(head_ref)
        bc_ref[...] = jnp.zeros_like(bc_ref)
        conv_ref[...] = jnp.zeros_like(conv_ref)

    @pl.when(pair == 0)
    def _():
        logit_ref[...] = jnp.zeros_like(logit_ref)

    outs, kws, adds = [], [], []
    head_sum = jnp.zeros((1, HD), f32)
    for h in range(PAIR):
        cut = slice(h * HD, (h + 1) * HD)
        mix, back = mix_ref[0, :, cut], back_ref[0, :, cut]
        scale = lax.rsqrt(jnp.mean(mix * mix, axis=-1, keepdims=True) + epsilon)
        unit = mix * scale
        head_sum = head_sum + jnp.sum(back * unit, axis=0, keepdims=True)
        scaled = back * gain_ref[...]
        out = scale * (scaled - unit * jnp.mean(scaled * unit, axis=-1, keepdims=True))
        outs.append(halves(out))
        adds.append(product(halves(carry_ref[0, :, cut]), outs[h], 0, 0))
        kws.append(halves(kw_ref[h]))
    head_ref[...] += jnp.broadcast_to(head_sum, head_ref.shape) * jnp.where(
        lax.broadcasted_iota(jnp.int32, head_ref.shape, 0) == 0, 1.0, 0.0
    )

    @pl.when(me < n - 1)
    def _():
        hop(step).wait_recv()

    ends = [recv_ref[step, h] for h in range(PAIR)]
    for h in range(PAIR):
        before = adds[h] + ends[h].astype(f32) - product(kws[h], ends[h], 0, 0)
        send_ref[step, h] = before.astype(bf16)

    @pl.when(me > 0)
    def _():
        hop(step).start()

    at_row, at_col = masks(rows)
    strengths = strength_ref[0]
    lane = lax.broadcasted_iota(jnp.int32, strengths.shape, 1)
    run_q, gate_q = conv_act(xq_ref, pq_ref[0], filt_ref, 0, rows)
    run_k, gate_k = conv_act(xk_ref, pk_ref[0], filt_ref, 1, rows)
    run_v, gate_v = conv_act(xv_ref, pv_ref[0], filt_ref, 2, rows)
    act_q, act_k, act_v = run_q * gate_q, run_k * gate_k, run_v * gate_v
    back_acts = ([], [], [])
    for h in range(PAIR):
        cut = slice(h * HD, (h + 1) * HD)
        scale_q, scale_k = unit_scale(act_q[:, cut]), unit_scale(act_k[:, cut])
        unit_q, unit_k = act_q[:, cut] * scale_q, act_k[:, cut] * scale_k
        q, k, v = unit_q.astype(bf16), unit_k.astype(bf16), act_v[:, cut].astype(bf16)
        chosen = lane == pair * PAIR + h
        beta = jnp.sum(jnp.where(chosen, strengths, 0.0), axis=-1, keepdims=True)
        gram = product(k, k, 1, 1)
        scores = halves(jnp.where(at_row >= at_col, product(q, k, 1, 1), 0.0))
        state, end, out = state_ref[h], ends[h], outs[h]
        inv = halves(inv_ref[h])
        rest = v.astype(f32) - product(k, state)
        update = halves(product(inv, halves(beta * rest)))
        back_update = product(scores, out, 0, 0) + product(k, end)
        back_scores = halves(jnp.where(at_row >= at_col, product(out, update, 1, 1), 0.0))
        solved = product(inv, halves(back_update), 0, 0)
        solved_terms = halves(solved)
        back_low = jnp.where(at_row > at_col, -product(solved_terms, update, 1, 1), 0.0)
        back_beta = jnp.sum(back_low * gram, axis=-1, keepdims=True) + jnp.sum(
            solved * rest, axis=-1, keepdims=True
        )
        back_gram = beta * back_low
        back_gram = halves(back_gram + back_gram.T)
        back_value = beta * solved
        back_q = product(out, state, 1, 1) + product(back_scores, k)
        back_k = (
            product(back_scores, q, 0, 0)
            + product(update, end, 1, 1)
            + product(back_gram, k)
            - product(halves(back_value), state, 1, 1)
        )
        logit_ref[0] += jnp.where(chosen, back_beta * beta * (1.0 - beta), 0.0)
        back_acts[0].append(
            (back_q - unit_q * jnp.sum(unit_q * back_q, axis=-1, keepdims=True)) * scale_q
        )
        back_acts[1].append(
            (back_k - unit_k * jnp.sum(unit_k * back_k, axis=-1, keepdims=True)) * scale_k
        )
        back_acts[2].append(back_value)

    for column, (running, gate, x_ref) in enumerate(
        ((run_q, gate_q, xq_ref), (run_k, gate_k, xk_ref), (run_v, gate_v, xv_ref))
    ):
        back_conv = jnp.concatenate(back_acts[column], axis=1) * gate * (1.0 + running * (1.0 - gate))
        bc_ref[pl.ds(RIM, rows), :] = back_conv
        back_x, back_rim = None, None
        for tap in range(KCONV):
            weight = filt_ref[pl.ds(column * KCONV + tap, 1), :]
            term = weight * bc_ref[pl.ds(RIM + KCONV - 1 - tap, rows), :]
            edge = weight * bc_ref[pl.ds(KCONV - 1 - tap, RIM), :]
            back_x = term if back_x is None else back_x + term
            back_rim = edge if back_rim is None else back_rim + edge
            grad = jnp.sum(
                back_conv * x_ref[pl.ds(RIM - KCONV + 1 + tap, rows), :], axis=0, keepdims=True
            )
            conv_ref[pair, pl.ds(column * KCONV + tap, 1), :] += grad
        lanes = pl.ds(pl.multiple_of(column * local + pair * wide, wide), wide)
        proj_ref[0, :, lanes] = back_x.astype(bf16)
        last_ref[0, :, lanes] = back_x[rows - RIM :, :]
        rim_ref[0, :, lanes] = back_rim.astype(bf16)

    @pl.when(step == steps - 1)
    def _():
        @pl.when(me > 0)
        def _():
            def done(at, carry):
                hop(at).wait_send()
                return carry

            lax.fori_loop(0, steps, done, 0)


def mixer_back(projected, strength, filters, gain, back_normed, mix, carry, inverse, kw, state):
    n = lax.axis_size("dp")
    seqs, extended, width = projected.shape
    rows = extended - RIM
    local = width // 3
    pairs = local // (PAIR * HD)
    wide = PAIR * HD

    def part(column):
        return pl.BlockSpec((1, extended, wide), lambda s, p: (s, 0, column * pairs + p))

    def flat():
        return pl.BlockSpec((1, rows, wide), lambda s, p: (s, 0, p))

    def square(size):
        return pl.BlockSpec((PAIR, size, size), lambda s, p: (s * pairs + p, 0, 0))

    def whole(size, span):
        return pl.BlockSpec((1, size, span), lambda s, p: (s, 0, 0))

    heads = strength.shape[2]
    return pl.pallas_call(
        functools.partial(mixer_back_kernel, n, rows),
        grid=(seqs, pairs),
        in_specs=[
            part(0), part(1), part(2),
            whole(rows, heads),
            pl.BlockSpec((3 * KCONV, wide), lambda s, p: (0, p)),
            pl.BlockSpec((1, HD), lambda s, p: (0, 0)),
            flat(), flat(), flat(), square(rows), square(HD), square(HD),
        ],
        out_specs=[
            whole(rows, width), whole(RIM, width), whole(RIM, width), whole(rows, heads),
            pl.BlockSpec((pairs, 3 * KCONV, wide), lambda s, p: (0, 0, 0)),
            pl.BlockSpec((8, HD), lambda s, p: (0, 0)),
        ],
        out_shape=[
            jax.ShapeDtypeStruct((seqs, rows, width), bf16),
            jax.ShapeDtypeStruct((seqs, RIM, width), f32),
            jax.ShapeDtypeStruct((seqs, RIM, width), bf16),
            jax.ShapeDtypeStruct((seqs, rows, heads), f32),
            jax.ShapeDtypeStruct((pairs, 3 * KCONV, wide), f32),
            jax.ShapeDtypeStruct((8, HD), f32),
        ],
        scratch_shapes=[
            pltpu.VMEM((extended, wide), f32),
            pltpu.VMEM((extended, wide), f32),
            pltpu.VMEM((extended, wide), f32),
            pltpu.VMEM((rows + 2 * RIM, wide), f32),
            pltpu.VMEM((seqs * pairs, PAIR, HD, HD), bf16),
            pltpu.VMEM((seqs * pairs, PAIR, HD, HD), bf16),
            pltpu.SemaphoreType.DMA((seqs * pairs,)),
            pltpu.SemaphoreType.DMA((seqs * pairs,)),
        ],
        compiler_params=pltpu.CompilerParams(
            collective_id=1, has_side_effects=True, vmem_limit_bytes=VMEM_LIMIT,
            dimension_semantics=("arbitrary", "arbitrary"),
        ),
        name="mixer_back",
    )(
        projected, projected, projected, strength, filters, gain,
        back_normed, mix, carry, inverse, kw, state,
    )


OUTER = 4
SUBS = 2


def ring_walk(place, n):
    inner = n // OUTER
    if inner == 1:
        return place
    late = jnp.maximum(place - OUTER, 0)
    turn, along = lax.div(late, inner - 1), lax.rem(late, inner - 1)
    odd = lax.rem(turn, 2)
    back = (OUTER - 1 - turn) * inner + (1 - odd) * (along + 1) + odd * (inner - 1 - along)
    return jnp.where(place < OUTER, place * inner, back)


def ring_place(index, n):
    inner = n // OUTER
    if inner == 1:
        return index
    out, along = lax.div(index, inner), lax.rem(index, inner)
    odd = lax.rem(OUTER - 1 - out, 2)
    turn = (1 - odd) * (along - 1) + odd * (inner - 1 - along)
    return jnp.where(along == 0, out, OUTER + (OUTER - 1 - out) * (inner - 1) + turn)


def remote(source, target, send, recv, **device):
    return pltpu.make_async_remote_copy(
        src_ref=source, dst_ref=target, send_sem=send, recv_sem=recv,
        device_id=device, device_id_type=MESH,
    )


def swap_pair(index):
    return index + 1 - 2 * lax.rem(index, 2)


def swap_half(index, count):
    return lax.rem(index + count // 2, count)


def opening_kernel(
    n, tensor,
    q_ref, k_ref, v_ref, small_ref, tokens_ref, cot_ref,
    qkv_ref, small_out, ext_ref, cot_out,
    zero_ref, local_sem, ring_send, ring_recv, side_send, side_recv, rim_send, rim_recv,
):
    me, t = lax.axis_index("dp"), lax.axis_index("tensor")
    place = ring_place(me, n)
    near = (ring_walk(lax.rem(place + 1, n), n), ring_walk(lax.rem(place + n - 1, n), n))
    core, cross = swap_pair(t), swap_half(t, tensor)
    rows, local = q_ref.shape
    own_len = tokens_ref.shape[1]
    slab = rows // (2 * SUBS)

    barrier = pltpu.get_barrier_semaphore()
    for device in ({"dp": near[0]}, {"dp": near[1]}, {"tensor": core}, {"tensor": cross}):
        pl.semaphore_signal(barrier, inc=1, device_id=device, device_id_type=MESH)

    @pl.when(me > 0)
    def _():
        pl.semaphore_signal(
            barrier, inc=1, device_id={"dp": lax.rem(me + n - 1, n), "tensor": tensor - 1},
            device_id_type=MESH,
        )

    def chunk(ref, at, offset):
        return ref.at[:, pl.ds(pl.multiple_of(offset + at * own_len, 8), own_len), :]

    mine = [
        pltpu.make_async_copy(ref, qkv_ref.at[me, :, pl.ds(c * local, local)], local_sem.at[c])
        for c, ref in enumerate((q_ref, k_ref, v_ref))
    ] + [
        pltpu.make_async_copy(small_ref, small_out.at[me], local_sem.at[3]),
        pltpu.make_async_copy(tokens_ref, chunk(ext_ref, t, RIM), local_sem.at[4]),
        pltpu.make_async_copy(cot_ref, chunk(cot_out, t, 0), local_sem.at[5]),
    ]
    for copy in mine:
        copy.start()

    @pl.when(me == 0)
    def _():
        zero_ref[...] = jnp.zeros_like(zero_ref)
        blank = pltpu.make_async_copy(zero_ref, ext_ref.at[:, pl.ds(0, RIM), :], local_sem.at[6])
        blank.start()
        blank.wait()

    sends_rim = (me < n - 1) & (t == tensor - 1)

    @pl.when(sends_rim)
    def _():
        pl.semaphore_wait(barrier, 4 + tensor)

    @pl.when(jnp.logical_not(sends_rim))
    def _():
        pl.semaphore_wait(barrier, 4)

    def to_rim(peer):
        return remote(
            tokens_ref.at[:, pl.ds(own_len - RIM, RIM), :], ext_ref.at[:, pl.ds(0, RIM), :],
            rim_send.at[peer], rim_recv, dp=lax.rem(me + 1, n), tensor=peer,
        )

    sides = []
    for i, (own, full, offset) in enumerate(((tokens_ref, ext_ref, RIM), (cot_ref, cot_out, 0))):
        to_core = remote(own, chunk(full, t, offset), side_send.at[i, 0], side_recv.at[i, 0], tensor=core)
        to_cross = remote(own, chunk(full, t, offset), side_send.at[i, 1], side_recv.at[i, 1], tensor=cross)
        onward = remote(
            chunk(full, cross, offset), chunk(full, cross, offset),
            side_send.at[i, 2], side_recv.at[i, 2], tensor=core,
        )
        sides.append((to_core, to_cross, onward))
        to_core.start()
        to_cross.start()

    for copy in mine:
        copy.wait()

    @pl.when(sends_rim)
    def _():
        for peer in range(tensor):
            to_rim(peer).start()

    def ring(hop, lane):
        if lane == 2 * SUBS:
            owner = ring_walk(lax.rem(place + n - hop + 1, n), n)
            return remote(
                small_out.at[owner], small_out.at[owner],
                ring_send.at[hop, lane], ring_recv.at[hop, lane], dp=near[0],
            )
        way = lane % 2
        owner = ring_walk(lax.rem(place + n + (2 * way - 1) * (hop - 1), n), n)
        piece = qkv_ref.at[owner, pl.ds(lane * slab, slab), :]
        return remote(piece, piece, ring_send.at[hop, lane], ring_recv.at[hop, lane], dp=near[way])

    lanes = range(2 * SUBS + 1)

    def advance(hop, carry):
        for lane in lanes:
            @pl.when(hop > 1)
            def _():
                ring(hop - 1, lane).wait_recv()

            ring(hop, lane).start()
        for i, at in ((0, n // 2), (1, n - 1)):
            @pl.when(hop == at)
            def _():
                sides[i][1].wait_recv()
                sides[i][2].start()

        return carry

    lax.fori_loop(1, n, advance, 0)
    for lane in lanes:
        ring(n - 1, lane).wait_recv()

    def drain(hop, carry):
        for lane in lanes:
            ring(hop, lane).wait_send()
        return carry

    lax.fori_loop(1, n, drain, 0)
    for to_core, to_cross, onward in sides:
        to_core.wait()
        to_cross.wait_send()
        onward.wait()

    @pl.when(sends_rim)
    def _():
        for peer in range(tensor):
            to_rim(peer).wait_send()

    @pl.when(me > 0)
    def _():
        to_rim(0).wait_recv()


def opening(query_weight, key_weight, value_weight, small, tokens, cotangent):
    n, tensor = lax.axis_size("dp"), lax.axis_size("tensor")
    rows, local = query_weight.shape
    seqs, own_len, width = tokens.shape
    vmem, anywhere = pl.BlockSpec(memory_space=pltpu.VMEM), pl.BlockSpec(memory_space=pl.ANY)
    lanes = 2 * SUBS + 1
    return pl.pallas_call(
        functools.partial(opening_kernel, n, tensor),
        in_specs=[vmem] * 6,
        out_specs=[anywhere] * 4,
        out_shape=[
            jax.ShapeDtypeStruct((n, rows, 3 * local), bf16),
            jax.ShapeDtypeStruct((n,) + small.shape, bf16),
            jax.ShapeDtypeStruct((seqs, RIM + tensor * own_len, width), bf16),
            jax.ShapeDtypeStruct((seqs, tensor * own_len, width), bf16),
        ],
        scratch_shapes=[
            pltpu.VMEM((seqs, RIM, width), bf16),
            pltpu.SemaphoreType.DMA((7,)),
            pltpu.SemaphoreType.DMA((n, lanes)),
            pltpu.SemaphoreType.DMA((n, lanes)),
            pltpu.SemaphoreType.DMA((2, 3)),
            pltpu.SemaphoreType.DMA((2, 3)),
            pltpu.SemaphoreType.DMA((tensor,)),
            pltpu.SemaphoreType.DMA,
        ],
        compiler_params=pltpu.CompilerParams(
            collective_id=2, has_side_effects=True, vmem_limit_bytes=VMEM_LIMIT
        ),
        name="opening",
    )(query_weight, key_weight, value_weight, small, tokens, cotangent)


def fold_kernel(
    n_seqs, tensor, backward,
    part_ref, own_ref, gain_ref, hidden_ref,
    rows_ref, keep_ref, sum_ref,
    near_ref, far_ref, send_ref, own_sum_ref, a_send, a_recv, x_send, x_recv, g_send, g_recv,
):
    t = lax.axis_index("tensor")
    core, cross = swap_pair(t), swap_half(t, tensor)
    both = swap_half(core, tensor)
    own_len = own_ref.shape[1]

    barrier = pltpu.get_barrier_semaphore()
    for device in (core, cross):
        pl.semaphore_signal(barrier, inc=1, device_id={"tensor": device}, device_id_type=MESH)
    pl.semaphore_wait(barrier, 2)

    def span(at):
        return pl.ds(pl.multiple_of(at * own_len, own_len), own_len)

    def to_core(s, i):
        return remote(
            part_ref.at[s, span((core, both)[i]), :], near_ref.at[s, i],
            a_send.at[s, i], a_recv.at[s, i], tensor=core,
        )

    def to_cross(s):
        return remote(send_ref.at[s], far_ref.at[s], x_send.at[s], x_recv.at[s], tensor=cross)

    def gather(s, i):
        if i == 2:
            piece, peer = rows_ref.at[s, span(cross), :], core
        else:
            piece, peer = rows_ref.at[s, span(t), :], (cross, core)[i]
        return remote(piece, piece, g_send.at[s, i], g_recv.at[s, i], tensor=peer)

    for s in range(n_seqs):
        for i in (1, 0):
            to_core(s, i).start()

    def first(s, carry):
        to_core(s, 1).wait_recv()
        send_ref[s] = (
            part_ref[s, span(cross), :].astype(f32) + near_ref[s, 1].astype(f32)
        ).astype(bf16)
        to_cross(s).start()
        to_core(s, 0).wait_recv()
        own_sum_ref[s] = part_ref[s, span(t), :].astype(f32) + near_ref[s, 0].astype(f32)
        return carry

    lax.fori_loop(0, n_seqs, first, 0)
    sum_ref[...] = jnp.zeros_like(sum_ref)

    def second(s, carry):
        to_cross(s).wait_recv()
        total = own_sum_ref[s] + far_ref[s].astype(f32)
        gain = gain_ref[...]
        own = own_ref[s].astype(f32)
        if backward:
            hidden = hidden_ref[s]
            scale = lax.rsqrt(jnp.mean(hidden * hidden, axis=-1, keepdims=True) + epsilon)
            unit = hidden * scale
            sum_ref[...] += jnp.sum(total * unit, axis=0, keepdims=True)
            scaled = total * gain
            kept = own + scale * (scaled - unit * jnp.mean(scaled * unit, axis=-1, keepdims=True))
            keep_ref[s] = kept
            rows_ref[s, span(t), :] = kept.astype(bf16)
        else:
            kept = own + total
            keep_ref[s] = kept
            scale = lax.rsqrt(jnp.mean(kept * kept, axis=-1, keepdims=True) + epsilon)
            rows_ref[s, span(t), :] = (kept * scale * gain).astype(bf16)
        gather(s, 0).start()
        gather(s, 1).start()
        return carry

    lax.fori_loop(0, n_seqs, second, 0)

    def third(s, carry):
        gather(s, 0).wait_recv()
        gather(s, 2).start()
        return carry

    lax.fori_loop(0, n_seqs, third, 0)

    def last(s, carry):
        gather(s, 1).wait_recv()
        gather(s, 2).wait_recv()
        for i in range(2):
            to_core(s, i).wait_send()
        to_cross(s).wait_send()
        for i in range(3):
            gather(s, i).wait_send()
        return carry

    lax.fori_loop(0, n_seqs, last, 0)


def fold(part, own, gain, hidden=None):
    tensor = lax.axis_size("tensor")
    seqs, own_len, width = own.shape
    backward = hidden is not None
    vmem = pl.BlockSpec(memory_space=pltpu.VMEM)
    if hidden is None:
        hidden = jnp.zeros((8, 128), f32)
    return pl.pallas_call(
        functools.partial(fold_kernel, seqs, tensor, backward),
        in_specs=[vmem] * 4,
        out_specs=[vmem] * 3,
        out_shape=[
            jax.ShapeDtypeStruct((seqs, tensor * own_len, width), bf16),
            jax.ShapeDtypeStruct((seqs, own_len, width), f32),
            jax.ShapeDtypeStruct((1, width), f32),
        ],
        scratch_shapes=[
            pltpu.VMEM((seqs, 2, own_len, width), bf16),
            pltpu.VMEM((seqs, own_len, width), bf16),
            pltpu.VMEM((seqs, own_len, width), bf16),
            pltpu.VMEM((seqs, own_len, width), f32),
            pltpu.SemaphoreType.DMA((seqs, 2)),
            pltpu.SemaphoreType.DMA((seqs, 2)),
            pltpu.SemaphoreType.DMA((seqs,)),
            pltpu.SemaphoreType.DMA((seqs,)),
            pltpu.SemaphoreType.DMA((seqs, 3)),
            pltpu.SemaphoreType.DMA((seqs, 3)),
        ],
        compiler_params=pltpu.CompilerParams(
            collective_id=4 if backward else 3, has_side_effects=True, vmem_limit_bytes=VMEM_LIMIT
        ),
        name="fold_back" if backward else "fold",
    )(part, own, gain, hidden)


def closing_kernel(
    n, n_seqs, tensor,
    part_ref, own_ref, tokens_ref, gain_ref, grad_ref,
    d_ref, sum_ref,
    near_ref, far_ref, send_ref, own_sum_ref, in_ref, out_ref,
    a_send, a_recv, x_send, x_recv, ring_send, ring_recv,
):
    me, t = lax.axis_index("dp"), lax.axis_index("tensor")
    place = ring_place(me, n)
    near = (ring_walk(lax.rem(place + 1, n), n), ring_walk(lax.rem(place + n - 1, n), n))
    core, cross = swap_pair(t), swap_half(t, tensor)
    both = swap_half(core, tensor)
    own_len = tokens_ref.shape[1]
    slab = grad_ref.shape[1] // (2 * SUBS)

    barrier = pltpu.get_barrier_semaphore()
    for device in ({"dp": near[0]}, {"dp": near[1]}, {"tensor": core}, {"tensor": cross}):
        pl.semaphore_signal(barrier, inc=1, device_id=device, device_id_type=MESH)
    pl.semaphore_wait(barrier, 4)

    def span(at):
        return pl.ds(pl.multiple_of(at * own_len, own_len), own_len)

    def to_core(s, i):
        return remote(
            part_ref.at[s, span((core, both)[i]), :], near_ref.at[s, i],
            a_send.at[s, i], a_recv.at[s, i], tensor=core,
        )

    def to_cross(s):
        return remote(send_ref.at[s], far_ref.at[s], x_send.at[s], x_recv.at[s], tensor=cross)

    def owner(hop, way):
        return ring_walk(lax.rem(place + n + (2 * way - 1) * hop, n), n)

    def strip(lane):
        return pl.ds(lane * slab, slab)

    def opened(lane):
        way = lane % 2
        return remote(
            grad_ref.at[owner(1, way), strip(lane), :], in_ref.at[1, strip(lane), :],
            ring_send.at[1, lane], ring_recv.at[1, lane], dp=near[way],
        )

    def ring(hop, lane):
        return remote(
            out_ref.at[hop, strip(lane), :], in_ref.at[hop, strip(lane), :],
            ring_send.at[hop, lane], ring_recv.at[hop, lane], dp=near[lane % 2],
        )

    lanes = range(2 * SUBS)
    for lane in lanes:
        opened(lane).start()
    for s in range(n_seqs):
        for i in (1, 0):
            to_core(s, i).start()

    def first(s, carry):
        to_core(s, 1).wait_recv()
        send_ref[s] = (
            part_ref[s, span(cross), :].astype(f32) + near_ref[s, 1].astype(f32)
        ).astype(bf16)
        to_cross(s).start()
        to_core(s, 0).wait_recv()
        own_sum_ref[s] = part_ref[s, span(t), :].astype(f32) + near_ref[s, 0].astype(f32)
        return carry

    lax.fori_loop(0, n_seqs, first, 0)

    def finish(s):
        to_cross(s).wait_recv()
        total = own_sum_ref[s] + far_ref[s].astype(f32)
        tokens = tokens_ref[s].astype(f32)
        scale = lax.rsqrt(jnp.mean(tokens * tokens, axis=-1, keepdims=True) + epsilon)
        unit = tokens * scale
        scaled = total * gain_ref[...]
        d_ref[s] = (
            own_ref[s] + scale * (scaled - unit * jnp.mean(scaled * unit, axis=-1, keepdims=True))
        ).astype(bf16)

    def advance(hop, carry):
        for lane in lanes:
            ring(hop - 1, lane).wait_recv()
            out_ref[hop, strip(lane), :] = (
                in_ref[hop - 1, strip(lane), :].astype(f32)
                + grad_ref[owner(hop, lane % 2), strip(lane), :].astype(f32)
            ).astype(bf16)
            ring(hop, lane).start()

        @pl.when(hop == n // 2)
        def _():
            for s in range(n_seqs):
                finish(s)

        return carry

    lax.fori_loop(2, n, advance, 0)
    for lane in lanes:
        ring(n - 1, lane).wait_recv()
        sum_ref[strip(lane), :] = in_ref[n - 1, strip(lane), :].astype(f32) + grad_ref[
            me, strip(lane), :
        ].astype(f32)
        opened(lane).wait_send()

    def drain(hop, carry):
        for lane in lanes:
            ring(hop, lane).wait_send()
        return carry

    lax.fori_loop(2, n, drain, 0)

    def last(s, carry):
        for i in range(2):
            to_core(s, i).wait_send()
        to_cross(s).wait_send()
        return carry

    lax.fori_loop(0, n_seqs, last, 0)


def closing(part, own, tokens, gain, grads):
    n, tensor = lax.axis_size("dp"), lax.axis_size("tensor")
    seqs, own_len, width = tokens.shape
    _, rows, columns = grads.shape
    vmem = pl.BlockSpec(memory_space=pltpu.VMEM)
    lanes = 2 * SUBS
    return pl.pallas_call(
        functools.partial(closing_kernel, n, seqs, tensor),
        in_specs=[vmem] * 5,
        out_specs=[vmem] * 2,
        out_shape=[
            jax.ShapeDtypeStruct((seqs, own_len, width), bf16),
            jax.ShapeDtypeStruct((rows, columns), f32),
        ],
        scratch_shapes=[
            pltpu.VMEM((seqs, 2, own_len, width), bf16),
            pltpu.VMEM((seqs, own_len, width), bf16),
            pltpu.VMEM((seqs, own_len, width), bf16),
            pltpu.VMEM((seqs, own_len, width), f32),
            pltpu.VMEM((n, rows, columns), bf16),
            pltpu.VMEM((n, rows, columns), bf16),
            pltpu.SemaphoreType.DMA((seqs, 2)),
            pltpu.SemaphoreType.DMA((seqs, 2)),
            pltpu.SemaphoreType.DMA((seqs,)),
            pltpu.SemaphoreType.DMA((seqs,)),
            pltpu.SemaphoreType.DMA((n, lanes)),
            pltpu.SemaphoreType.DMA((n, lanes)),
        ],
        compiler_params=pltpu.CompilerParams(
            collective_id=5, has_side_effects=True, vmem_limit_bytes=VMEM_LIMIT
        ),
        name="closing",
    )(part, own, tokens, gain, grads)


def from_behind(block, axis, distance):
    devices = range(lax.axis_size(axis))
    route = [(i - distance, i) for i in devices if i - distance in devices]
    return lax.ppermute(block, axis, route)


def rms_unit(values):
    scale = lax.rsqrt(jnp.mean(values * values, axis=-1, keepdims=True) + epsilon)
    return values * scale, scale


def rms_back(back, unit, scale, gain):
    scaled = back * gain
    return scale * (scaled - unit * jnp.mean(scaled * unit, axis=-1, keepdims=True))


def matmul(spec, left, right):
    return jnp.einsum(spec, left, right, preferred_element_type=f32)


def swap(block, axis, half):
    count = lax.axis_size(axis)
    route = [(i, (i + count // 2) % count if half else i ^ 1) for i in range(count)]
    return lax.ppermute(block, axis, route)


def tensor_scatter(part):
    tensor, t = lax.axis_size("tensor"), lax.axis_index("tensor")
    seqs, rows, width = part.shape
    chunks = part.reshape(seqs, tensor, rows // tensor, width)

    def chunk(at):
        return lax.dynamic_index_in_dim(chunks, at, 1, keepdims=False)

    core, cross = swap_pair(t), swap_half(t, tensor)
    both = swap_half(core, tensor)
    near_own, near_cross = swap(chunk(core), "tensor", False), swap(chunk(both), "tensor", False)
    far = swap((chunk(cross).astype(f32) + near_cross.astype(f32)).astype(bf16), "tensor", True)
    return chunk(t).astype(f32) + near_own.astype(f32) + far.astype(f32)


def tensor_sum(value):
    value = value + swap(value, "tensor", False)
    return value + swap(value, "tensor", True)


def direct_scatter(grads):
    n, me = lax.axis_size("dp"), lax.axis_index("dp")
    total = lax.dynamic_index_in_dim(grads, me, 0, keepdims=False).astype(f32)
    for step in range(1, n):
        block = lax.dynamic_index_in_dim(grads, lax.rem(me + step, n), 0, keepdims=False)
        total = total + lax.ppermute(block, "dp", [(i, (i + step) % n) for i in range(n)]).astype(f32)
    return total


def shards(
    tokens,
    cotangent,
    query_weight,
    key_weight,
    value_weight,
    beta_weight,
    conv_filter,
    norm_gain,
    head_gain,
    out_weight,
    gate_weight,
    up_weight,
    down_weight,
):
    n = lax.axis_size("dp")
    tensor = lax.axis_size("tensor")
    seqs, own_len, width = tokens.shape
    local = query_weight.shape[1]
    heads = local // HD
    hidden = gate_weight.shape[1]

    packed = jnp.concatenate(
        [conv_filter.reshape(-1), norm_gain.reshape(-1), head_gain, beta_weight.reshape(-1)]
    )
    block = -(-packed.size // 2048) * 2048
    small = jnp.pad(packed, (0, block - packed.size)).reshape(-1, 128)
    full_qkv, full_small, extended, rows_cotangent = opening(
        query_weight, key_weight, value_weight, small, tokens, cotangent
    )
    full_qkv = full_qkv.reshape(width, 3 * local)
    full_small = full_small.reshape(n, block)
    full_out = lax.all_gather(out_weight.T, "dp", axis=0, tiled=True)
    full_gate = lax.all_gather(gate_weight, "dp", axis=0, tiled=True)
    full_up = lax.all_gather(up_weight, "dp", axis=0, tiled=True)
    full_down = lax.all_gather(down_weight.T, "dp", axis=0, tiled=True)
    sizes = [conv_filter.size, norm_gain.size, head_gain.size, beta_weight.size]
    ends = [sum(sizes[: i + 1]) for i in range(4)]
    filters = (
        full_small[:, : ends[0]]
        .reshape(n, 3 * KCONV, heads, HD // n)
        .transpose(1, 2, 0, 3)
        .reshape(3 * KCONV, local)
        .astype(f32)
    )
    gains = (
        full_small[:, ends[0] : ends[1]].reshape(n, 2, width // n).transpose(1, 0, 2).reshape(2, width)
    ).astype(f32)
    head_row = full_small[:, ends[1] : ends[2]].reshape(1, HD).astype(f32)
    full_beta = full_small[:, ends[2] : ends[3]].reshape(width, heads)

    unit_ext, _ = rms_unit(extended.astype(f32))
    normed_ext = (unit_ext * gains[0]).astype(bf16)
    normed_first = normed_ext[:, RIM:]
    projected = matmul("std,dm->stm", normed_ext, full_qkv).astype(bf16)
    strength = jax.nn.sigmoid(matmul("std,dh->sth", normed_first, full_beta))
    normed_mix, mix, carry, inverse, kw, state = mixer(projected, strength, filters, head_row)

    branch_part = matmul("stk,dk->std", normed_mix, full_out).astype(bf16)
    normed_second, hidden_state, _ = fold(branch_part, tokens, gains[1:2])
    gate_pre = matmul("std,df->stf", normed_second, full_gate)
    up_pre = matmul("std,df->stf", normed_second, full_up)
    gate_sigmoid = jax.nn.sigmoid(gate_pre)
    ffn_hidden = (gate_pre * gate_sigmoid * up_pre).astype(bf16)

    back_hidden = matmul("std,df->stf", rows_cotangent, full_down)
    back_gate = (
        back_hidden * up_pre * gate_sigmoid * (1.0 + gate_pre * (1.0 - gate_sigmoid))
    ).astype(bf16)
    back_up = (back_hidden * gate_pre * gate_sigmoid).astype(bf16)
    back_second = matmul("stf,df->std", back_gate, full_gate) + matmul("stf,df->std", back_up, full_up)
    rows_back, back_state, gain_second = fold(
        back_second.astype(bf16), cotangent, gains[1:2], hidden_state
    )
    grad_down = matmul("std,stf->df", rows_cotangent, ffn_hidden)
    grad_gate = matmul("std,stf->df", normed_second, back_gate)
    grad_up = matmul("std,stf->df", normed_second, back_up)
    ffn_part = matmul("stf,df->std", ffn_hidden, full_down).astype(bf16)
    layer_out = (hidden_state + tensor_scatter(ffn_part)).astype(bf16)
    grad_out = matmul("std,stk->dk", rows_back, normed_mix)
    back_normed = matmul("std,dk->stk", rows_back, full_out)
    back_proj, last, rim, back_logit, conv_part, head_part = mixer_back(
        projected, strength, filters, head_row, back_normed, mix, carry, inverse, kw, state
    )
    rim = from_behind(rim, "dp", -1).astype(f32)
    back_proj = lax.dynamic_update_slice_in_dim(
        back_proj, (last + rim).astype(bf16), back_proj.shape[1] - RIM, 1
    )
    back_logit = back_logit.astype(bf16)
    grad_qkv = matmul("std,stm->dm", normed_first, back_proj)
    grad_beta = matmul("std,sth->dh", normed_first, back_logit)
    back_first = matmul("stm,dm->std", back_proj, full_qkv) + matmul(
        "sth,dh->std", back_logit, full_beta
    )
    gain_first = jnp.sum(back_first * unit_ext[:, RIM:], axis=(0, 1))
    grads = jnp.concatenate([grad_qkv.astype(bf16), grad_out.astype(bf16)], axis=1)
    d_tokens, grad_main = closing(
        back_first.astype(bf16), back_state, tokens, gains[0:1], grads.reshape(n, width // n, -1)
    )

    grad_conv = conv_part.transpose(1, 0, 2).reshape(3 * KCONV, local)
    gain_grads = jnp.stack([gain_first, gain_second[0]])
    small_grads = jnp.concatenate(
        [
            grad_conv.reshape(3 * KCONV, heads, n, HD // n).transpose(2, 0, 1, 3).reshape(n, -1),
            gain_grads.reshape(2, n, width // n).transpose(1, 0, 2).reshape(n, -1),
            head_part[0].reshape(n, HD // n),
            grad_beta.reshape(n, -1),
        ],
        axis=1,
    )
    small_grads = direct_scatter(small_grads.astype(bf16))
    shared = tensor_sum(small_grads[ends[0] : ends[2]])

    def scatter(grad):
        return lax.psum_scatter(grad.astype(bf16), "dp", scatter_dimension=0, tiled=True).astype(f32)

    grad_down = scatter(grad_down).T
    grad_gate = scatter(grad_gate)
    grad_up = scatter(grad_up)
    return (
        layer_out,
        d_tokens,
        grad_main[:, :local],
        grad_main[:, local : 2 * local],
        grad_main[:, 2 * local : 3 * local],
        small_grads[ends[2] :].reshape(beta_weight.shape),
        small_grads[: ends[0]].reshape(conv_filter.shape),
        shared[: ends[1] - ends[0]].reshape(norm_gain.shape),
        shared[ends[1] - ends[0] :],
        grad_main[:, 3 * local :].T,
        grad_gate,
        grad_up,
        grad_down,
    )


def solution(mesh):
    both = P(None, ("dp", "tensor"), None)
    rows, cols = P("dp", "tensor"), P("tensor", "dp")
    conv, gain, head = P(None, "tensor", "dp"), P(None, "dp"), P("dp")
    return jax.shard_map(
        shards,
        mesh=mesh,
        in_specs=(both, both, rows, rows, rows, rows, conv, gain, head, cols, rows, rows, cols),
        out_specs=(both, both, rows, rows, rows, rows, conv, gain, head, cols, rows, rows, cols),
        check_vma=False,
    )
```

```python
import functools

import jax
import jax.numpy as jnp
from jax import lax
from jax.experimental import pallas as pl
from jax.experimental.pallas import tpu as pltpu
from jax.sharding import PartitionSpec as P

HD = 128
KCONV = 4
RIM = 8
PAIR = 2
OUTER = 4
SUBS = 2

epsilon = 1e-06
f32 = jnp.float32
bf16 = jnp.bfloat16
MESH = pl.DeviceIdType.MESH
VMEM_LIMIT = 60 * 1024 * 1024


def ring_walk(place, n):
    inner = n // OUTER
    if inner == 1:
        return place
    late = jnp.maximum(place - OUTER, 0)
    turn, along = lax.div(late, inner - 1), lax.rem(late, inner - 1)
    odd = lax.rem(turn, 2)
    back = (OUTER - 1 - turn) * inner + (1 - odd) * (along + 1) + odd * (inner - 1 - along)
    return jnp.where(place < OUTER, place * inner, back)


def ring_place(index, n):
    inner = n // OUTER
    if inner == 1:
        return index
    out, along = lax.div(index, inner), lax.rem(index, inner)
    odd = lax.rem(OUTER - 1 - out, 2)
    turn = (1 - odd) * (along - 1) + odd * (inner - 1 - along)
    return jnp.where(along == 0, out, OUTER + (OUTER - 1 - out) * (inner - 1) + turn)


def remote(source, target, send, recv, **device):
    return pltpu.make_async_remote_copy(
        src_ref=source, dst_ref=target, send_sem=send, recv_sem=recv,
        device_id=device, device_id_type=MESH,
    )


def swap_pair(index):
    return index + 1 - 2 * lax.rem(index, 2)


def swap_half(index, count):
    return lax.rem(index + count // 2, count)


class Ring:
    def __init__(self, n, rows, lanes, send, recv):
        self.n, self.lanes, self.send, self.recv = n, range(lanes), send, recv
        self.me = lax.axis_index("dp")
        self.place = ring_place(self.me, n)
        self.near = (
            ring_walk(lax.rem(self.place + 1, n), n),
            ring_walk(lax.rem(self.place + n - 1, n), n),
        )
        self.slab = rows // lanes

    def greet(self, barrier):
        for device in self.near:
            pl.semaphore_signal(barrier, inc=1, device_id={"dp": device}, device_id_type=MESH)

    def strip(self, lane):
        return pl.ds(lane * self.slab, self.slab)

    def owner(self, hop, lane):
        return ring_walk(lax.rem(self.place + self.n + (2 * (lane % 2) - 1) * hop, self.n), self.n)

    def copy(self, source, target, hop, lane):
        return remote(
            source, target, self.send.at[hop, lane], self.recv.at[hop, lane], dp=self.near[lane % 2]
        )


class RingGather(Ring):
    def __init__(self, n, rows, full, send, recv, own=None, local=None, lanes=2 * SUBS):
        super().__init__(n, rows, lanes, send, recv)
        self.own, self.full, self.local = own, full, local

    def first(self, lane):
        strip = self.strip(lane)
        return self.copy(self.own.at[strip, :], self.full.at[self.me, strip, :], 1, lane)

    def later(self, hop, lane):
        piece = self.full.at[self.owner(hop - 1, lane), self.strip(lane), :]
        return self.copy(piece, piece, hop, lane)

    def stay(self):
        return pltpu.make_async_copy(self.own, self.full.at[self.me], self.local)

    def start(self):
        self.stay().start()
        for lane in self.lanes:
            self.first(lane).start()

    def resume(self, hop):
        for lane in self.lanes:
            self.later(hop, lane).start()

    def advance(self, hop):
        for lane in self.lanes:
            self.later(hop - 1, lane).wait_recv()
            self.later(hop, lane).start()

    def settle(self, begin, end):
        for lane in self.lanes:
            self.later(end, lane).wait_recv()
            if begin == 1:
                self.first(lane).wait_send()

        def drain(hop, carry):
            for lane in self.lanes:
                self.later(hop, lane).wait_send()
            return carry

        lax.fori_loop(max(begin, 2), end + 1, drain, 0)
        if begin == 1:
            self.stay().wait()


class RingScatter(Ring):
    def __init__(self, n, rows, part, inward, total, send, recv, lanes=2 * SUBS):
        super().__init__(n, rows, lanes, send, recv)
        self.part, self.inward, self.total = part, inward, total
        self.half = rows // 2

    def strip(self, lane):
        return pl.ds((lane % 2) * self.half + (lane // 2) * self.slab, self.slab)

    def sender(self, hop, lane):
        strip = self.strip(lane)
        return self.copy(self.inward.at[hop - 1, strip, :], self.inward.at[hop, strip, :], hop, lane)

    def ways(self, value_of):
        for way in range(2):
            value = value_of(way)
            for lane in self.lanes[way::2]:
                at = (lane // 2) * self.slab
                yield lane, value[at : at + self.slab]

    def start(self):
        for lane, value in self.ways(lambda way: self.part(self.owner(1, way), way)):
            self.inward[0, self.strip(lane), :] = value.astype(bf16)
            self.sender(1, lane).start()

    def summed(self, hop, lane, value):
        self.sender(hop, lane).wait_recv()
        return self.inward[hop, self.strip(lane), :].astype(f32) + value

    def advance(self, hop):
        for lane, value in self.ways(lambda way: self.part(self.owner(hop, way), way)):
            self.inward[hop - 1, self.strip(lane), :] = self.summed(hop - 1, lane, value).astype(bf16)
            self.sender(hop, lane).start()

    def finish(self):
        for lane, value in self.ways(lambda way: self.part(self.me, way)):
            self.total[self.strip(lane), :] = self.summed(self.n - 1, lane, value)

        def drain(hop, carry):
            for lane in self.lanes:
                self.sender(hop, lane).wait_send()
            return carry

        lax.fori_loop(1, self.n, drain, 0)


def held_part(ref):
    half = ref.shape[1] // 2
    return lambda owner, way: ref[owner, way * half : (way + 1) * half, :].astype(f32)


def grad_part(rows, left_ref, right_ref, spare_ref=None):
    half = rows // 2

    def part(owner, way):
        at = owner * rows + way * half
        if half % 128 == 0:
            return dot(left_ref[:, pl.ds(pl.multiple_of(at, half), half)], right_ref[...], 0, 0)
        block = lax.div(at, 128) * 128
        spare_ref[...] = dot(left_ref[:, pl.ds(pl.multiple_of(block, 128), 128)], right_ref[...], 0, 0)
        return spare_ref[pl.ds(pl.multiple_of(at - block, half), half), :]

    return part


def spare(rows, columns):
    return pltpu.VMEM((8, 128) if (rows // 2) % 128 == 0 else (128, columns), f32)


def ring_semaphores(n, lanes=2 * SUBS):
    return [pltpu.SemaphoreType.DMA((n, lanes)), pltpu.SemaphoreType.DMA((n, lanes))]


def halves(value):
    high = value.astype(bf16)
    return (high, (value - high.astype(f32)).astype(bf16))


def dot(left, right, left_dim=1, right_dim=0):
    return lax.dot_general(
        left, right, (((left_dim,), (right_dim,)), ((), ())), preferred_element_type=f32
    )


def beside(*parts):
    return jnp.concatenate(parts, axis=1)


def full_product(left, right, left_dim=1, right_dim=0):
    return (
        dot(left[0], right[0], left_dim, right_dim)
        + dot(left[1], right[0], left_dim, right_dim)
        + dot(left[0], right[1], left_dim, right_dim)
    )


def narrow_product(left, right, left_dim=1):
    both = dot(left[0], beside(*right), left_dim, 0)
    width = right[0].shape[1]
    return both[:, :width] + both[:, width:] + dot(left[1], right[0], left_dim, 0)


def short_product(left, right):
    return dot(beside(*left), jnp.concatenate([right, right], axis=0))


def short_product_t(left, right):
    return dot(beside(*left), beside(right, right), 1, 1)


def square_product(left, right):
    lower = beside(right[0], jnp.zeros_like(right[0]))
    both = dot(beside(*left), jnp.concatenate([beside(*right), lower], axis=0))
    return both[:, :HD] + both[:, HD:]


def conv_act(x_ref, x_in, filt_ref, column, rows):
    x_ref[...] = x_in.astype(f32)
    running = None
    for tap in range(KCONV):
        term = filt_ref[pl.ds(column * KCONV + tap, 1), :] * x_ref[pl.ds(RIM - KCONV + 1 + tap, rows), :]
        running = term if running is None else running + term
    gate = jax.nn.sigmoid(running)
    return running, gate


def unit_scale(act):
    return lax.rsqrt(jnp.sum(act * act, axis=-1, keepdims=True) + epsilon)


def masks(rows):
    at_row = lax.broadcasted_iota(jnp.int32, (rows, rows), 0)
    at_col = lax.broadcasted_iota(jnp.int32, (rows, rows), 1)
    return at_row, at_col


def chain_lag(me, limit):
    return jnp.minimum(lax.div(3 * me + 4, 5), limit)


def mixer_kernel(
    n, rows, steps, pairs, limit,
    pq_ref, pk_ref, pv_ref, strength_ref, filt_ref, gain_ref, own_ref,
    normed_ref, mix_ref, carry_ref, inv_ref, kw_ref, state_ref, full_ref,
    x_ref, low_ref, sol_ref, end_ref, recv_ref, send_ref,
    send_sem, recv_sem, ring_send, ring_recv, local_sem,
):
    me = lax.axis_index("dp")
    step = pl.program_id(0)
    lag = chain_lag(me, limit)
    ring = RingGather(n, own_ref.shape[0], full_ref, ring_send, ring_recv, own_ref, local_sem)

    def hop(at, h):
        return remote(
            send_ref.at[at, h], recv_ref.at[at, h], send_sem.at[at, h], recv_sem.at[at, h],
            dp=lax.rem(me + 1, n),
        )

    @pl.when(step == 0)
    def _():
        barrier = pltpu.get_barrier_semaphore()
        ring.greet(barrier)

        @pl.when(me > 0)
        def _():
            pl.semaphore_signal(
                barrier, inc=1, device_id={"dp": lax.rem(me + n - 1, n)}, device_id_type=MESH
            )

        @pl.when(me == 0)
        def _():
            recv_ref[...] = jnp.zeros_like(recv_ref)

        @pl.when(me < n - 1)
        def _():
            pl.semaphore_wait(barrier, 3)

        @pl.when(me == n - 1)
        def _():
            pl.semaphore_wait(barrier, 2)

        ring.start()

    each = -(-(n - 2) // (steps - 1))

    @pl.when(step > 0)
    def _():
        for i in range(each):
            at = (step - 1) * each + i + 2

            @pl.when(at < n)
            def _():
                ring.advance(at)

    @pl.when(step < steps)
    def _():
        pair = lax.rem(step, pairs)
        at_row, at_col = masks(HD)
        all_row, all_col = masks(rows)
        acts = []
        for column, ref in enumerate((pq_ref, pk_ref, pv_ref)):
            running, gate = conv_act(x_ref, ref[0], filt_ref, column, rows)
            acts.append(running * gate)
        strengths = strength_ref[0]
        lane = lax.broadcasted_iota(jnp.int32, strengths.shape, 1)
        heads = []
        for h in range(PAIR):
            cut = slice(h * HD, (h + 1) * HD)
            act_q, act_k = acts[0][:, cut], acts[1][:, cut]
            q = (act_q * unit_scale(act_q)).astype(bf16)
            k = (act_k * unit_scale(act_k)).astype(bf16)
            v = acts[2][:, cut].astype(bf16)
            beta = jnp.sum(jnp.where(lane == pair * PAIR + h, strengths, 0.0), axis=-1, keepdims=True)
            low = jnp.where(all_row > all_col, beta * dot(k, k, 1, 1), 0.0)
            low_ref[h] = low
            first = (at_row & 1 == 1) & (at_row - 1 == at_col)
            for b in range(2):
                block = low[b * HD : (b + 1) * HD, b * HD : (b + 1) * HD]
                sol_ref[h, b] = jnp.where(at_row == at_col, 1.0, 0.0) - jnp.where(first, block, 0.0)
            heads.append((q, k, v, beta))
        blocks = [(h, b) for h in range(PAIR) for b in range(2)]

        def refine(level, carry):
            band_row, band_col = at_row >> level, at_col >> level
            band = (band_row & 1 == 1) & (band_row - 1 == band_col)
            sols = [halves(sol_ref[h, b]) for h, b in blocks]
            mids = [
                halves(
                    square_product(
                        halves(
                            jnp.where(
                                band, low_ref[h, b * HD : (b + 1) * HD, b * HD : (b + 1) * HD], 0.0
                            )
                        ),
                        sol,
                    )
                )
                for (h, b), sol in zip(blocks, sols)
            ]
            for (h, b), sol, mid in zip(blocks, sols, mids):
                sol_ref[h, b] = sol_ref[h, b] - square_product(sol, mid)
            return carry

        lax.fori_loop(1, (HD - 1).bit_length(), refine, 0)

        wides = []
        for h in range(PAIR):
            q, k, v, beta = heads[h]
            top, low = halves(sol_ref[h, 0]), halves(sol_ref[h, 1])
            mid = halves(square_product(halves(low_ref[h, HD:, :HD]), top))
            corner = -square_product(low, mid)
            inv = jnp.concatenate(
                [
                    beside(sol_ref[h, 0], jnp.zeros((HD, HD), f32)),
                    beside(corner, sol_ref[h, 1]),
                ],
                axis=0,
            )
            inv_ref[h] = inv
            right = beside(beta * k.astype(f32), beta * v.astype(f32))
            wides.append(halves(full_product(halves(inv), halves(right))))
        for h in range(PAIR):
            q, k, v, beta = heads[h]
            scores = halves(jnp.where(all_row >= all_col, dot(q, k, 1, 1), 0.0))
            seen = full_product(scores, wides[h])
            carry_ref[step, h] = q.astype(f32) - seen[:, :HD]
            mix_ref[step, h] = seen[:, HD:]
            kwu = dot(k, wides[h][0], 0, 0) + dot(k, wides[h][1], 0, 0)
            kw_ref[step, h] = kwu[:, :HD]
            end_ref[step, h] = kwu[:, HD:]

    at = step - lag

    @pl.when((at >= 0) & (at < steps))
    def _():
        for h in range(PAIR):
            @pl.when(me > 0)
            def _():
                hop(at, h).wait_recv()

            state = recv_ref[at, h]
            out_state = end_ref[at, h] + state.astype(f32) - short_product(halves(kw_ref[at, h]), state)
            send_ref[at, h] = out_state.astype(bf16)

            @pl.when(me < n - 1)
            def _():
                hop(at, h).start()

        seq, pair = lax.div(at, pairs), lax.rem(at, pairs)
        for h in range(PAIR):
            state = recv_ref[at, h]
            state_ref[at, h] = state
            mix = mix_ref[at, h] + short_product(halves(carry_ref[at, h]), state)
            mix_ref[at, h] = mix
            scale = lax.rsqrt(jnp.mean(mix * mix, axis=-1, keepdims=True) + epsilon)
            lanes = pl.ds(pl.multiple_of((pair * PAIR + h) * HD, HD), HD)
            normed_ref[seq, :, lanes] = (mix * scale * gain_ref[...]).astype(bf16)

    @pl.when(step == steps + limit - 1)
    def _():
        ring.settle(1, n - 1)

        @pl.when(me < n - 1)
        def _():
            def done(at, carry):
                for h in range(PAIR):
                    hop(at, h).wait_send()
                return carry

            lax.fori_loop(0, steps, done, 0)


def mixer(projected, strength, filters, gain, weight):
    n = lax.axis_size("dp")
    seqs, extended, width = projected.shape
    rows = extended - RIM
    local = width // 3
    pairs = local // (PAIR * HD)
    wide = PAIR * HD
    steps = seqs * pairs
    limit = min((3 * (n - 1) + 4) // 5, steps)
    assert rows == 2 * HD
    vmem, anywhere = pl.BlockSpec(memory_space=pltpu.VMEM), pl.BlockSpec(memory_space=pl.ANY)

    def now(i):
        return jnp.minimum(i, steps - 1)

    def part(column):
        return pl.BlockSpec(
            (1, extended, wide),
            lambda i: (lax.div(now(i), pairs), 0, column * pairs + lax.rem(now(i), pairs)),
        )

    def whole(*shape):
        return pl.BlockSpec(shape, lambda i: (0,) * len(shape))

    total = steps * PAIR
    return pl.pallas_call(
        functools.partial(mixer_kernel, n, rows, steps, pairs, limit),
        grid=(steps + limit,),
        in_specs=[
            part(0), part(1), part(2),
            pl.BlockSpec((1, rows, strength.shape[2]), lambda i: (lax.div(now(i), pairs), 0, 0)),
            pl.BlockSpec((3 * KCONV, wide), lambda i: (0, lax.rem(now(i), pairs))),
            whole(1, HD),
            vmem,
        ],
        out_specs=[
            whole(seqs, rows, local),
            whole(steps, PAIR, rows, HD),
            whole(steps, PAIR, rows, HD),
            pl.BlockSpec((PAIR, rows, rows), lambda i: (now(i), 0, 0)),
            whole(steps, PAIR, HD, HD),
            whole(steps, PAIR, HD, HD),
            anywhere,
        ],
        out_shape=[
            jax.ShapeDtypeStruct((seqs, rows, local), bf16),
            jax.ShapeDtypeStruct((steps, PAIR, rows, HD), f32),
            jax.ShapeDtypeStruct((steps, PAIR, rows, HD), f32),
            jax.ShapeDtypeStruct((total, rows, rows), f32),
            jax.ShapeDtypeStruct((steps, PAIR, HD, HD), f32),
            jax.ShapeDtypeStruct((steps, PAIR, HD, HD), bf16),
            jax.ShapeDtypeStruct((n,) + weight.shape, bf16),
        ],
        scratch_shapes=[
            pltpu.VMEM((extended, wide), f32),
            pltpu.VMEM((PAIR, rows, rows), f32),
            pltpu.VMEM((PAIR, 2, HD, HD), f32),
            pltpu.VMEM((steps, PAIR, HD, HD), f32),
            pltpu.VMEM((steps, PAIR, HD, HD), bf16),
            pltpu.VMEM((steps, PAIR, HD, HD), bf16),
            pltpu.SemaphoreType.DMA((steps, PAIR)),
            pltpu.SemaphoreType.DMA((steps, PAIR)),
        ]
        + ring_semaphores(n)
        + [pltpu.SemaphoreType.DMA],
        compiler_params=pltpu.CompilerParams(
            collective_id=0, has_side_effects=True, vmem_limit_bytes=VMEM_LIMIT,
            dimension_semantics=("arbitrary",),
        ),
        name="mixer",
    )(projected, projected, projected, strength, filters, gain, weight)


def mixer_back_kernel(
    n, rows, steps, pairs,
    pq_ref, pk_ref, pv_ref, strength_ref, filt_ref, gain_ref,
    back_ref, mix_ref, carry_ref, inv_ref, kw_ref, state_ref,
    proj_ref, logit_ref, conv_ref, head_ref,
    xq_ref, xk_ref, xv_ref, bc_ref, high_ref, low_ref, recv_ref, send_ref, last_ref, rim_ref, next_ref,
    send_sem, recv_sem, rim_send, rim_recv,
):
    me = lax.axis_index("dp")
    step = pl.program_id(0)
    wide = PAIR * HD
    local = proj_ref.shape[2] // 3

    def to_rim(seq):
        return remote(
            rim_ref.at[seq], next_ref.at[seq], rim_send.at[seq], rim_recv.at[seq],
            dp=lax.rem(me + n - 1, n),
        )

    def hop(at, h):
        return remote(
            send_ref.at[at, h], recv_ref.at[at, h], send_sem.at[at, h], recv_sem.at[at, h],
            dp=lax.rem(me + n - 1, n),
        )

    @pl.when(step == 0)
    def _():
        barrier = pltpu.get_barrier_semaphore()

        @pl.when(me < n - 1)
        def _():
            pl.semaphore_signal(barrier, inc=1, device_id={"dp": lax.rem(me + 1, n)}, device_id_type=MESH)

        @pl.when(me == n - 1)
        def _():
            recv_ref[...] = jnp.zeros_like(recv_ref)
            next_ref[...] = jnp.zeros_like(next_ref)

        @pl.when(me > 0)
        def _():
            pl.semaphore_wait(barrier, 1)

        head_ref[...] = jnp.zeros_like(head_ref)
        bc_ref[...] = jnp.zeros_like(bc_ref)
        conv_ref[...] = jnp.zeros_like(conv_ref)

    @pl.when(step < steps)
    def _():
        adds = []
        head_sum = jnp.zeros((1, HD), f32)
        for h in range(PAIR):
            mix, back = mix_ref[0, h], back_ref[0, :, h * HD : (h + 1) * HD]
            scale = lax.rsqrt(jnp.mean(mix * mix, axis=-1, keepdims=True) + epsilon)
            unit = mix * scale
            head_sum = head_sum + jnp.sum(back * unit, axis=0, keepdims=True)
            scaled = back * gain_ref[...]
            out = halves(scale * (scaled - unit * jnp.mean(scaled * unit, axis=-1, keepdims=True)))
            high_ref[step, h], low_ref[step, h] = out
            adds.append(narrow_product(halves(carry_ref[0, h]), out, 0))
        head_ref[...] += jnp.where(
            lax.broadcasted_iota(jnp.int32, head_ref.shape, 0) == 0, head_sum, 0.0
        )

        for h in range(PAIR):
            @pl.when(me < n - 1)
            def _():
                hop(step, h).wait_recv()

            end, kw = recv_ref[step, h], halves(kw_ref[0, h])
            before = adds[h] + end.astype(f32) - dot(kw[0], end, 0, 0) - dot(kw[1], end, 0, 0)
            send_ref[step, h] = before.astype(bf16)

            @pl.when(me > 0)
            def _():
                hop(step, h).start()

    @pl.when(step >= steps)
    def _():
        now = step - steps
        seq, pair = lax.div(now, pairs), lax.rem(now, pairs)
        @pl.when(pair == 0)
        def _():
            logit_ref[...] = jnp.zeros_like(logit_ref)

        at_row, at_col = masks(rows)
        strengths = strength_ref[0]
        lane = lax.broadcasted_iota(jnp.int32, strengths.shape, 1)
        run_q, gate_q = conv_act(xq_ref, pq_ref[0], filt_ref, 0, rows)
        run_k, gate_k = conv_act(xk_ref, pk_ref[0], filt_ref, 1, rows)
        run_v, gate_v = conv_act(xv_ref, pv_ref[0], filt_ref, 2, rows)
        act_q, act_k, act_v = run_q * gate_q, run_k * gate_k, run_v * gate_v
        back_acts = ([], [], [])
        for h in range(PAIR):
            cut = slice(h * HD, (h + 1) * HD)
            scale_q, scale_k = unit_scale(act_q[:, cut]), unit_scale(act_k[:, cut])
            unit_q, unit_k = act_q[:, cut] * scale_q, act_k[:, cut] * scale_k
            q, k, v = unit_q.astype(bf16), unit_k.astype(bf16), act_v[:, cut].astype(bf16)
            chosen = lane == pair * PAIR + h
            beta = jnp.sum(jnp.where(chosen, strengths, 0.0), axis=-1, keepdims=True)
            gram = dot(k, k, 1, 1)
            scores = halves(jnp.where(at_row >= at_col, dot(q, k, 1, 1), 0.0))
            state, end = state_ref[0, h], recv_ref[now, h]
            out = (high_ref[now, h], low_ref[now, h])
            inv = halves(inv_ref[h])
            through = dot(k, beside(state, end))
            rest = v.astype(f32) - through[:, :HD]
            update = halves(narrow_product(inv, halves(beta * rest)))
            back_update = halves(narrow_product(scores, out, 0) + through[:, HD:])
            back_scores = short_product_t(out, update[0]) + dot(out[0], update[1], 1, 1)
            back_scores = halves(jnp.where(at_row >= at_col, back_scores, 0.0))
            solved = narrow_product(inv, back_update, 0)
            terms = halves(solved)
            back_low = short_product_t(terms, update[0]) + dot(terms[0], update[1], 1, 1)
            back_low = jnp.where(at_row > at_col, -back_low, 0.0)
            back_beta = jnp.sum(back_low * gram, axis=-1, keepdims=True) + jnp.sum(
                solved * rest, axis=-1, keepdims=True
            )
            back_gram = beta * back_low
            back_gram = halves(back_gram + back_gram.T)
            back_value = beta * solved
            back_q = short_product_t(out, state) + dot(back_scores[0], k) + dot(back_scores[1], k)
            back_k = (
                dot(back_scores[0], q, 0, 0)
                + dot(back_scores[1], q, 0, 0)
                + short_product_t(update, end)
                + dot(back_gram[0], k)
                + dot(back_gram[1], k)
                - short_product_t(halves(back_value), state)
            )
            logit_ref[0] += jnp.where(chosen, back_beta * beta * (1.0 - beta), 0.0)
            back_acts[0].append(
                (back_q - unit_q * jnp.sum(unit_q * back_q, axis=-1, keepdims=True)) * scale_q
            )
            back_acts[1].append(
                (back_k - unit_k * jnp.sum(unit_k * back_k, axis=-1, keepdims=True)) * scale_k
            )
            back_acts[2].append(back_value)

        for column, (running, gate, x_ref) in enumerate(
            ((run_q, gate_q, xq_ref), (run_k, gate_k, xk_ref), (run_v, gate_v, xv_ref))
        ):
            back_conv = beside(*back_acts[column]) * gate * (1.0 + running * (1.0 - gate))
            bc_ref[pl.ds(RIM, rows), :] = back_conv
            back_x, back_rim = None, None
            for tap in range(KCONV):
                weight = filt_ref[pl.ds(column * KCONV + tap, 1), :]
                term = weight * bc_ref[pl.ds(RIM + KCONV - 1 - tap, rows), :]
                edge = weight * bc_ref[pl.ds(KCONV - 1 - tap, RIM), :]
                back_x = term if back_x is None else back_x + term
                back_rim = edge if back_rim is None else back_rim + edge
                grad = jnp.sum(
                    back_conv * x_ref[pl.ds(RIM - KCONV + 1 + tap, rows), :], axis=0, keepdims=True
                )
                conv_ref[pair, pl.ds(column * KCONV + tap, 1), :] += grad
            lanes = pl.ds(pl.multiple_of(column * local + pair * wide, wide), wide)
            proj_ref[seq, :, lanes] = back_x.astype(bf16)
            last_ref[seq, :, lanes] = back_x[rows - RIM :, :]
            rim_ref[seq, :, lanes] = back_rim.astype(bf16)

        @pl.when((pair == pairs - 1) & (me > 0))
        def _():
            to_rim(seq).start()

    @pl.when(step == 2 * steps - 1)
    def _():
        seqs = steps // pairs

        @pl.when(me > 0)
        def _():
            def done(at, carry):
                for h in range(PAIR):
                    hop(at, h).wait_send()
                return carry

            lax.fori_loop(0, steps, done, 0)
            for seq in range(seqs):
                to_rim(seq).wait_send()

        @pl.when(me < n - 1)
        def _():
            for seq in range(seqs):
                to_rim(seq).wait_recv()

        for seq in range(seqs):
            edge = last_ref[seq] + next_ref[seq].astype(f32)
            proj_ref[seq, pl.ds(rows - RIM, RIM), :] = edge.astype(bf16)


def mixer_back(projected, strength, filters, gain, back_normed, mix, carry, inverse, kw, state):
    n = lax.axis_size("dp")
    seqs, extended, width = projected.shape
    rows = extended - RIM
    local = width // 3
    pairs = local // (PAIR * HD)
    wide = PAIR * HD
    steps = seqs * pairs
    def early(i):
        return jnp.minimum(i, steps - 1)

    def late(i):
        return jnp.maximum(i - steps, 0)

    def part(column):
        return pl.BlockSpec(
            (1, extended, wide),
            lambda i: (lax.div(late(i), pairs), 0, column * pairs + lax.rem(late(i), pairs)),
        )

    def tall(size, when):
        return pl.BlockSpec((1, PAIR, size, HD), lambda i: (when(i), 0, 0, 0))

    def seq(size, span):
        return pl.BlockSpec((1, size, span), lambda i: (lax.div(late(i), pairs), 0, 0))

    heads = strength.shape[2]
    return pl.pallas_call(
        functools.partial(mixer_back_kernel, n, rows, steps, pairs),
        grid=(2 * steps,),
        in_specs=[
            part(0), part(1), part(2),
            seq(rows, heads),
            pl.BlockSpec((3 * KCONV, wide), lambda i: (0, lax.rem(late(i), pairs))),
            pl.BlockSpec((1, HD), lambda i: (0, 0)),
            pl.BlockSpec(
                (1, rows, wide), lambda i: (lax.div(early(i), pairs), 0, lax.rem(early(i), pairs))
            ),
            tall(rows, early), tall(rows, early),
            pl.BlockSpec((PAIR, rows, rows), lambda i: (late(i), 0, 0)),
            tall(HD, early), tall(HD, late),
        ],
        out_specs=[
            pl.BlockSpec((seqs, rows, width), lambda i: (0, 0, 0)),
            seq(rows, heads),
            pl.BlockSpec((pairs, 3 * KCONV, wide), lambda i: (0, 0, 0)),
            pl.BlockSpec((8, HD), lambda i: (0, 0)),
        ],
        out_shape=[
            jax.ShapeDtypeStruct((seqs, rows, width), bf16),
            jax.ShapeDtypeStruct((seqs, rows, heads), f32),
            jax.ShapeDtypeStruct((pairs, 3 * KCONV, wide), f32),
            jax.ShapeDtypeStruct((8, HD), f32),
        ],
        scratch_shapes=[
            pltpu.VMEM((extended, wide), f32),
            pltpu.VMEM((extended, wide), f32),
            pltpu.VMEM((extended, wide), f32),
            pltpu.VMEM((rows + 2 * RIM, wide), f32),
            pltpu.VMEM((steps, PAIR, rows, HD), bf16),
            pltpu.VMEM((steps, PAIR, rows, HD), bf16),
            pltpu.VMEM((steps, PAIR, HD, HD), bf16),
            pltpu.VMEM((steps, PAIR, HD, HD), bf16),
            pltpu.VMEM((seqs, RIM, width), f32),
            pltpu.VMEM((seqs, RIM, width), bf16),
            pltpu.VMEM((seqs, RIM, width), bf16),
            pltpu.SemaphoreType.DMA((steps, PAIR)),
            pltpu.SemaphoreType.DMA((steps, PAIR)),
            pltpu.SemaphoreType.DMA((seqs,)),
            pltpu.SemaphoreType.DMA((seqs,)),
        ],
        compiler_params=pltpu.CompilerParams(
            collective_id=1, has_side_effects=True, vmem_limit_bytes=VMEM_LIMIT,
            dimension_semantics=("arbitrary",),
        ),
        name="mixer_back",
    )(
        projected, projected, projected, strength, filters, gain,
        back_normed, mix, carry, inverse, kw, state,
    )


def opening_kernel(
    n, tensor,
    q_ref, k_ref, v_ref, small_ref, tokens_ref, cot_ref, out_ref,
    qkv_ref, small_out, ext_ref, cot_out, full_out,
    zero_ref, local_sem, ring_send, ring_recv, side_send, side_recv, rim_send, rim_recv,
):
    me, t = lax.axis_index("dp"), lax.axis_index("tensor")
    place = ring_place(me, n)
    near = (ring_walk(lax.rem(place + 1, n), n), ring_walk(lax.rem(place + n - 1, n), n))
    core, cross = swap_pair(t), swap_half(t, tensor)
    rows, local = q_ref.shape
    own_len = tokens_ref.shape[1]
    slab = rows // (2 * SUBS)

    barrier = pltpu.get_barrier_semaphore()
    for device in ({"dp": near[0]}, {"dp": near[1]}, {"tensor": core}, {"tensor": cross}):
        pl.semaphore_signal(barrier, inc=1, device_id=device, device_id_type=MESH)

    @pl.when(me > 0)
    def _():
        pl.semaphore_signal(
            barrier, inc=1, device_id={"dp": lax.rem(me + n - 1, n), "tensor": tensor - 1},
            device_id_type=MESH,
        )

    def chunk(ref, at, offset):
        return ref.at[:, pl.ds(pl.multiple_of(offset + at * own_len, 8), own_len), :]

    mine = [
        pltpu.make_async_copy(ref, qkv_ref.at[me, :, pl.ds(c * local, local)], local_sem.at[c])
        for c, ref in enumerate((q_ref, k_ref, v_ref))
    ] + [
        pltpu.make_async_copy(small_ref, small_out.at[me], local_sem.at[3]),
        pltpu.make_async_copy(tokens_ref, chunk(ext_ref, t, RIM), local_sem.at[4]),
        pltpu.make_async_copy(cot_ref, chunk(cot_out, t, 0), local_sem.at[5]),
        pltpu.make_async_copy(out_ref, full_out.at[me], local_sem.at[7]),
    ]
    for copy in mine:
        copy.start()

    @pl.when(me == 0)
    def _():
        zero_ref[...] = jnp.zeros_like(zero_ref)
        blank = pltpu.make_async_copy(zero_ref, ext_ref.at[:, pl.ds(0, RIM), :], local_sem.at[6])
        blank.start()
        blank.wait()

    sends_rim = (me < n - 1) & (t == tensor - 1)

    @pl.when(sends_rim)
    def _():
        pl.semaphore_wait(barrier, 4 + tensor)

    @pl.when(jnp.logical_not(sends_rim))
    def _():
        pl.semaphore_wait(barrier, 4)

    def to_rim(peer):
        return remote(
            tokens_ref.at[:, pl.ds(own_len - RIM, RIM), :], ext_ref.at[:, pl.ds(0, RIM), :],
            rim_send.at[peer], rim_recv, dp=lax.rem(me + 1, n), tensor=peer,
        )

    sides = []
    for i, (own, full, offset) in enumerate(((tokens_ref, ext_ref, RIM), (cot_ref, cot_out, 0))):
        to_core = remote(own, chunk(full, t, offset), side_send.at[i, 0], side_recv.at[i, 0], tensor=core)
        to_cross = remote(own, chunk(full, t, offset), side_send.at[i, 1], side_recv.at[i, 1], tensor=cross)
        onward = remote(
            chunk(full, cross, offset), chunk(full, cross, offset),
            side_send.at[i, 2], side_recv.at[i, 2], tensor=core,
        )
        sides.append((to_core, to_cross, onward))
        to_core.start()
        to_cross.start()

    for copy in mine:
        copy.wait()

    @pl.when(sends_rim)
    def _():
        for peer in range(tensor):
            to_rim(peer).start()

    def ring(hop, lane):
        if lane == 2 * SUBS:
            owner = ring_walk(lax.rem(place + n - hop + 1, n), n)
            return remote(
                small_out.at[owner], small_out.at[owner],
                ring_send.at[hop, lane], ring_recv.at[hop, lane], dp=near[0],
            )
        way = lane % 2 if lane < 2 * SUBS else lane - 2 * SUBS - 1
        owner = ring_walk(lax.rem(place + n + (2 * way - 1) * (hop - 1), n), n)
        if lane > 2 * SUBS:
            piece = full_out.at[owner, pl.ds(way * (rows // 2), rows // 2), :]
            return remote(piece, piece, ring_send.at[hop, lane], ring_recv.at[hop, lane], dp=near[way])
        piece = qkv_ref.at[owner, pl.ds(lane * slab, slab), :]
        return remote(piece, piece, ring_send.at[hop, lane], ring_recv.at[hop, lane], dp=near[way])

    lanes = range(2 * SUBS + 3)

    def advance(hop, carry):
        for lane in lanes:
            @pl.when(hop > 1)
            def _():
                ring(hop - 1, lane).wait_recv()

            ring(hop, lane).start()
        for i, at in ((0, n // 2), (1, n - 1)):
            @pl.when(hop == at)
            def _():
                sides[i][1].wait_recv()
                sides[i][2].start()

        return carry

    lax.fori_loop(1, n, advance, 0)
    for lane in lanes:
        ring(n - 1, lane).wait_recv()

    def drain(hop, carry):
        for lane in lanes:
            ring(hop, lane).wait_send()
        return carry

    lax.fori_loop(1, n, drain, 0)
    for to_core, to_cross, onward in sides:
        to_core.wait()
        to_cross.wait_send()
        onward.wait()

    @pl.when(sends_rim)
    def _():
        for peer in range(tensor):
            to_rim(peer).wait_send()

    @pl.when(me > 0)
    def _():
        to_rim(0).wait_recv()


def opening(query_weight, key_weight, value_weight, small, tokens, cotangent, out_rows):
    n, tensor = lax.axis_size("dp"), lax.axis_size("tensor")
    rows, local = query_weight.shape
    seqs, own_len, width = tokens.shape
    vmem, anywhere = pl.BlockSpec(memory_space=pltpu.VMEM), pl.BlockSpec(memory_space=pl.ANY)
    lanes = 2 * SUBS + 3
    return pl.pallas_call(
        functools.partial(opening_kernel, n, tensor),
        in_specs=[vmem] * 7,
        out_specs=[anywhere] * 5,
        out_shape=[
            jax.ShapeDtypeStruct((n, rows, 3 * local), bf16),
            jax.ShapeDtypeStruct((n,) + small.shape, bf16),
            jax.ShapeDtypeStruct((seqs, RIM + tensor * own_len, width), bf16),
            jax.ShapeDtypeStruct((seqs, tensor * own_len, width), bf16),
            jax.ShapeDtypeStruct((n,) + out_rows.shape, bf16),
        ],
        scratch_shapes=[
            pltpu.VMEM((seqs, RIM, width), bf16),
            pltpu.SemaphoreType.DMA((8,)),
            pltpu.SemaphoreType.DMA((n, lanes)),
            pltpu.SemaphoreType.DMA((n, lanes)),
            pltpu.SemaphoreType.DMA((2, 3)),
            pltpu.SemaphoreType.DMA((2, 3)),
            pltpu.SemaphoreType.DMA((tensor,)),
            pltpu.SemaphoreType.DMA,
        ],
        compiler_params=pltpu.CompilerParams(
            collective_id=2, has_side_effects=True, vmem_limit_bytes=VMEM_LIMIT
        ),
        name="opening",
    )(query_weight, key_weight, value_weight, small, tokens, cotangent, out_rows)


def fold_kernel(
    n, n_seqs, tensor, backward, count,
    part_ref, own_ref, gain_ref, hidden_ref, *refs,
):
    t = lax.axis_index("tensor")
    core, cross = swap_pair(t), swap_half(t, tensor)
    both = swap_half(core, tensor)
    own_len = own_ref.shape[1]
    refs = list(refs)
    pieces, refs = refs[:count], refs[count:]
    outs = 1 if backward else count
    (rows_ref, keep_ref, sum_ref), made, refs = refs[:3], refs[3 : 3 + outs], refs[3 + outs :]
    (
        near_ref, far_ref, send_ref, own_sum_ref, a_send, a_recv, x_send, x_recv, g_send, g_recv,
        ring_send, ring_recv,
    ) = refs[:12]
    ring_refs = refs[12:]
    if backward:
        rings = [
            RingScatter(
                n, made[0].shape[0], grad_part(made[0].shape[0], *pieces, ring_refs[1]), ring_refs[0],
                made[0], ring_send.at[0], ring_recv.at[0],
            )
        ]
    else:
        rings = [
            RingGather(
                n, pieces[i].shape[0], made[i], ring_send.at[i], ring_recv.at[i], pieces[i], ring_refs[i]
            )
            for i in range(count)
        ]

    def advance(hop):
        if hop < n:
            for ring in rings:
                ring.advance(hop)

    barrier = pltpu.get_barrier_semaphore()
    rings[0].greet(barrier)
    for device in (core, cross):
        pl.semaphore_signal(barrier, inc=1, device_id={"tensor": device}, device_id_type=MESH)
    pl.semaphore_wait(barrier, 4)

    def span(at):
        return pl.ds(pl.multiple_of(at * own_len, own_len), own_len)

    def to_core(s, i):
        return remote(
            part_ref.at[s, span((core, both)[i]), :], near_ref.at[s, i],
            a_send.at[s, i], a_recv.at[s, i], tensor=core,
        )

    def to_cross(s):
        return remote(send_ref.at[s], far_ref.at[s], x_send.at[s], x_recv.at[s], tensor=cross)

    def gather(s, i):
        if i == 2:
            piece, peer = rows_ref.at[s, span(cross), :], core
        else:
            piece, peer = rows_ref.at[s, span(t), :], (cross, core)[i]
        return remote(piece, piece, g_send.at[s, i], g_recv.at[s, i], tensor=peer)

    for s in range(n_seqs):
        for i in (1, 0):
            to_core(s, i).start()
    for ring in rings:
        ring.start()

    def first(s, carry):
        to_core(s, 1).wait_recv()
        send_ref[s] = (
            part_ref[s, span(cross), :].astype(f32) + near_ref[s, 1].astype(f32)
        ).astype(bf16)
        to_cross(s).start()
        to_core(s, 0).wait_recv()
        own_sum_ref[s] = part_ref[s, span(t), :].astype(f32) + near_ref[s, 0].astype(f32)
        return carry

    lax.fori_loop(0, n_seqs, first, 0)
    sum_ref[...] = jnp.zeros_like(sum_ref)

    moments = (0, 1, 2, 3, 1) if backward else (0, 2, 0)

    def second(s, carry):
        to_cross(s).wait_recv()
        total = own_sum_ref[s] + far_ref[s].astype(f32)
        gain = gain_ref[...]
        own = own_ref[s].astype(f32)
        if backward:
            hidden = hidden_ref[s]
            scale = lax.rsqrt(jnp.mean(hidden * hidden, axis=-1, keepdims=True) + epsilon)
            unit = hidden * scale
            sum_ref[...] += jnp.sum(total * unit, axis=0, keepdims=True)
            scaled = total * gain
            kept = own + scale * (scaled - unit * jnp.mean(scaled * unit, axis=-1, keepdims=True))
            keep_ref[s] = kept
            rows_ref[s, span(t), :] = kept.astype(bf16)
        else:
            kept = own + total
            keep_ref[s] = kept
            scale = lax.rsqrt(jnp.mean(kept * kept, axis=-1, keepdims=True) + epsilon)
            rows_ref[s, span(t), :] = (kept * scale * gain).astype(bf16)
        gather(s, 0).start()
        gather(s, 1).start()

        for i, at in enumerate(moments[:-1]):
            @pl.when(s == at)
            def _():
                advance(2 + i)

        return carry

    lax.fori_loop(0, n_seqs, second, 0)

    def third(s, carry):
        gather(s, 0).wait_recv()
        gather(s, 2).start()

        @pl.when(s == moments[-1])
        def _():
            advance(1 + len(moments))

        return carry

    lax.fori_loop(0, n_seqs, third, 0)

    def rest(hop, carry):
        for ring in rings:
            ring.advance(hop)
        return carry

    lax.fori_loop(2 + len(moments), n, rest, 0)
    for ring in rings:
        if backward:
            ring.finish()
        else:
            ring.settle(1, n - 1)

    def last(s, carry):
        gather(s, 1).wait_recv()
        gather(s, 2).wait_recv()
        for i in range(2):
            to_core(s, i).wait_send()
        to_cross(s).wait_send()
        for i in range(3):
            gather(s, i).wait_send()
        return carry

    lax.fori_loop(0, n_seqs, last, 0)


def fold(part, own, gain, pieces, hidden=None):
    n, tensor = lax.axis_size("dp"), lax.axis_size("tensor")
    seqs, own_len, width = own.shape
    backward, count = hidden is not None, len(pieces)
    vmem, anywhere = pl.BlockSpec(memory_space=pltpu.VMEM), pl.BlockSpec(memory_space=pl.ANY)
    if backward:
        rows, columns = pieces[0].shape[1] // n, pieces[1].shape[1]
        made = [jax.ShapeDtypeStruct((rows, columns), f32)]
        ring_scratch = [pltpu.VMEM((n, rows, columns), bf16), spare(rows, columns)]
    else:
        hidden = jnp.zeros((8, 128), f32)
        made = [jax.ShapeDtypeStruct((n,) + piece.shape, bf16) for piece in pieces]
        ring_scratch = [pltpu.SemaphoreType.DMA for _ in pieces]
    return pl.pallas_call(
        functools.partial(fold_kernel, n, seqs, tensor, backward, count),
        in_specs=[vmem] * (4 + count),
        out_specs=[vmem] * 3 + [vmem if backward else anywhere] * len(made),
        out_shape=[
            jax.ShapeDtypeStruct((seqs, tensor * own_len, width), bf16),
            jax.ShapeDtypeStruct((seqs, own_len, width), f32),
            jax.ShapeDtypeStruct((1, width), f32),
        ]
        + made,
        scratch_shapes=[
            pltpu.VMEM((seqs, 2, own_len, width), bf16),
            pltpu.VMEM((seqs, own_len, width), bf16),
            pltpu.VMEM((seqs, own_len, width), bf16),
            pltpu.VMEM((seqs, own_len, width), f32),
            pltpu.SemaphoreType.DMA((seqs, 2)),
            pltpu.SemaphoreType.DMA((seqs, 2)),
            pltpu.SemaphoreType.DMA((seqs,)),
            pltpu.SemaphoreType.DMA((seqs,)),
            pltpu.SemaphoreType.DMA((seqs, 3)),
            pltpu.SemaphoreType.DMA((seqs, 3)),
            pltpu.SemaphoreType.DMA((count, n, 2 * SUBS)),
            pltpu.SemaphoreType.DMA((count, n, 2 * SUBS)),
        ]
        + ring_scratch,
        compiler_params=pltpu.CompilerParams(
            collective_id=4 if backward else 3, has_side_effects=True, vmem_limit_bytes=VMEM_LIMIT
        ),
        name="fold_back" if backward else "fold",
    )(part, own, gain, hidden, *pieces)


def closing_kernel(
    n, n_seqs, tensor,
    own_ref, tokens_ref, gain_ref, small_ref, *refs,
):
    hbm, refs = refs[:9], refs[9:]
    d_ref, gate_sum, out_sum, qkv_sum, small_sum, gain_sum, shared_ref = refs[:7]
    refs = refs[7:]
    held, refs = refs[:9], refs[9:]
    (
        gate_in, out_in, qkv_in, small_in, gain_in, spare_gate, spare_out, spare_qkv,
        part_ref, near_ref, far_ref, send_ref, total_ref, pass_ref, got_ref,
        load_sem, a_send, a_recv, x_send, x_recv, ring_send, ring_recv, s_send, s_recv,
    ) = refs
    second_ref, gate_ref, back_ref, mix_ref, proj_ref, weight_ref, logit_ref, beta_ref, first_ref = held
    me, t = lax.axis_index("dp"), lax.axis_index("tensor")
    core, cross = swap_pair(t), swap_half(t, tensor)
    both = swap_half(core, tensor)
    own_len = tokens_ref.shape[1]
    length = own_len * tensor
    rows, width = gate_sum.shape[0], gain_ref.shape[1]
    block = gain_sum.shape[1]

    loads = [
        pltpu.make_async_copy(source, target, load_sem.at[i])
        for i, (source, target) in enumerate(zip(hbm, held))
    ]
    for load in loads:
        load.start()

    def gain_part(owner, way):
        at = lax.div(owner * (width // n), block) * block
        return total_ref[pl.ds(way * 16, 16), pl.ds(pl.multiple_of(at, 128), block)]

    def ring(i, count, part, inward, total, lanes=2 * SUBS):
        return RingScatter(n, count, part, inward, total, ring_send.at[i], ring_recv.at[i], lanes)

    gate = ring(0, rows, grad_part(rows, second_ref, gate_ref, spare_gate), gate_in, gate_sum)
    out = ring(1, rows, grad_part(rows, back_ref, mix_ref, spare_out), out_in, out_sum)
    qkv = ring(2, rows, grad_part(rows, first_ref, proj_ref, spare_qkv), qkv_in, qkv_sum)
    small = ring(3, small_ref.shape[1], held_part(small_ref), small_in, small_sum, 2)
    gains = ring(4, 32, gain_part, gain_in, gain_sum, 2)

    barrier = pltpu.get_barrier_semaphore()
    gate.greet(barrier)
    for device in (core, cross):
        pl.semaphore_signal(barrier, inc=1, device_id={"tensor": device}, device_id_type=MESH)
    pl.semaphore_wait(barrier, 4)

    def span(at):
        return pl.ds(pl.multiple_of(at * own_len, own_len), own_len)

    def to_core(s, i):
        return remote(
            part_ref.at[s, span((core, both)[i]), :], near_ref.at[s, i],
            a_send.at[s, i], a_recv.at[s, i], tensor=core,
        )

    def to_cross(s):
        return remote(send_ref.at[s], far_ref.at[s], x_send.at[s], x_recv.at[s], tensor=cross)

    early = (gate, out, small)
    for load in loads[:4]:
        load.wait()
    for chain in early:
        chain.start()
    for load in loads[4:]:
        load.wait()

    def input_grad(s, carry):
        here = pl.ds(pl.multiple_of(s * length, length), length)
        part_ref[s] = (
            dot(proj_ref[here, :], weight_ref[...], 1, 1) + dot(logit_ref[here, :], beta_ref[...], 1, 1)
        ).astype(bf16)
        for i in (1, 0):
            to_core(s, i).start()
        for chain in early:
            chain.advance(2 + s)
        return carry

    lax.fori_loop(0, n_seqs, input_grad, 0)

    def first(s, carry):
        to_core(s, 1).wait_recv()
        send_ref[s] = (
            part_ref[s, span(cross), :].astype(f32) + near_ref[s, 1].astype(f32)
        ).astype(bf16)
        to_cross(s).start()
        return carry

    lax.fori_loop(0, n_seqs, first, 0)
    for chain in early:
        chain.advance(2 + n_seqs)
    total_ref[...] = jnp.zeros_like(total_ref)

    def second(s, carry):
        to_core(s, 0).wait_recv()
        to_cross(s).wait_recv()
        total = (
            part_ref[s, span(t), :].astype(f32) + near_ref[s, 0].astype(f32) + far_ref[s].astype(f32)
        )
        tokens = tokens_ref[s].astype(f32)
        scale = lax.rsqrt(jnp.mean(tokens * tokens, axis=-1, keepdims=True) + epsilon)
        unit = tokens * scale
        total_ref[...] += jnp.sum(total * unit, axis=0, keepdims=True)
        scaled = total * gain_ref[...]
        d_ref[s] = (
            own_ref[s] + scale * (scaled - unit * jnp.mean(scaled * unit, axis=-1, keepdims=True))
        ).astype(bf16)
        return carry

    lax.fori_loop(0, n_seqs, second, 0)

    def rest(hop, carry):
        for chain in early:
            chain.advance(hop)
        return carry

    lax.fori_loop(3 + n_seqs, n, rest, 0)
    qkv.start()
    gains.start()
    for chain in early:
        chain.finish()

    def final(hop, carry):
        for chain in (qkv, gains):
            chain.advance(hop)
        return carry

    lax.fori_loop(2, n, final, 0)
    gains.finish()
    shared_ref[0, :, :] = small_sum[...]
    shared_ref[1, :, :] = jnp.zeros_like(small_sum)
    for c in range(block // 128):
        shared_ref[1, pl.ds(c, 1), :] = gain_sum[pl.ds(0, 1), c * 128 : (c + 1) * 128]
    for i, peer in enumerate((core, cross)):
        pass_ref[i] = shared_ref[...]
        share = remote(pass_ref.at[i], got_ref.at[i], s_send.at[i], s_recv.at[i], tensor=peer)
        share.start()
        share.wait()
        shared_ref[...] += got_ref[i]
    qkv.finish()

    def last(s, carry):
        for i in range(2):
            to_core(s, i).wait_send()
        to_cross(s).wait_send()
        return carry

    lax.fori_loop(0, n_seqs, last, 0)


def closing(own, tokens, gain, small, factors):
    n, tensor = lax.axis_size("dp"), lax.axis_size("tensor")
    seqs, own_len, width = tokens.shape
    rows, block = width // n, max(128, width // n)
    columns = [factors[i].shape[1] for i in (1, 3, 4)]
    vmem, anywhere = pl.BlockSpec(memory_space=pltpu.VMEM), pl.BlockSpec(memory_space=pl.ANY)
    shared = (2,) + small.shape[1:]
    return pl.pallas_call(
        functools.partial(closing_kernel, n, seqs, tensor),
        in_specs=[vmem] * 4 + [anywhere] * 9,
        out_specs=[vmem] * 7,
        out_shape=[jax.ShapeDtypeStruct((seqs, own_len, width), bf16)]
        + [jax.ShapeDtypeStruct((rows, count), f32) for count in columns]
        + [
            jax.ShapeDtypeStruct(small.shape[1:], f32),
            jax.ShapeDtypeStruct((32, block), f32),
            jax.ShapeDtypeStruct(shared, f32),
        ],
        scratch_shapes=[pltpu.VMEM(factor.shape, bf16) for factor in factors]
        + [pltpu.VMEM((n, rows, count), bf16) for count in columns]
        + [pltpu.VMEM(small.shape, bf16), pltpu.VMEM((n, 32, block), bf16)]
        + [spare(rows, count) for count in columns]
        + [
            pltpu.VMEM((seqs, own_len * tensor, width), bf16),
            pltpu.VMEM((seqs, 2, own_len, width), bf16),
            pltpu.VMEM((seqs, own_len, width), bf16),
            pltpu.VMEM((seqs, own_len, width), bf16),
            pltpu.VMEM((32, width), f32),
            pltpu.VMEM((2,) + shared, f32),
            pltpu.VMEM((2,) + shared, f32),
            pltpu.SemaphoreType.DMA((9,)),
            pltpu.SemaphoreType.DMA((seqs, 2)),
            pltpu.SemaphoreType.DMA((seqs, 2)),
            pltpu.SemaphoreType.DMA((seqs,)),
            pltpu.SemaphoreType.DMA((seqs,)),
            pltpu.SemaphoreType.DMA((5, n, 2 * SUBS)),
            pltpu.SemaphoreType.DMA((5, n, 2 * SUBS)),
            pltpu.SemaphoreType.DMA((2,)),
            pltpu.SemaphoreType.DMA((2,)),
        ],
        compiler_params=pltpu.CompilerParams(
            collective_id=5, has_side_effects=True, vmem_limit_bytes=63 * 1024 * 1024
        ),
        name="closing",
    )(own, tokens, gain, small, *factors)


def rms_unit(values):
    scale = lax.rsqrt(jnp.mean(values * values, axis=-1, keepdims=True) + epsilon)
    return values * scale, scale


def rms_back(back, unit, scale, gain):
    scaled = back * gain
    return scale * (scaled - unit * jnp.mean(scaled * unit, axis=-1, keepdims=True))


def flat(array):
    return array.reshape(-1, array.shape[-1])


def matmul(spec, left, right):
    return jnp.einsum(spec, left, right, preferred_element_type=f32)


def swap(block, axis, half):
    count = lax.axis_size(axis)
    route = [(i, (i + count // 2) % count if half else i ^ 1) for i in range(count)]
    return lax.ppermute(block, axis, route)


def tensor_scatter(part):
    tensor, t = lax.axis_size("tensor"), lax.axis_index("tensor")
    seqs, rows, width = part.shape
    chunks = part.reshape(seqs, tensor, rows // tensor, width)

    def chunk(at):
        return lax.dynamic_index_in_dim(chunks, at, 1, keepdims=False)

    core, cross = swap_pair(t), swap_half(t, tensor)
    both = swap_half(core, tensor)
    near_own, near_cross = swap(chunk(core), "tensor", False), swap(chunk(both), "tensor", False)
    far = swap((chunk(cross).astype(f32) + near_cross.astype(f32)).astype(bf16), "tensor", True)
    return chunk(t).astype(f32) + near_own.astype(f32) + far.astype(f32)


def shards(
    tokens,
    cotangent,
    query_weight,
    key_weight,
    value_weight,
    beta_weight,
    conv_filter,
    norm_gain,
    head_gain,
    out_weight,
    gate_weight,
    up_weight,
    down_weight,
):
    n = lax.axis_size("dp")
    tensor = lax.axis_size("tensor")
    seqs, own_len, width = tokens.shape
    local = query_weight.shape[1]
    heads = local // HD
    hidden = gate_weight.shape[1]

    packed = jnp.concatenate(
        [conv_filter.reshape(-1), norm_gain.reshape(-1), head_gain, beta_weight.reshape(-1)]
    )
    block = -(-packed.size // 4096) * 4096
    small = jnp.pad(packed, (0, block - packed.size)).reshape(-1, 128)
    full_qkv, full_small, extended, rows_cotangent, full_out = opening(
        query_weight, key_weight, value_weight, small, tokens, cotangent, out_weight.T
    )
    full_out = full_out.reshape(width, local)
    full_qkv = full_qkv.reshape(width, 3 * local)
    full_small = full_small.reshape(n, block)
    sizes = [conv_filter.size, norm_gain.size, head_gain.size, beta_weight.size]
    ends = [sum(sizes[: i + 1]) for i in range(4)]
    filters = (
        full_small[:, : ends[0]]
        .reshape(n, 3 * KCONV, heads, HD // n)
        .transpose(1, 2, 0, 3)
        .reshape(3 * KCONV, local)
        .astype(f32)
    )
    gains = (
        full_small[:, ends[0] : ends[1]].reshape(n, 2, width // n).transpose(1, 0, 2).reshape(2, width)
    ).astype(f32)
    head_row = full_small[:, ends[1] : ends[2]].reshape(1, HD).astype(f32)
    full_beta = full_small[:, ends[2] : ends[3]].reshape(width, heads)

    unit_ext, _ = rms_unit(extended.astype(f32))
    normed_ext = (unit_ext * gains[0]).astype(bf16)
    normed_first = normed_ext[:, RIM:]
    projected = matmul("std,dm->stm", normed_ext, full_qkv).astype(bf16)
    strength = jax.nn.sigmoid(matmul("std,dh->sth", normed_first, full_beta))
    normed_mix, mix, carry, inverse, kw, state, full_gate = mixer(
        projected, strength, filters, head_row, gate_weight
    )
    full_gate = full_gate.reshape(width, hidden)

    branch_part = matmul("stk,dk->std", normed_mix, full_out).astype(bf16)
    normed_second, hidden_state, _, full_up, full_down = fold(
        branch_part, tokens, gains[1:2], [up_weight, down_weight.T]
    )
    full_up, full_down = full_up.reshape(width, hidden), full_down.reshape(width, hidden)
    gate_pre = matmul("std,df->stf", normed_second, full_gate)
    up_pre = matmul("std,df->stf", normed_second, full_up)
    gate_sigmoid = jax.nn.sigmoid(gate_pre)
    ffn_hidden = (gate_pre * gate_sigmoid * up_pre).astype(bf16)

    back_hidden = matmul("std,df->stf", rows_cotangent, full_down)
    back_gate = (
        back_hidden * up_pre * gate_sigmoid * (1.0 + gate_pre * (1.0 - gate_sigmoid))
    ).astype(bf16)
    back_up = (back_hidden * gate_pre * gate_sigmoid).astype(bf16)
    back_second = matmul("stf,df->std", back_gate, full_gate) + matmul("stf,df->std", back_up, full_up)
    rows_back, back_state, gain_second, grad_down = fold(
        back_second.astype(bf16), cotangent, gains[1:2],
        [flat(rows_cotangent), flat(ffn_hidden)], hidden_state,
    )
    rows_back, back_up, ffn_hidden = lax.optimization_barrier((rows_back, back_up, ffn_hidden))
    grad_up = matmul("std,stf->df", normed_second, back_up)
    ffn_part = matmul("stf,df->std", ffn_hidden, full_down).astype(bf16)
    layer_out = (hidden_state + tensor_scatter(ffn_part)).astype(bf16)
    back_normed = matmul("std,dk->stk", rows_back, full_out)
    back_proj, back_logit, conv_part, head_part = mixer_back(
        projected, strength, filters, head_row, back_normed, mix, carry, inverse, kw, state
    )
    back_logit = back_logit.astype(bf16)
    grad_beta = matmul("std,sth->dh", normed_first, back_logit)
    grad_conv = conv_part.transpose(1, 0, 2).reshape(3 * KCONV, local)
    gain_grads = jnp.concatenate([jnp.zeros_like(gain_second), gain_second])
    small_grads = jnp.concatenate(
        [
            grad_conv.reshape(3 * KCONV, heads, n, HD // n).transpose(2, 0, 1, 3).reshape(n, -1),
            gain_grads.reshape(2, n, width // n).transpose(1, 0, 2).reshape(n, -1),
            head_part[0].reshape(n, HD // n),
            grad_beta.reshape(n, -1),
        ],
        axis=1,
    )
    small_grads = jnp.pad(small_grads, ((0, 0), (0, block - small_grads.shape[1])))
    lanes = ((0, 0), (0, 128 - heads))
    d_tokens, grad_gate, grad_out, grad_qkv, small_grads, _, shared = closing(
        back_state, tokens, gains[0:1], small_grads.astype(bf16).reshape(n, -1, 128),
        [
            flat(normed_second), flat(back_gate), flat(rows_back), flat(normed_mix), flat(back_proj),
            full_qkv, jnp.pad(flat(back_logit), lanes), jnp.pad(full_beta, lanes), flat(normed_first),
        ],
    )
    gain_row = shared[1, : max(1, width // n // 128)].reshape(-1)
    if width // n < 128:
        start = lax.rem(lax.axis_index("dp") * (width // n), 128)
        gain_row = lax.dynamic_slice_in_dim(gain_row, start, width // n)
    shared = shared[0]
    small_grads, shared = small_grads.reshape(-1), shared.reshape(-1)

    def scatter(grad):
        return lax.psum_scatter(grad.astype(bf16), "dp", scatter_dimension=0, tiled=True).astype(f32)

    grad_up = scatter(grad_up)
    return (
        layer_out,
        d_tokens,
        grad_qkv[:, :local],
        grad_qkv[:, local : 2 * local],
        grad_qkv[:, 2 * local :],
        small_grads[ends[2] : ends[3]].reshape(beta_weight.shape),
        small_grads[: ends[0]].reshape(conv_filter.shape),
        jnp.stack([gain_row, shared[ends[0] + width // n : ends[1]]]),
        shared[ends[1] : ends[2]],
        grad_out.T,
        grad_gate,
        grad_up,
        grad_down.T,
    )


def solution(mesh):
    both = P(None, ("dp", "tensor"), None)
    rows, cols = P("dp", "tensor"), P("tensor", "dp")
    conv, gain, head = P(None, "tensor", "dp"), P(None, "dp"), P("dp")
    return jax.shard_map(
        shards,
        mesh=mesh,
        in_specs=(both, both, rows, rows, rows, rows, conv, gain, head, cols, rows, rows, cols),
        out_specs=(both, both, rows, rows, rows, rows, conv, gain, head, cols, rows, rows, cols),
        check_vma=False,
    )
```

```python
import functools

import jax
import jax.numpy as jnp
from jax import lax
from jax.experimental import pallas as pl
from jax.experimental.pallas import tpu as pltpu
from jax.sharding import PartitionSpec as P

HD = 128
KCONV = 4
RIM = 8
PAIR = 2
OUTER = 4
SUBS = 2

epsilon = 1e-06
f32 = jnp.float32
bf16 = jnp.bfloat16
MESH = pl.DeviceIdType.MESH
VMEM_LIMIT = 60 * 1024 * 1024


def ring_walk(place, n):
    inner = n // OUTER
    if inner == 1:
        return place
    late = jnp.maximum(place - OUTER, 0)
    turn, along = lax.div(late, inner - 1), lax.rem(late, inner - 1)
    odd = lax.rem(turn, 2)
    back = (OUTER - 1 - turn) * inner + (1 - odd) * (along + 1) + odd * (inner - 1 - along)
    return jnp.where(place < OUTER, place * inner, back)


def ring_place(index, n):
    inner = n // OUTER
    if inner == 1:
        return index
    out, along = lax.div(index, inner), lax.rem(index, inner)
    odd = lax.rem(OUTER - 1 - out, 2)
    turn = (1 - odd) * (along - 1) + odd * (inner - 1 - along)
    return jnp.where(along == 0, out, OUTER + (OUTER - 1 - out) * (inner - 1) + turn)


def remote(source, target, send, recv, **device):
    return pltpu.make_async_remote_copy(
        src_ref=source, dst_ref=target, send_sem=send, recv_sem=recv,
        device_id=device, device_id_type=MESH,
    )


def swap_pair(index):
    return index + 1 - 2 * lax.rem(index, 2)


def swap_half(index, count):
    return lax.rem(index + count // 2, count)


class Ring:
    def __init__(self, n, rows, lanes, send, recv):
        self.n, self.lanes, self.send, self.recv = n, range(lanes), send, recv
        self.me = lax.axis_index("dp")
        self.place = ring_place(self.me, n)
        self.near = (
            ring_walk(lax.rem(self.place + 1, n), n),
            ring_walk(lax.rem(self.place + n - 1, n), n),
        )
        self.slab = rows // lanes

    def greet(self, barrier):
        for device in self.near:
            pl.semaphore_signal(barrier, inc=1, device_id={"dp": device}, device_id_type=MESH)

    def strip(self, lane):
        return pl.ds(lane * self.slab, self.slab)

    def owner(self, hop, lane):
        return ring_walk(lax.rem(self.place + self.n + (2 * (lane % 2) - 1) * hop, self.n), self.n)

    def copy(self, source, target, hop, lane):
        return remote(
            source, target, self.send.at[hop, lane], self.recv.at[hop, lane], dp=self.near[lane % 2]
        )


class RingGather(Ring):
    def __init__(self, n, rows, full, send, recv, own=None, local=None, lanes=2 * SUBS):
        super().__init__(n, rows, lanes, send, recv)
        self.own, self.full, self.local = own, full, local

    def first(self, lane):
        strip = self.strip(lane)
        return self.copy(self.own.at[strip, :], self.full.at[self.me, strip, :], 1, lane)

    def later(self, hop, lane):
        piece = self.full.at[self.owner(hop - 1, lane), self.strip(lane), :]
        return self.copy(piece, piece, hop, lane)

    def stay(self):
        return pltpu.make_async_copy(self.own, self.full.at[self.me], self.local)

    def start(self):
        self.stay().start()
        for lane in self.lanes:
            self.first(lane).start()

    def advance(self, hop, lanes=None):
        for lane in self.lanes if lanes is None else lanes:
            self.later(hop - 1, lane).wait_recv()
            self.later(hop, lane).start()

    def settle(self, begin, end):
        for lane in self.lanes:
            self.later(end, lane).wait_recv()
            if begin == 1:
                self.first(lane).wait_send()

        def drain(hop, carry):
            for lane in self.lanes:
                self.later(hop, lane).wait_send()
            return carry

        lax.fori_loop(max(begin, 2), end + 1, drain, 0)
        if begin == 1:
            self.stay().wait()


class RingScatter(Ring):
    def __init__(self, n, rows, part, inward, total, send, recv, lanes=2 * SUBS):
        super().__init__(n, rows, lanes, send, recv)
        self.part, self.inward, self.total = part, inward, total
        self.half = rows // 2

    def strip(self, lane):
        return pl.ds((lane % 2) * self.half + (lane // 2) * self.slab, self.slab)

    def sender(self, hop, lane):
        strip = self.strip(lane)
        return self.copy(self.inward.at[hop - 1, strip, :], self.inward.at[hop, strip, :], hop, lane)

    def ways(self, value_of):
        for way in range(2):
            value = value_of(way)
            for lane in self.lanes[way::2]:
                at = (lane // 2) * self.slab
                yield lane, value[at : at + self.slab]

    def start(self):
        for lane, value in self.ways(lambda way: self.part(self.owner(1, way), way)):
            self.inward[0, self.strip(lane), :] = value.astype(bf16)
            self.sender(1, lane).start()

    def summed(self, hop, lane, value):
        self.sender(hop, lane).wait_recv()
        return self.inward[hop, self.strip(lane), :].astype(f32) + value

    def advance(self, hop):
        for lane, value in self.ways(lambda way: self.part(self.owner(hop, way), way)):
            self.forward(hop, lane, value)

    def advance_first(self, hop, kept):
        for way in range(2):
            value = self.part(self.owner(hop, way), way)
            kept[way] = value[self.slab :]
            self.forward(hop, way, value[: self.slab])

    def advance_second(self, hop, kept):
        for way in range(2):
            self.forward(hop, 2 + way, kept[way])

    def forward(self, hop, lane, value):
        self.inward[hop - 1, self.strip(lane), :] = self.summed(hop - 1, lane, value).astype(bf16)
        self.sender(hop, lane).start()

    def finish(self):
        for lane, value in self.ways(lambda way: self.part(self.me, way)):
            self.total[self.strip(lane), :] = self.summed(self.n - 1, lane, value)

        def drain(hop, carry):
            for lane in self.lanes:
                self.sender(hop, lane).wait_send()
            return carry

        lax.fori_loop(1, self.n, drain, 0)


def held_part(ref):
    half = ref.shape[1] // 2
    return lambda owner, way: ref[owner, way * half : (way + 1) * half, :].astype(f32)


def grad_part(rows, left_ref, right_ref, spare_ref=None):
    half = rows // 2

    def part(owner, way):
        at = owner * rows + way * half
        if half % 128 == 0:
            return dot(left_ref[:, pl.ds(pl.multiple_of(at, half), half)], right_ref[...], 0, 0)
        block = lax.div(at, 128) * 128
        spare_ref[...] = dot(left_ref[:, pl.ds(pl.multiple_of(block, 128), 128)], right_ref[...], 0, 0)
        return spare_ref[pl.ds(pl.multiple_of(at - block, half), half), :]

    return part


def spare(rows, columns):
    return pltpu.VMEM((8, 128) if (rows // 2) % 128 == 0 else (128, columns), f32)


def ring_semaphores(n, lanes=2 * SUBS):
    return [pltpu.SemaphoreType.DMA((n, lanes)), pltpu.SemaphoreType.DMA((n, lanes))]


def halves(value):
    high = value.astype(bf16)
    return (high, (value - high.astype(f32)).astype(bf16))


def dot(left, right, left_dim=1, right_dim=0):
    return lax.dot_general(
        left, right, (((left_dim,), (right_dim,)), ((), ())), preferred_element_type=f32
    )


def beside(*parts):
    return jnp.concatenate(parts, axis=1)


def full_product(left, right, left_dim=1, right_dim=0):
    return (
        dot(left[0], right[0], left_dim, right_dim)
        + dot(left[1], right[0], left_dim, right_dim)
        + dot(left[0], right[1], left_dim, right_dim)
    )


def narrow_product(left, right, left_dim=1):
    both = dot(left[0], beside(*right), left_dim, 0)
    width = right[0].shape[1]
    return both[:, :width] + both[:, width:] + dot(left[1], right[0], left_dim, 0)


def short_product(left, right):
    return dot(beside(*left), jnp.concatenate([right, right], axis=0))


def short_product_t(left, right):
    return dot(beside(*left), beside(right, right), 1, 1)


def square_product(left, right):
    lower = beside(right[0], jnp.zeros_like(right[0]))
    both = dot(beside(*left), jnp.concatenate([beside(*right), lower], axis=0))
    return both[:, :HD] + both[:, HD:]


def conv_act(x_ref, x_in, filt_ref, column, rows):
    x_ref[...] = x_in.astype(f32)
    running = None
    for tap in range(KCONV):
        term = filt_ref[pl.ds(column * KCONV + tap, 1), :] * x_ref[pl.ds(RIM - KCONV + 1 + tap, rows), :]
        running = term if running is None else running + term
    gate = jax.nn.sigmoid(running)
    return running, gate


def unit_scale(act):
    return lax.rsqrt(jnp.sum(act * act, axis=-1, keepdims=True) + epsilon)


def masks(rows):
    at_row = lax.broadcasted_iota(jnp.int32, (rows, rows), 0)
    at_col = lax.broadcasted_iota(jnp.int32, (rows, rows), 1)
    return at_row, at_col


def chain_lag(me, limit):
    return jnp.minimum(lax.div(3 * me + 4, 5), limit)


def mixer_kernel(
    n, rows, steps, pairs, limit,
    pq_ref, pk_ref, pv_ref, strength_ref, filt_ref, gain_ref, own_ref,
    normed_ref, mix_ref, carry_ref, inv_ref, kw_ref, state_ref, full_ref,
    x_ref, low_ref, sol_ref, end_ref, recv_ref, send_ref,
    send_sem, recv_sem, ring_send, ring_recv, local_sem,
):
    me = lax.axis_index("dp")
    step = pl.program_id(0)
    lag = chain_lag(me, limit)
    ring = RingGather(n, own_ref.shape[0], full_ref, ring_send, ring_recv, own_ref, local_sem)

    def hop(at, h):
        return remote(
            send_ref.at[at, h], recv_ref.at[at, h], send_sem.at[at, h], recv_sem.at[at, h],
            dp=lax.rem(me + 1, n),
        )

    @pl.when(step == 0)
    def _():
        barrier = pltpu.get_barrier_semaphore()
        ring.greet(barrier)

        @pl.when(me > 0)
        def _():
            pl.semaphore_signal(
                barrier, inc=1, device_id={"dp": lax.rem(me + n - 1, n)}, device_id_type=MESH
            )

        @pl.when(me == 0)
        def _():
            recv_ref[...] = jnp.zeros_like(recv_ref)

        @pl.when(me < n - 1)
        def _():
            pl.semaphore_wait(barrier, 3)

        @pl.when(me == n - 1)
        def _():
            pl.semaphore_wait(barrier, 2)

        ring.start()

    each = -(-(n - 2) // (steps - 1))

    @pl.when(step > 0)
    def _():
        for i in range(each):
            at = (step - 1) * each + i + 2

            @pl.when(at < n)
            def _():
                ring.advance(at, range(2) if each == 1 else None)

    @pl.when(step < steps)
    def _():
        pair = lax.rem(step, pairs)
        at_row, at_col = masks(HD)
        all_row, all_col = masks(rows)
        acts = []
        for column, ref in enumerate((pq_ref, pk_ref, pv_ref)):
            running, gate = conv_act(x_ref, ref[0], filt_ref, column, rows)
            acts.append(running * gate)
        strengths = strength_ref[0]
        lane = lax.broadcasted_iota(jnp.int32, strengths.shape, 1)
        heads = []
        for h in range(PAIR):
            cut = slice(h * HD, (h + 1) * HD)
            act_q, act_k = acts[0][:, cut], acts[1][:, cut]
            q = (act_q * unit_scale(act_q)).astype(bf16)
            k = (act_k * unit_scale(act_k)).astype(bf16)
            v = acts[2][:, cut].astype(bf16)
            beta = jnp.sum(jnp.where(lane == pair * PAIR + h, strengths, 0.0), axis=-1, keepdims=True)
            low = jnp.where(all_row > all_col, beta * dot(k, k, 1, 1), 0.0)
            low_ref[h] = low
            first = (at_row & 1 == 1) & (at_row - 1 == at_col)
            for b in range(2):
                block = low[b * HD : (b + 1) * HD, b * HD : (b + 1) * HD]
                sol_ref[h, b] = jnp.where(at_row == at_col, 1.0, 0.0) - jnp.where(first, block, 0.0)
            heads.append((q, k, v, beta))
        blocks = [(h, b) for h in range(PAIR) for b in range(2)]

        def refine(level, carry):
            band_row, band_col = at_row >> level, at_col >> level
            band = (band_row & 1 == 1) & (band_row - 1 == band_col)
            sols = [halves(sol_ref[h, b]) for h, b in blocks]
            mids = [
                halves(
                    square_product(
                        halves(
                            jnp.where(
                                band, low_ref[h, b * HD : (b + 1) * HD, b * HD : (b + 1) * HD], 0.0
                            )
                        ),
                        sol,
                    )
                )
                for (h, b), sol in zip(blocks, sols)
            ]
            for (h, b), sol, mid in zip(blocks, sols, mids):
                sol_ref[h, b] = sol_ref[h, b] - square_product(sol, mid)
            return carry

        lax.fori_loop(1, (HD - 1).bit_length(), refine, 0)

        wides = []
        for h in range(PAIR):
            q, k, v, beta = heads[h]
            top, low = halves(sol_ref[h, 0]), halves(sol_ref[h, 1])
            mid = halves(square_product(halves(low_ref[h, HD:, :HD]), top))
            corner = -square_product(low, mid)
            inv = jnp.concatenate(
                [
                    beside(sol_ref[h, 0], jnp.zeros((HD, HD), f32)),
                    beside(corner, sol_ref[h, 1]),
                ],
                axis=0,
            )
            inv_ref[h] = inv
            right = beside(beta * k.astype(f32), beta * v.astype(f32))
            wides.append(halves(full_product(halves(inv), halves(right))))
        for h in range(PAIR):
            q, k, v, beta = heads[h]
            scores = halves(jnp.where(all_row >= all_col, dot(q, k, 1, 1), 0.0))
            seen = full_product(scores, wides[h])
            carry_ref[step, h] = q.astype(f32) - seen[:, :HD]
            mix_ref[step, h] = seen[:, HD:]
            kwu = dot(k, wides[h][0], 0, 0) + dot(k, wides[h][1], 0, 0)
            kw_ref[step, h] = kwu[:, :HD]
            end_ref[step, h] = kwu[:, HD:]

    if each == 1:
        @pl.when((step > 0) & (step + 1 < n))
        def _():
            ring.advance(step + 1, range(2, 2 * SUBS))

    at = step - lag

    @pl.when((at >= 0) & (at < steps))
    def _():
        kws = [halves(kw_ref[at, h]) for h in range(PAIR)]
        for h in range(PAIR):
            @pl.when(me > 0)
            def _():
                hop(at, h).wait_recv()

            state = recv_ref[at, h]
            out_state = end_ref[at, h] + state.astype(f32) - short_product(kws[h], state)
            send_ref[at, h] = out_state.astype(bf16)

            @pl.when(me < n - 1)
            def _():
                hop(at, h).start()

        seq, pair = lax.div(at, pairs), lax.rem(at, pairs)
        for h in range(PAIR):
            state = recv_ref[at, h]
            state_ref[at, h] = state
            mix = mix_ref[at, h] + short_product(halves(carry_ref[at, h]), state)
            mix_ref[at, h] = mix
            scale = lax.rsqrt(jnp.mean(mix * mix, axis=-1, keepdims=True) + epsilon)
            lanes = pl.ds(pl.multiple_of((pair * PAIR + h) * HD, HD), HD)
            normed_ref[seq, :, lanes] = (mix * scale * gain_ref[...]).astype(bf16)

    @pl.when(step == steps + limit - 1)
    def _():
        ring.settle(1, n - 1)

        @pl.when(me < n - 1)
        def _():
            def done(at, carry):
                for h in range(PAIR):
                    hop(at, h).wait_send()
                return carry

            lax.fori_loop(0, steps, done, 0)


def mixer(projected, strength, filters, gain, weight):
    n = lax.axis_size("dp")
    seqs, extended, width = projected.shape
    rows = extended - RIM
    local = width // 3
    pairs = local // (PAIR * HD)
    wide = PAIR * HD
    steps = seqs * pairs
    limit = min((3 * (n - 1) + 4) // 5, steps)
    assert rows == 2 * HD
    vmem, anywhere = pl.BlockSpec(memory_space=pltpu.VMEM), pl.BlockSpec(memory_space=pl.ANY)

    def now(i):
        return jnp.minimum(i, steps - 1)

    def part(column):
        return pl.BlockSpec(
            (1, extended, wide),
            lambda i: (lax.div(now(i), pairs), 0, column * pairs + lax.rem(now(i), pairs)),
        )

    def whole(*shape):
        return pl.BlockSpec(shape, lambda i: (0,) * len(shape))

    total = steps * PAIR
    return pl.pallas_call(
        functools.partial(mixer_kernel, n, rows, steps, pairs, limit),
        grid=(steps + limit,),
        in_specs=[
            part(0), part(1), part(2),
            pl.BlockSpec((1, rows, strength.shape[2]), lambda i: (lax.div(now(i), pairs), 0, 0)),
            pl.BlockSpec((3 * KCONV, wide), lambda i: (0, lax.rem(now(i), pairs))),
            whole(1, HD),
            vmem,
        ],
        out_specs=[
            whole(seqs, rows, local),
            whole(steps, PAIR, rows, HD),
            whole(steps, PAIR, rows, HD),
            pl.BlockSpec((PAIR, rows, rows), lambda i: (now(i), 0, 0)),
            whole(steps, PAIR, HD, HD),
            whole(steps, PAIR, HD, HD),
            anywhere,
        ],
        out_shape=[
            jax.ShapeDtypeStruct((seqs, rows, local), bf16),
            jax.ShapeDtypeStruct((steps, PAIR, rows, HD), f32),
            jax.ShapeDtypeStruct((steps, PAIR, rows, HD), f32),
            jax.ShapeDtypeStruct((total, rows, rows), f32),
            jax.ShapeDtypeStruct((steps, PAIR, HD, HD), f32),
            jax.ShapeDtypeStruct((steps, PAIR, HD, HD), bf16),
            jax.ShapeDtypeStruct((n,) + weight.shape, bf16),
        ],
        scratch_shapes=[
            pltpu.VMEM((extended, wide), f32),
            pltpu.VMEM((PAIR, rows, rows), f32),
            pltpu.VMEM((PAIR, 2, HD, HD), f32),
            pltpu.VMEM((steps, PAIR, HD, HD), f32),
            pltpu.VMEM((steps, PAIR, HD, HD), bf16),
            pltpu.VMEM((steps, PAIR, HD, HD), bf16),
            pltpu.SemaphoreType.DMA((steps, PAIR)),
            pltpu.SemaphoreType.DMA((steps, PAIR)),
        ]
        + ring_semaphores(n)
        + [pltpu.SemaphoreType.DMA],
        compiler_params=pltpu.CompilerParams(
            collective_id=0, has_side_effects=True, vmem_limit_bytes=VMEM_LIMIT,
            dimension_semantics=("arbitrary",),
        ),
        name="mixer",
    )(projected, projected, projected, strength, filters, gain, weight)


def state_back_kernel(
    n, rows, steps, pairs,
    rows_ref, weight_ref, gain_ref, mix_ref, carry_ref, kw_ref,
    high_ref, low_ref, end_ref, head_ref,
    recv_ref, send_ref, send_sem, recv_sem,
):
    me = lax.axis_index("dp")
    step = pl.program_id(0)

    def hop(at, h):
        return remote(
            send_ref.at[at, h], recv_ref.at[at, h], send_sem.at[at, h], recv_sem.at[at, h],
            dp=lax.rem(me + n - 1, n),
        )

    @pl.when(step == 0)
    def _():
        barrier = pltpu.get_barrier_semaphore()

        @pl.when(me < n - 1)
        def _():
            pl.semaphore_signal(barrier, inc=1, device_id={"dp": lax.rem(me + 1, n)}, device_id_type=MESH)

        @pl.when(me == n - 1)
        def _():
            recv_ref[...] = jnp.zeros_like(recv_ref)

        @pl.when(me > 0)
        def _():
            pl.semaphore_wait(barrier, 1)

        head_ref[...] = jnp.zeros_like(head_ref)

    back_normed = dot(rows_ref[0], weight_ref[...])
    adds = []
    head_sum = jnp.zeros((1, HD), f32)
    for h in range(PAIR):
        mix, back = mix_ref[0, h], back_normed[:, h * HD : (h + 1) * HD]
        scale = lax.rsqrt(jnp.mean(mix * mix, axis=-1, keepdims=True) + epsilon)
        unit = mix * scale
        head_sum = head_sum + jnp.sum(back * unit, axis=0, keepdims=True)
        scaled = back * gain_ref[...]
        out = halves(scale * (scaled - unit * jnp.mean(scaled * unit, axis=-1, keepdims=True)))
        high_ref[0, h], low_ref[0, h] = out
        adds.append(narrow_product(halves(carry_ref[0, h]), out, 0))
    head_ref[...] += jnp.where(
        lax.broadcasted_iota(jnp.int32, head_ref.shape, 0) == 0, head_sum, 0.0
    )
    kws = [halves(kw_ref[0, h].T) for h in range(PAIR)]
    for h in range(PAIR):
        @pl.when(me < n - 1)
        def _():
            hop(step, h).wait_recv()

        end = recv_ref[step, h]
        before = adds[h] + end.astype(f32) - short_product(kws[h], end)
        send_ref[step, h] = before.astype(bf16)

        @pl.when(me > 0)
        def _():
            hop(step, h).start()

        end_ref[0, h] = end

    @pl.when((step == steps - 1) & (me > 0))
    def _():
        def done(at, carry):
            for h in range(PAIR):
                hop(at, h).wait_send()
            return carry

        lax.fori_loop(0, steps, done, 0)


def state_back(rows_back, out_weight, gain, mix, carry, kw):
    n = lax.axis_size("dp")
    seqs, rows, width = rows_back.shape
    steps = mix.shape[0]
    pairs = steps // seqs
    wide = PAIR * HD

    def tall(size):
        return pl.BlockSpec((1, PAIR, size, HD), lambda i: (i, 0, 0, 0))

    def shape(size):
        return jax.ShapeDtypeStruct((steps, PAIR, size, HD), bf16)

    return pl.pallas_call(
        functools.partial(state_back_kernel, n, rows, steps, pairs),
        grid=(steps,),
        in_specs=[
            pl.BlockSpec((1, rows, width), lambda i: (lax.div(i, pairs), 0, 0)),
            pl.BlockSpec((width, wide), lambda i: (0, lax.rem(i, pairs))),
            pl.BlockSpec((1, HD), lambda i: (0, 0)),
            tall(rows), tall(rows), tall(HD),
        ],
        out_specs=[tall(rows), tall(rows), tall(HD), pl.BlockSpec((8, HD), lambda i: (0, 0))],
        out_shape=[shape(rows), shape(rows), shape(HD), jax.ShapeDtypeStruct((8, HD), f32)],
        scratch_shapes=[
            pltpu.VMEM((steps, PAIR, HD, HD), bf16),
            pltpu.VMEM((steps, PAIR, HD, HD), bf16),
            pltpu.SemaphoreType.DMA((steps, PAIR)),
            pltpu.SemaphoreType.DMA((steps, PAIR)),
        ],
        compiler_params=pltpu.CompilerParams(
            collective_id=6, has_side_effects=True, vmem_limit_bytes=VMEM_LIMIT,
            dimension_semantics=("arbitrary",),
        ),
        name="state_back",
    )(rows_back, out_weight, gain, mix, carry, kw)


def mixer_back_kernel(
    n, tensor, rows, steps, pairs,
    pq_ref, pk_ref, pv_ref, strength_ref, filt_ref, high_ref, low_ref, inv_ref, end_ref, state_ref,
    second_ref, gate_ref, ffn_ref, down_ref, hidden_ref,
    proj_ref, logit_ref, conv_ref, total_ref, layer_ref,
    xq_ref, xk_ref, xv_ref, bc_ref, last_ref, rim_ref, next_ref, inward_ref, spare_ref, kept_ref,
    part_ref, near_ref, far_ref, pass_ref,
    rim_send, rim_recv, ring_send, ring_recv, a_send, a_recv, x_send, x_recv,
):
    me, t = lax.axis_index("dp"), lax.axis_index("tensor")
    step = pl.program_id(0)
    wide = PAIR * HD
    local = proj_ref.shape[2] // 3
    seqs = steps // pairs
    own_len = rows // tensor
    core, cross = swap_pair(t), swap_half(t, tensor)
    both = swap_half(core, tensor)
    count = total_ref.shape[0]
    ring = RingScatter(
        n, count, grad_part(count, second_ref, gate_ref, spare_ref), inward_ref, total_ref,
        ring_send, ring_recv,
    )

    def to_rim(seq):
        return remote(
            rim_ref.at[seq], next_ref.at[seq], rim_send.at[seq], rim_recv.at[seq],
            dp=lax.rem(me + n - 1, n),
        )

    def span(at):
        return pl.ds(pl.multiple_of(at * own_len, own_len), own_len)

    def to_core(s, i):
        return remote(
            part_ref.at[s, span((core, both)[i]), :], near_ref.at[s, i],
            a_send.at[s, i], a_recv.at[s, i], tensor=core,
        )

    def to_cross(s):
        return remote(pass_ref.at[s], far_ref.at[s], x_send.at[s], x_recv.at[s], tensor=cross)

    @pl.when(step == 0)
    def _():
        barrier = pltpu.get_barrier_semaphore()
        ring.greet(barrier)
        for device in (core, cross):
            pl.semaphore_signal(barrier, inc=1, device_id={"tensor": device}, device_id_type=MESH)

        @pl.when(me < n - 1)
        def _():
            pl.semaphore_signal(barrier, inc=1, device_id={"dp": lax.rem(me + 1, n)}, device_id_type=MESH)

        @pl.when(me == n - 1)
        def _():
            next_ref[...] = jnp.zeros_like(next_ref)

        @pl.when(me > 0)
        def _():
            pl.semaphore_wait(barrier, 5)

        @pl.when(me == 0)
        def _():
            pl.semaphore_wait(barrier, 4)

        ring.start()
        bc_ref[...] = jnp.zeros_like(bc_ref)
        conv_ref[...] = jnp.zeros_like(conv_ref)

    @pl.when(step < seqs)
    def _():
        here = pl.ds(pl.multiple_of(step * rows, rows), rows)
        part_ref[step] = dot(ffn_ref[here, :], down_ref[...], 1, 1).astype(bf16)
        for i in (1, 0):
            to_core(step, i).start()

    @pl.when(step >= steps - seqs)
    def _():
        s = step - (steps - seqs)
        to_core(s, 1).wait_recv()
        pass_ref[s] = (
            part_ref[s, span(cross), :].astype(f32) + near_ref[s, 1].astype(f32)
        ).astype(bf16)
        to_cross(s).start()

    each = -(-(n - 2) // (steps - 1))

    @pl.when(step > 0)
    def _():
        for i in range(each):
            at = (step - 1) * each + i + 2

            @pl.when(at < n)
            def _():
                if each == 1:
                    ring.advance_first(at, kept_ref)
                else:
                    ring.advance(at)

    seq, pair = lax.div(step, pairs), lax.rem(step, pairs)

    @pl.when(pair == 0)
    def _():
        logit_ref[...] = jnp.zeros_like(logit_ref)

    at_row, at_col = masks(rows)
    strengths = strength_ref[0]
    lane = lax.broadcasted_iota(jnp.int32, strengths.shape, 1)
    run_q, gate_q = conv_act(xq_ref, pq_ref[0], filt_ref, 0, rows)
    run_k, gate_k = conv_act(xk_ref, pk_ref[0], filt_ref, 1, rows)
    run_v, gate_v = conv_act(xv_ref, pv_ref[0], filt_ref, 2, rows)
    act_q, act_k, act_v = run_q * gate_q, run_k * gate_k, run_v * gate_v
    back_acts = ([], [], [])
    for h in range(PAIR):
        cut = slice(h * HD, (h + 1) * HD)
        scale_q, scale_k = unit_scale(act_q[:, cut]), unit_scale(act_k[:, cut])
        unit_q, unit_k = act_q[:, cut] * scale_q, act_k[:, cut] * scale_k
        q, k, v = unit_q.astype(bf16), unit_k.astype(bf16), act_v[:, cut].astype(bf16)
        chosen = lane == pair * PAIR + h
        beta = jnp.sum(jnp.where(chosen, strengths, 0.0), axis=-1, keepdims=True)
        gram = dot(k, k, 1, 1)
        scores = halves(jnp.where(at_row >= at_col, dot(q, k, 1, 1), 0.0))
        state, end = state_ref[0, h], end_ref[0, h]
        out = (high_ref[0, h], low_ref[0, h])
        inv = halves(inv_ref[h])
        through = dot(k, beside(state, end))
        rest = v.astype(f32) - through[:, :HD]
        update = halves(narrow_product(inv, halves(beta * rest)))
        back_update = halves(narrow_product(scores, out, 0) + through[:, HD:])
        back_scores = short_product_t(out, update[0]) + dot(out[0], update[1], 1, 1)
        back_scores = halves(jnp.where(at_row >= at_col, back_scores, 0.0))
        solved = narrow_product(inv, back_update, 0)
        terms = halves(solved)
        back_low = short_product_t(terms, update[0]) + dot(terms[0], update[1], 1, 1)
        back_low = jnp.where(at_row > at_col, -back_low, 0.0)
        back_beta = jnp.sum(back_low * gram, axis=-1, keepdims=True) + jnp.sum(
            solved * rest, axis=-1, keepdims=True
        )
        back_gram = beta * back_low
        back_gram = halves(back_gram + back_gram.T)
        back_value = beta * solved
        back_q = short_product_t(out, state) + dot(back_scores[0], k) + dot(back_scores[1], k)
        back_k = (
            dot(back_scores[0], q, 0, 0)
            + dot(back_scores[1], q, 0, 0)
            + short_product_t(update, end)
            + dot(back_gram[0], k)
            + dot(back_gram[1], k)
            - short_product_t(halves(back_value), state)
        )
        logit_ref[0] += jnp.where(chosen, back_beta * beta * (1.0 - beta), 0.0)
        back_acts[0].append(
            (back_q - unit_q * jnp.sum(unit_q * back_q, axis=-1, keepdims=True)) * scale_q
        )
        back_acts[1].append(
            (back_k - unit_k * jnp.sum(unit_k * back_k, axis=-1, keepdims=True)) * scale_k
        )
        back_acts[2].append(back_value)

    if each == 1:
        @pl.when((step > 0) & (step + 1 < n))
        def _():
            ring.advance_second(step + 1, kept_ref)

    for column, (running, gate, x_ref) in enumerate(
        ((run_q, gate_q, xq_ref), (run_k, gate_k, xk_ref), (run_v, gate_v, xv_ref))
    ):
        back_conv = beside(*back_acts[column]) * gate * (1.0 + running * (1.0 - gate))
        bc_ref[pl.ds(RIM, rows), :] = back_conv
        back_x, back_rim = None, None
        for tap in range(KCONV):
            weight = filt_ref[pl.ds(column * KCONV + tap, 1), :]
            term = weight * bc_ref[pl.ds(RIM + KCONV - 1 - tap, rows), :]
            edge = weight * bc_ref[pl.ds(KCONV - 1 - tap, RIM), :]
            back_x = term if back_x is None else back_x + term
            back_rim = edge if back_rim is None else back_rim + edge
            grad = jnp.sum(
                back_conv * x_ref[pl.ds(RIM - KCONV + 1 + tap, rows), :], axis=0, keepdims=True
            )
            conv_ref[pair, pl.ds(column * KCONV + tap, 1), :] += grad
        lanes = pl.ds(pl.multiple_of(column * local + pair * wide, wide), wide)
        proj_ref[seq, :, lanes] = back_x.astype(bf16)
        last_ref[seq, :, lanes] = back_x[rows - RIM :, :]
        rim_ref[seq, :, lanes] = back_rim.astype(bf16)


    @pl.when((pair == pairs - 1) & (me > 0))
    def _():
        to_rim(seq).start()

    @pl.when(step == steps - 1)
    def _():
        @pl.when(me > 0)
        def _():
            for seq in range(seqs):
                to_rim(seq).wait_send()

        @pl.when(me < n - 1)
        def _():
            for seq in range(seqs):
                to_rim(seq).wait_recv()

        for seq in range(seqs):
            edge = last_ref[seq] + next_ref[seq].astype(f32)
            proj_ref[seq, pl.ds(rows - RIM, RIM), :] = edge.astype(bf16)

        def close(s, carry):
            to_core(s, 0).wait_recv()
            to_cross(s).wait_recv()
            total = (
                part_ref[s, span(t), :].astype(f32) + near_ref[s, 0].astype(f32) + far_ref[s].astype(f32)
            )
            layer_ref[s] = (hidden_ref[s] + total).astype(bf16)
            for i in range(2):
                to_core(s, i).wait_send()
            to_cross(s).wait_send()
            return carry

        lax.fori_loop(0, seqs, close, 0)
        ring.finish()


def mixer_back(projected, strength, filters, out_terms, inverse, end, state, gate_factors, ffn_factors, hidden):
    n, tensor = lax.axis_size("dp"), lax.axis_size("tensor")
    seqs, extended, width = projected.shape
    rows = extended - RIM
    local = width // 3
    pairs = local // (PAIR * HD)
    wide = PAIR * HD
    steps = seqs * pairs
    vmem = pl.BlockSpec(memory_space=pltpu.VMEM)

    def part(column):
        return pl.BlockSpec(
            (1, extended, wide), lambda i: (lax.div(i, pairs), 0, column * pairs + lax.rem(i, pairs))
        )

    def tall(size):
        return pl.BlockSpec((1, PAIR, size, HD), lambda i: (i, 0, 0, 0))

    def seq(size, span):
        return pl.BlockSpec((1, size, span), lambda i: (lax.div(i, pairs), 0, 0))

    heads = strength.shape[2]
    own_len, model = hidden.shape[1:]
    count, columns = gate_factors[0].shape[1] // n, gate_factors[1].shape[1]
    return pl.pallas_call(
        functools.partial(mixer_back_kernel, n, tensor, rows, steps, pairs),
        grid=(steps,),
        in_specs=[
            part(0), part(1), part(2),
            seq(rows, heads),
            pl.BlockSpec((3 * KCONV, wide), lambda i: (0, lax.rem(i, pairs))),
            tall(rows), tall(rows),
            pl.BlockSpec((PAIR, rows, rows), lambda i: (i, 0, 0)),
            tall(HD), tall(HD),
        ]
        + [vmem] * 5,
        out_specs=[
            pl.BlockSpec((seqs, rows, width), lambda i: (0, 0, 0)),
            seq(rows, heads),
            pl.BlockSpec((pairs, 3 * KCONV, wide), lambda i: (0, 0, 0)),
            vmem, vmem,
        ],
        out_shape=[
            jax.ShapeDtypeStruct((seqs, rows, width), bf16),
            jax.ShapeDtypeStruct((seqs, rows, heads), f32),
            jax.ShapeDtypeStruct((pairs, 3 * KCONV, wide), f32),
            jax.ShapeDtypeStruct((count, columns), f32),
            jax.ShapeDtypeStruct((seqs, own_len, model), bf16),
        ],
        scratch_shapes=[
            pltpu.VMEM((extended, wide), f32),
            pltpu.VMEM((extended, wide), f32),
            pltpu.VMEM((extended, wide), f32),
            pltpu.VMEM((rows + 2 * RIM, wide), f32),
            pltpu.VMEM((seqs, RIM, width), f32),
            pltpu.VMEM((seqs, RIM, width), bf16),
            pltpu.VMEM((seqs, RIM, width), bf16),
            pltpu.VMEM((n, count, columns), bf16),
            spare(count, columns),
            pltpu.VMEM((2, count // (2 * SUBS), columns), f32),
            pltpu.VMEM((seqs, rows, model), bf16),
            pltpu.VMEM((seqs, 2, own_len, model), bf16),
            pltpu.VMEM((seqs, own_len, model), bf16),
            pltpu.VMEM((seqs, own_len, model), bf16),
            pltpu.SemaphoreType.DMA((seqs,)),
            pltpu.SemaphoreType.DMA((seqs,)),
        ]
        + ring_semaphores(n)
        + [
            pltpu.SemaphoreType.DMA((seqs, 2)),
            pltpu.SemaphoreType.DMA((seqs, 2)),
            pltpu.SemaphoreType.DMA((seqs,)),
            pltpu.SemaphoreType.DMA((seqs,)),
        ],
        compiler_params=pltpu.CompilerParams(
            collective_id=1, has_side_effects=True, vmem_limit_bytes=VMEM_LIMIT,
            dimension_semantics=("arbitrary",),
        ),
        name="mixer_back",
    )(
        projected, projected, projected, strength, filters, *out_terms, inverse, end, state,
        *gate_factors, *ffn_factors, hidden,
    )


def opening_kernel(
    n, tensor,
    q_ref, k_ref, v_ref, small_ref, tokens_ref, cot_ref, out_ref,
    qkv_ref, small_out, ext_ref, cot_out, full_out,
    zero_ref, local_sem, ring_send, ring_recv, side_send, side_recv, rim_send, rim_recv,
):
    me, t = lax.axis_index("dp"), lax.axis_index("tensor")
    place = ring_place(me, n)
    near = (ring_walk(lax.rem(place + 1, n), n), ring_walk(lax.rem(place + n - 1, n), n))
    core, cross = swap_pair(t), swap_half(t, tensor)
    rows, local = q_ref.shape
    own_len = tokens_ref.shape[1]
    slab = rows // (2 * SUBS)

    barrier = pltpu.get_barrier_semaphore()
    for device in ({"dp": near[0]}, {"dp": near[1]}, {"tensor": core}, {"tensor": cross}):
        pl.semaphore_signal(barrier, inc=1, device_id=device, device_id_type=MESH)

    @pl.when(me > 0)
    def _():
        pl.semaphore_signal(
            barrier, inc=1, device_id={"dp": lax.rem(me + n - 1, n), "tensor": tensor - 1},
            device_id_type=MESH,
        )

    def chunk(ref, at, offset):
        return ref.at[:, pl.ds(pl.multiple_of(offset + at * own_len, 8), own_len), :]

    mine = [
        pltpu.make_async_copy(ref, qkv_ref.at[me, :, pl.ds(c * local, local)], local_sem.at[c])
        for c, ref in enumerate((q_ref, k_ref, v_ref))
    ] + [
        pltpu.make_async_copy(small_ref, small_out.at[me], local_sem.at[3]),
        pltpu.make_async_copy(tokens_ref, chunk(ext_ref, t, RIM), local_sem.at[4]),
        pltpu.make_async_copy(cot_ref, chunk(cot_out, t, 0), local_sem.at[5]),
        pltpu.make_async_copy(out_ref, full_out.at[me], local_sem.at[7]),
    ]
    for copy in mine:
        copy.start()

    @pl.when(me == 0)
    def _():
        zero_ref[...] = jnp.zeros_like(zero_ref)
        blank = pltpu.make_async_copy(zero_ref, ext_ref.at[:, pl.ds(0, RIM), :], local_sem.at[6])
        blank.start()
        blank.wait()

    sends_rim = (me < n - 1) & (t == tensor - 1)

    @pl.when(sends_rim)
    def _():
        pl.semaphore_wait(barrier, 4 + tensor)

    @pl.when(jnp.logical_not(sends_rim))
    def _():
        pl.semaphore_wait(barrier, 4)

    def to_rim(peer):
        return remote(
            tokens_ref.at[:, pl.ds(own_len - RIM, RIM), :], ext_ref.at[:, pl.ds(0, RIM), :],
            rim_send.at[peer], rim_recv, dp=lax.rem(me + 1, n), tensor=peer,
        )

    sides = []
    for i, (own, full, offset) in enumerate(((tokens_ref, ext_ref, RIM), (cot_ref, cot_out, 0))):
        to_core = remote(own, chunk(full, t, offset), side_send.at[i, 0], side_recv.at[i, 0], tensor=core)
        to_cross = remote(own, chunk(full, t, offset), side_send.at[i, 1], side_recv.at[i, 1], tensor=cross)
        onward = remote(
            chunk(full, cross, offset), chunk(full, cross, offset),
            side_send.at[i, 2], side_recv.at[i, 2], tensor=core,
        )
        sides.append((to_core, to_cross, onward))
        to_core.start()
        to_cross.start()

    for copy in mine:
        copy.wait()

    @pl.when(sends_rim)
    def _():
        for peer in range(tensor):
            to_rim(peer).start()

    def ring(hop, lane):
        if lane == 2 * SUBS:
            owner = ring_walk(lax.rem(place + n - hop + 1, n), n)
            return remote(
                small_out.at[owner], small_out.at[owner],
                ring_send.at[hop, lane], ring_recv.at[hop, lane], dp=near[0],
            )
        way = lane % 2 if lane < 2 * SUBS else lane - 2 * SUBS - 1
        owner = ring_walk(lax.rem(place + n + (2 * way - 1) * (hop - 1), n), n)
        if lane > 2 * SUBS:
            piece = full_out.at[owner, pl.ds(way * (rows // 2), rows // 2), :]
            return remote(piece, piece, ring_send.at[hop, lane], ring_recv.at[hop, lane], dp=near[way])
        piece = qkv_ref.at[owner, pl.ds(lane * slab, slab), :]
        return remote(piece, piece, ring_send.at[hop, lane], ring_recv.at[hop, lane], dp=near[way])

    lanes = range(2 * SUBS + 3)

    def advance(hop, carry):
        for lane in lanes:
            @pl.when(hop > 1)
            def _():
                ring(hop - 1, lane).wait_recv()

            ring(hop, lane).start()
        for i, at in ((0, n // 2), (1, n - 1)):
            @pl.when(hop == at)
            def _():
                sides[i][1].wait_recv()
                sides[i][2].start()

        return carry

    lax.fori_loop(1, n, advance, 0)
    for lane in lanes:
        ring(n - 1, lane).wait_recv()

    def drain(hop, carry):
        for lane in lanes:
            ring(hop, lane).wait_send()
        return carry

    lax.fori_loop(1, n, drain, 0)
    for to_core, to_cross, onward in sides:
        to_core.wait()
        to_cross.wait_send()
        onward.wait()

    @pl.when(sends_rim)
    def _():
        for peer in range(tensor):
            to_rim(peer).wait_send()

    @pl.when(me > 0)
    def _():
        to_rim(0).wait_recv()


def opening(query_weight, key_weight, value_weight, small, tokens, cotangent, out_rows):
    n, tensor = lax.axis_size("dp"), lax.axis_size("tensor")
    rows, local = query_weight.shape
    seqs, own_len, width = tokens.shape
    vmem, anywhere = pl.BlockSpec(memory_space=pltpu.VMEM), pl.BlockSpec(memory_space=pl.ANY)
    lanes = 2 * SUBS + 3
    return pl.pallas_call(
        functools.partial(opening_kernel, n, tensor),
        in_specs=[vmem] * 7,
        out_specs=[anywhere] * 5,
        out_shape=[
            jax.ShapeDtypeStruct((n, rows, 3 * local), bf16),
            jax.ShapeDtypeStruct((n,) + small.shape, bf16),
            jax.ShapeDtypeStruct((seqs, RIM + tensor * own_len, width), bf16),
            jax.ShapeDtypeStruct((seqs, tensor * own_len, width), bf16),
            jax.ShapeDtypeStruct((n,) + out_rows.shape, bf16),
        ],
        scratch_shapes=[
            pltpu.VMEM((seqs, RIM, width), bf16),
            pltpu.SemaphoreType.DMA((8,)),
            pltpu.SemaphoreType.DMA((n, lanes)),
            pltpu.SemaphoreType.DMA((n, lanes)),
            pltpu.SemaphoreType.DMA((2, 3)),
            pltpu.SemaphoreType.DMA((2, 3)),
            pltpu.SemaphoreType.DMA((tensor,)),
            pltpu.SemaphoreType.DMA,
        ],
        compiler_params=pltpu.CompilerParams(
            collective_id=2, has_side_effects=True, vmem_limit_bytes=VMEM_LIMIT
        ),
        name="opening",
    )(query_weight, key_weight, value_weight, small, tokens, cotangent, out_rows)


def fold_kernel(
    n, n_seqs, tensor, backward, count, terms,
    own_ref, gain_ref, hidden_ref, *refs,
):
    t = lax.axis_index("tensor")
    core, cross = swap_pair(t), swap_half(t, tensor)
    both = swap_half(core, tensor)
    own_len = own_ref.shape[1]
    refs = list(refs)
    term_hbm, refs = refs[:terms], refs[terms:]
    pieces, refs = refs[:count], refs[count:]
    outs = 1 if backward else count - 1
    (rows_ref, keep_ref, sum_ref), made, refs = refs[:3], refs[3 : 3 + outs], refs[3 + outs :]
    if not backward:
        (gate_full, *pieces), (gate_out, up_out), refs = pieces, refs[:2], refs[2:]
        count -= 1
    held, part_ref, load_sem, refs = refs[:terms], refs[terms], refs[terms + 1], refs[terms + 2 :]
    (
        near_ref, far_ref, send_ref, own_sum_ref, a_send, a_recv, x_send, x_recv, g_send, g_recv,
        ring_send, ring_recv,
    ) = refs[:12]
    ring_refs = refs[12:]
    if backward:
        factors, ring_refs = ring_refs[2:], ring_refs[:2]
        loads = [
            pltpu.make_async_copy(source, target, load_sem.at[terms + i])
            for i, (source, target) in enumerate(zip(pieces, factors))
        ]
        pieces = factors
    else:
        loads = []
    ahead = len(loads)
    loads += [
        pltpu.make_async_copy(source, target, load_sem.at[i])
        for i, (source, target) in enumerate(zip(term_hbm, held))
    ]
    for load in loads:
        load.start()
    if backward:
        rings = [
            RingScatter(
                n, made[0].shape[0], grad_part(made[0].shape[0], *pieces, ring_refs[1]), ring_refs[0],
                made[0], ring_send.at[0], ring_recv.at[0],
            )
        ]
    else:
        rings = [
            RingGather(
                n, pieces[i].shape[0], made[i], ring_send.at[i], ring_recv.at[i], pieces[i], ring_refs[i]
            )
            for i in range(count)
        ]

    def advance(hop):
        if hop < n:
            rings[0].advance(hop)

    barrier = pltpu.get_barrier_semaphore()
    rings[0].greet(barrier)
    for device in (core, cross):
        pl.semaphore_signal(barrier, inc=1, device_id={"tensor": device}, device_id_type=MESH)
    pl.semaphore_wait(barrier, 4)

    def span(at):
        return pl.ds(pl.multiple_of(at * own_len, own_len), own_len)

    def to_core(s, i):
        return remote(
            part_ref.at[s, span((core, both)[i]), :], near_ref.at[s, i],
            a_send.at[s, i], a_recv.at[s, i], tensor=core,
        )

    def to_cross(s):
        return remote(send_ref.at[s], far_ref.at[s], x_send.at[s], x_recv.at[s], tensor=cross)

    def gather(s, i):
        if i == 2:
            piece, peer = rows_ref.at[s, span(cross), :], core
        else:
            piece, peer = rows_ref.at[s, span(t), :], (cross, core)[i]
        return remote(piece, piece, g_send.at[s, i], g_recv.at[s, i], tensor=peer)

    for load in loads[:ahead]:
        load.wait()
    rings[0].start()
    for load in loads[ahead:]:
        load.wait()
    if not backward:
        gate_ref, up_ref, stage_ref, hold_sem, out_sem = ring_refs[2:]
        load_gate = pltpu.make_async_copy(gate_full, gate_ref, hold_sem.at[0])
        load_up = pltpu.make_async_copy(made[0], up_ref, hold_sem.at[1])
        load_gate.start()

    def first(s, carry):
        to_core(s, 1).wait_recv()
        send_ref[s] = (
            part_ref[s, span(cross), :].astype(f32) + near_ref[s, 1].astype(f32)
        ).astype(bf16)
        to_cross(s).start()
        to_core(s, 0).wait_recv()
        own_sum_ref[s] = part_ref[s, span(t), :].astype(f32) + near_ref[s, 0].astype(f32)
        return carry

    length = own_len * tensor

    def zeroth(s, carry):
        here = pl.ds(pl.multiple_of(s * length, length), length)
        part = dot(held[0][here, :], held[1][...], 1, 1)
        for i in range(2, terms, 2):
            part = part + dot(held[i][here, :], held[i + 1][...], 1, 1)
        part_ref[s] = part.astype(bf16)
        for i in (1, 0):
            to_core(s, i).start()

        @pl.when(s > 0)
        def _():
            first(s - 1, 0)

        for i, at in enumerate(moments[0]):
            @pl.when(s == at)
            def _():
                advance(2 + i)

        return carry

    moments = ((1, 3), (0, 2, 3), (1,)) if backward else ((), (0, 1, 2, 3), (1,))
    done = [2, 2 + len(moments[0]), 2 + len(moments[0]) + len(moments[1])]
    lax.fori_loop(0, n_seqs, zeroth, 0)
    first(n_seqs - 1, 0)
    sum_ref[...] = jnp.zeros_like(sum_ref)

    def second(s, carry):
        to_cross(s).wait_recv()
        total = own_sum_ref[s] + far_ref[s].astype(f32)
        gain = gain_ref[...]
        own = own_ref[s].astype(f32)
        if backward:
            hidden = hidden_ref[s]
            scale = lax.rsqrt(jnp.mean(hidden * hidden, axis=-1, keepdims=True) + epsilon)
            unit = hidden * scale
            sum_ref[...] += jnp.sum(total * unit, axis=0, keepdims=True)
            scaled = total * gain
            kept = own + scale * (scaled - unit * jnp.mean(scaled * unit, axis=-1, keepdims=True))
            keep_ref[s] = kept
            rows_ref[s, span(t), :] = kept.astype(bf16)
        else:
            kept = own + total
            keep_ref[s] = kept
            scale = lax.rsqrt(jnp.mean(kept * kept, axis=-1, keepdims=True) + epsilon)
            rows_ref[s, span(t), :] = (kept * scale * gain).astype(bf16)
        gather(s, 0).start()
        gather(s, 1).start()

        for i, at in enumerate(moments[1]):
            @pl.when(s == at)
            def _():
                advance(done[1] + i)

        return carry

    lax.fori_loop(0, n_seqs, second, 0)

    def third(s, carry):
        gather(s, 0).wait_recv()
        gather(s, 2).start()

        @pl.when(s == moments[2][0])
        def _():
            advance(done[2])

        return carry

    lax.fori_loop(0, n_seqs, third, 0)

    def rest(hop, carry):
        rings[0].advance(hop)
        return carry

    lax.fori_loop(done[2] + 1, n, rest, 0)
    if backward:
        rings[0].finish()
    else:
        def others(s, carry):
            gather(s, 1).wait_recv()
            gather(s, 2).wait_recv()
            return carry

        lax.fori_loop(0, n_seqs, others, 0)
        rings[1].start()

        def store(which, s):
            return pltpu.make_async_copy(
                stage_ref.at[which, s], (gate_out, up_out)[which].at[s], out_sem.at[which, s]
            )

        def product(which, weight_ref, begin):
            def one(s, carry):
                value = dot(rows_ref[s], weight_ref[...].reshape(-1, weight_ref.shape[2]))
                stage_ref[which, s] = value
                store(which, s).start()

                @pl.when(begin + s < n)
                def _():
                    rings[1].advance(begin + s)

                return carry

            lax.fori_loop(0, n_seqs, one, 0)

        load_gate.wait()
        product(0, gate_ref, 2)
        rings[0].settle(1, n - 1)
        load_up.start()
        load_up.wait()
        product(1, up_ref, 2 + n_seqs)

        def remaining(hop, carry):
            rings[1].advance(hop)
            return carry

        lax.fori_loop(2 + 2 * n_seqs, n, remaining, 0)
        rings[1].settle(1, n - 1)

        def stored(s, carry):
            for which in range(2):
                store(which, s).wait()
            return carry

        lax.fori_loop(0, n_seqs, stored, 0)

    def last(s, carry):
        if backward:
            gather(s, 1).wait_recv()
            gather(s, 2).wait_recv()
        for i in range(2):
            to_core(s, i).wait_send()
        to_cross(s).wait_send()
        for i in range(3):
            gather(s, i).wait_send()
        return carry

    lax.fori_loop(0, n_seqs, last, 0)


def fold(terms, own, gain, pieces, hidden=None):
    n, tensor = lax.axis_size("dp"), lax.axis_size("tensor")
    seqs, own_len, width = own.shape
    backward, count = hidden is not None, len(pieces)
    vmem, anywhere = pl.BlockSpec(memory_space=pltpu.VMEM), pl.BlockSpec(memory_space=pl.ANY)
    if backward:
        rows, columns = pieces[0].shape[1] // n, pieces[1].shape[1]
        made = [jax.ShapeDtypeStruct((rows, columns), f32)]
        ring_scratch = [pltpu.VMEM((n, rows, columns), bf16), spare(rows, columns)]
        ring_scratch += [pltpu.VMEM(piece.shape, bf16) for piece in pieces]
        piece_specs = [anywhere] * count
    else:
        hidden = jnp.zeros((8, 128), f32)
        made = [jax.ShapeDtypeStruct((n,) + piece.shape, bf16) for piece in pieces[1:]]
        columns = pieces[0].shape[2]
        made += [jax.ShapeDtypeStruct((seqs, tensor * own_len, columns), f32)] * 2
        ring_scratch = [pltpu.SemaphoreType.DMA for _ in pieces[1:]] + [
            pltpu.VMEM(pieces[0].shape, bf16),
            pltpu.VMEM(pieces[0].shape, bf16),
            pltpu.VMEM((2, seqs, tensor * own_len, columns), f32),
            pltpu.SemaphoreType.DMA((2,)),
            pltpu.SemaphoreType.DMA((2, seqs)),
        ]
        piece_specs = [anywhere] + [vmem] * (count - 1)
    return pl.pallas_call(
        functools.partial(fold_kernel, n, seqs, tensor, backward, count, len(terms)),
        in_specs=[vmem] * 3 + [anywhere] * len(terms) + piece_specs,
        out_specs=[vmem] * 3 + [vmem if backward else anywhere] * len(made),
        out_shape=[
            jax.ShapeDtypeStruct((seqs, tensor * own_len, width), bf16),
            jax.ShapeDtypeStruct((seqs, own_len, width), f32),
            jax.ShapeDtypeStruct((1, width), f32),
        ]
        + made,
        scratch_shapes=[pltpu.VMEM(term.shape, bf16) for term in terms]
        + [
            pltpu.VMEM((seqs, own_len * tensor, width), bf16),
            pltpu.SemaphoreType.DMA((len(terms) + count,)),
            pltpu.VMEM((seqs, 2, own_len, width), bf16),
            pltpu.VMEM((seqs, own_len, width), bf16),
            pltpu.VMEM((seqs, own_len, width), bf16),
            pltpu.VMEM((seqs, own_len, width), f32),
            pltpu.SemaphoreType.DMA((seqs, 2)),
            pltpu.SemaphoreType.DMA((seqs, 2)),
            pltpu.SemaphoreType.DMA((seqs,)),
            pltpu.SemaphoreType.DMA((seqs,)),
            pltpu.SemaphoreType.DMA((seqs, 3)),
            pltpu.SemaphoreType.DMA((seqs, 3)),
            pltpu.SemaphoreType.DMA((count, n, 2 * SUBS)),
            pltpu.SemaphoreType.DMA((count, n, 2 * SUBS)),
        ]
        + ring_scratch,
        compiler_params=pltpu.CompilerParams(
            collective_id=4 if backward else 3, has_side_effects=True, vmem_limit_bytes=VMEM_LIMIT
        ),
        name="fold_back" if backward else "fold",
    )(own, gain, hidden, *terms, *pieces)


def closing_kernel(
    n, n_seqs, tensor,
    own_ref, tokens_ref, gain_ref, small_ref, *refs,
):
    hbm, refs = refs[:9], refs[9:]
    d_ref, up_sum, out_sum, qkv_sum, small_sum, gain_sum, shared_ref = refs[:7]
    refs = refs[7:]
    held, refs = refs[:9], refs[9:]
    (
        up_in, out_in, qkv_in, small_in, gain_in, spare_up, spare_out, spare_qkv,
        part_ref, near_ref, far_ref, send_ref, total_ref, pass_ref, got_ref,
        load_sem, a_send, a_recv, x_send, x_recv, ring_send, ring_recv, s_send, s_recv,
    ) = refs
    second_ref, up_ref, back_ref, mix_ref, proj_ref, weight_ref, logit_ref, beta_ref, first_ref = held
    me, t = lax.axis_index("dp"), lax.axis_index("tensor")
    core, cross = swap_pair(t), swap_half(t, tensor)
    both = swap_half(core, tensor)
    own_len = tokens_ref.shape[1]
    length = own_len * tensor
    rows, width = up_sum.shape[0], gain_ref.shape[1]
    block = gain_sum.shape[1]

    loads = [
        pltpu.make_async_copy(source, target, load_sem.at[i])
        for i, (source, target) in enumerate(zip(hbm[:8], held))
    ] + [
        pltpu.make_async_copy(
            hbm[8].at[s, pl.ds(RIM, length), :], first_ref.at[pl.ds(s * length, length), :],
            load_sem.at[8 + s],
        )
        for s in range(n_seqs)
    ]
    for load in loads:
        load.start()

    def gain_part(owner, way):
        at = lax.div(owner * (width // n), block) * block
        return total_ref[pl.ds(way * 16, 16), pl.ds(pl.multiple_of(at, 128), block)]

    def ring(i, count, part, inward, total, lanes=2 * SUBS):
        return RingScatter(n, count, part, inward, total, ring_send.at[i], ring_recv.at[i], lanes)

    up = ring(0, rows, grad_part(rows, second_ref, up_ref, spare_up), up_in, up_sum)
    out = ring(1, rows, grad_part(rows, back_ref, mix_ref, spare_out), out_in, out_sum)
    qkv = ring(2, rows, grad_part(rows, first_ref, proj_ref, spare_qkv), qkv_in, qkv_sum)
    small = ring(3, small_ref.shape[1], held_part(small_ref), small_in, small_sum, 2)
    gains = ring(4, 32, gain_part, gain_in, gain_sum, 2)

    barrier = pltpu.get_barrier_semaphore()
    up.greet(barrier)
    for device in (core, cross):
        pl.semaphore_signal(barrier, inc=1, device_id={"tensor": device}, device_id_type=MESH)
    pl.semaphore_wait(barrier, 4)

    def span(at):
        return pl.ds(pl.multiple_of(at * own_len, own_len), own_len)

    def to_core(s, i):
        return remote(
            part_ref.at[s, span((core, both)[i]), :], near_ref.at[s, i],
            a_send.at[s, i], a_recv.at[s, i], tensor=core,
        )

    def to_cross(s):
        return remote(send_ref.at[s], far_ref.at[s], x_send.at[s], x_recv.at[s], tensor=cross)

    early = (up, out, small)
    for load in loads[:4]:
        load.wait()
    for chain in early:
        chain.start()
    for load in loads[4:]:
        load.wait()

    def input_grad(s, carry):
        here = pl.ds(pl.multiple_of(s * length, length), length)
        part_ref[s] = (
            dot(proj_ref[here, :], weight_ref[...], 1, 1) + dot(logit_ref[here, :], beta_ref[...], 1, 1)
        ).astype(bf16)
        for i in (1, 0):
            to_core(s, i).start()
        for chain in early:
            chain.advance(2 + s)
        return carry

    lax.fori_loop(0, n_seqs, input_grad, 0)

    def first(s, carry):
        to_core(s, 1).wait_recv()
        send_ref[s] = (
            part_ref[s, span(cross), :].astype(f32) + near_ref[s, 1].astype(f32)
        ).astype(bf16)
        to_cross(s).start()
        return carry

    lax.fori_loop(0, n_seqs, first, 0)
    for chain in early:
        chain.advance(2 + n_seqs)
    total_ref[...] = jnp.zeros_like(total_ref)

    def second(s, carry):
        to_core(s, 0).wait_recv()
        to_cross(s).wait_recv()
        total = (
            part_ref[s, span(t), :].astype(f32) + near_ref[s, 0].astype(f32) + far_ref[s].astype(f32)
        )
        tokens = tokens_ref[s].astype(f32)
        scale = lax.rsqrt(jnp.mean(tokens * tokens, axis=-1, keepdims=True) + epsilon)
        unit = tokens * scale
        total_ref[...] += jnp.sum(total * unit, axis=0, keepdims=True)
        scaled = total * gain_ref[...]
        d_ref[s] = (
            own_ref[s] + scale * (scaled - unit * jnp.mean(scaled * unit, axis=-1, keepdims=True))
        ).astype(bf16)
        return carry

    lax.fori_loop(0, n_seqs, second, 0)

    def rest(hop, carry):
        for chain in early:
            chain.advance(hop)
        return carry

    lax.fori_loop(3 + n_seqs, n, rest, 0)
    qkv.start()
    gains.start()
    for chain in early:
        chain.finish()

    def final(hop, carry):
        for chain in (qkv, gains):
            chain.advance(hop)
        return carry

    lax.fori_loop(2, n, final, 0)
    gains.finish()
    shared_ref[0, :, :] = small_sum[...]
    shared_ref[1, :, :] = jnp.zeros_like(small_sum)
    for c in range(block // 128):
        shared_ref[1, pl.ds(c, 1), :] = gain_sum[pl.ds(0, 1), c * 128 : (c + 1) * 128]
    for i, peer in enumerate((core, cross)):
        pass_ref[i] = shared_ref[...]
        share = remote(pass_ref.at[i], got_ref.at[i], s_send.at[i], s_recv.at[i], tensor=peer)
        share.start()
        share.wait()
        shared_ref[...] += got_ref[i]
    qkv.finish()

    def last(s, carry):
        for i in range(2):
            to_core(s, i).wait_send()
        to_cross(s).wait_send()
        return carry

    lax.fori_loop(0, n_seqs, last, 0)


def closing(own, tokens, gain, small, factors):
    n, tensor = lax.axis_size("dp"), lax.axis_size("tensor")
    seqs, own_len, width = tokens.shape
    rows, block = width // n, max(128, width // n)
    columns = [factors[i].shape[1] for i in (1, 3, 4)]
    vmem, anywhere = pl.BlockSpec(memory_space=pltpu.VMEM), pl.BlockSpec(memory_space=pl.ANY)
    shared = (2,) + small.shape[1:]
    return pl.pallas_call(
        functools.partial(closing_kernel, n, seqs, tensor),
        in_specs=[vmem] * 4 + [anywhere] * 9,
        out_specs=[vmem] * 7,
        out_shape=[jax.ShapeDtypeStruct((seqs, own_len, width), bf16)]
        + [jax.ShapeDtypeStruct((rows, count), f32) for count in columns]
        + [
            jax.ShapeDtypeStruct(small.shape[1:], f32),
            jax.ShapeDtypeStruct((32, block), f32),
            jax.ShapeDtypeStruct(shared, f32),
        ],
        scratch_shapes=[pltpu.VMEM(factor.shape, bf16) for factor in factors[:8]]
        + [pltpu.VMEM((seqs * own_len * tensor, width), bf16)]
        + [pltpu.VMEM((n, rows, count), bf16) for count in columns]
        + [pltpu.VMEM(small.shape, bf16), pltpu.VMEM((n, 32, block), bf16)]
        + [spare(rows, count) for count in columns]
        + [
            pltpu.VMEM((seqs, own_len * tensor, width), bf16),
            pltpu.VMEM((seqs, 2, own_len, width), bf16),
            pltpu.VMEM((seqs, own_len, width), bf16),
            pltpu.VMEM((seqs, own_len, width), bf16),
            pltpu.VMEM((32, width), f32),
            pltpu.VMEM((2,) + shared, f32),
            pltpu.VMEM((2,) + shared, f32),
            pltpu.SemaphoreType.DMA((8 + seqs,)),
            pltpu.SemaphoreType.DMA((seqs, 2)),
            pltpu.SemaphoreType.DMA((seqs, 2)),
            pltpu.SemaphoreType.DMA((seqs,)),
            pltpu.SemaphoreType.DMA((seqs,)),
            pltpu.SemaphoreType.DMA((5, n, 2 * SUBS)),
            pltpu.SemaphoreType.DMA((5, n, 2 * SUBS)),
            pltpu.SemaphoreType.DMA((2,)),
            pltpu.SemaphoreType.DMA((2,)),
        ],
        compiler_params=pltpu.CompilerParams(
            collective_id=5, has_side_effects=True, vmem_limit_bytes=63 * 1024 * 1024
        ),
        name="closing",
    )(own, tokens, gain, small, *factors)


def rms_unit(values):
    scale = lax.rsqrt(jnp.mean(values * values, axis=-1, keepdims=True) + epsilon)
    return values * scale, scale


def rms_back(back, unit, scale, gain):
    scaled = back * gain
    return scale * (scaled - unit * jnp.mean(scaled * unit, axis=-1, keepdims=True))


def flat(array):
    return array.reshape(-1, array.shape[-1])


def matmul(spec, left, right):
    return jnp.einsum(spec, left, right, preferred_element_type=f32)


def shards(
    tokens,
    cotangent,
    query_weight,
    key_weight,
    value_weight,
    beta_weight,
    conv_filter,
    norm_gain,
    head_gain,
    out_weight,
    gate_weight,
    up_weight,
    down_weight,
):
    n = lax.axis_size("dp")
    tensor = lax.axis_size("tensor")
    seqs, own_len, width = tokens.shape
    local = query_weight.shape[1]
    heads = local // HD
    hidden = gate_weight.shape[1]

    packed = jnp.concatenate(
        [conv_filter.reshape(-1), norm_gain.reshape(-1), head_gain, beta_weight.reshape(-1)]
    )
    block = -(-packed.size // 4096) * 4096
    small = jnp.pad(packed, (0, block - packed.size)).reshape(-1, 128)
    full_qkv, full_small, extended, rows_cotangent, full_out = opening(
        query_weight, key_weight, value_weight, small, tokens, cotangent, out_weight.T
    )
    full_out = full_out.reshape(width, local)
    full_qkv = full_qkv.reshape(width, 3 * local)
    full_small = full_small.reshape(n, block)
    sizes = [conv_filter.size, norm_gain.size, head_gain.size, beta_weight.size]
    ends = [sum(sizes[: i + 1]) for i in range(4)]
    filters = (
        full_small[:, : ends[0]]
        .reshape(n, 3 * KCONV, heads, HD // n)
        .transpose(1, 2, 0, 3)
        .reshape(3 * KCONV, local)
        .astype(f32)
    )
    gains = (
        full_small[:, ends[0] : ends[1]].reshape(n, 2, width // n).transpose(1, 0, 2).reshape(2, width)
    ).astype(f32)
    head_row = full_small[:, ends[1] : ends[2]].reshape(1, HD).astype(f32)
    full_beta = full_small[:, ends[2] : ends[3]].reshape(width, heads)

    unit_ext, _ = rms_unit(extended.astype(f32))
    normed_ext = (unit_ext * gains[0]).astype(bf16)
    normed_first = normed_ext[:, RIM:]
    projected = matmul("std,dm->stm", normed_ext, full_qkv).astype(bf16)
    strength = jax.nn.sigmoid(matmul("std,dh->sth", normed_first, full_beta))
    normed_mix, mix, carry, inverse, kw, state, full_gate = mixer(
        projected, strength, filters, head_row, gate_weight
    )

    normed_second, hidden_state, _, full_up, full_down, gate_pre, up_pre = fold(
        [flat(normed_mix), full_out], tokens, gains[1:2], [full_gate, up_weight, down_weight.T]
    )
    full_gate, full_up, full_down = (
        weight.reshape(width, hidden) for weight in (full_gate, full_up, full_down)
    )
    gate_sigmoid = jax.nn.sigmoid(gate_pre)
    ffn_hidden = (gate_pre * gate_sigmoid * up_pre).astype(bf16)

    back_hidden = matmul("std,df->stf", rows_cotangent, full_down)
    back_gate = (
        back_hidden * up_pre * gate_sigmoid * (1.0 + gate_pre * (1.0 - gate_sigmoid))
    ).astype(bf16)
    back_up = (back_hidden * gate_pre * gate_sigmoid).astype(bf16)
    rows_back, back_state, gain_second, grad_down = fold(
        [flat(back_gate), full_gate, flat(back_up), full_up], cotangent, gains[1:2],
        [flat(rows_cotangent), flat(ffn_hidden)], hidden_state,
    )
    high, low, end, head_part = state_back(rows_back, full_out, head_row, mix, carry, kw)
    back_proj, back_logit, conv_part, grad_gate, layer_out = mixer_back(
        projected, strength, filters, (high, low), inverse, end, state,
        (flat(normed_second), flat(back_gate)), (flat(ffn_hidden), full_down), hidden_state,
    )
    back_logit = back_logit.astype(bf16)
    grad_beta = matmul("std,sth->dh", normed_first, back_logit)
    grad_conv = conv_part.transpose(1, 0, 2).reshape(3 * KCONV, local)
    gain_grads = jnp.concatenate([jnp.zeros_like(gain_second), gain_second])
    small_grads = jnp.concatenate(
        [
            grad_conv.reshape(3 * KCONV, heads, n, HD // n).transpose(2, 0, 1, 3).reshape(n, -1),
            gain_grads.reshape(2, n, width // n).transpose(1, 0, 2).reshape(n, -1),
            head_part[0].reshape(n, HD // n),
            grad_beta.reshape(n, -1),
        ],
        axis=1,
    )
    small_grads = jnp.pad(small_grads, ((0, 0), (0, block - small_grads.shape[1])))
    lanes = ((0, 0), (0, 128 - heads))
    d_tokens, grad_up, grad_out, grad_qkv, small_grads, _, shared = closing(
        back_state, tokens, gains[0:1], small_grads.astype(bf16).reshape(n, -1, 128),
        [
            flat(normed_second), flat(back_up), flat(rows_back), flat(normed_mix), flat(back_proj),
            full_qkv, jnp.pad(flat(back_logit), lanes), jnp.pad(full_beta, lanes), normed_ext,
        ],
    )
    gain_row = shared[1, : max(1, width // n // 128)].reshape(-1)
    if width // n < 128:
        start = lax.rem(lax.axis_index("dp") * (width // n), 128)
        gain_row = lax.dynamic_slice_in_dim(gain_row, start, width // n)
    shared = shared[0]
    small_grads, shared = small_grads.reshape(-1), shared.reshape(-1)

    return (
        layer_out,
        d_tokens,
        grad_qkv[:, :local],
        grad_qkv[:, local : 2 * local],
        grad_qkv[:, 2 * local :],
        small_grads[ends[2] : ends[3]].reshape(beta_weight.shape),
        small_grads[: ends[0]].reshape(conv_filter.shape),
        jnp.stack([gain_row, shared[ends[0] + width // n : ends[1]]]),
        shared[ends[1] : ends[2]],
        grad_out.T,
        grad_gate,
        grad_up,
        grad_down.T,
    )


def solution(mesh):
    both = P(None, ("dp", "tensor"), None)
    rows, cols = P("dp", "tensor"), P("tensor", "dp")
    conv, gain, head = P(None, "tensor", "dp"), P(None, "dp"), P("dp")
    return jax.shard_map(
        shards,
        mesh=mesh,
        in_specs=(both, both, rows, rows, rows, rows, conv, gain, head, cols, rows, rows, cols),
        out_specs=(both, both, rows, rows, rows, rows, conv, gain, head, cols, rows, rows, cols),
        check_vma=False,
    )
```
